32 devices in a mesh: section: 2 (over core), dp: 16 (over z, y, x).
Axes of the slice: x: 2, y: 2, z: 4, core: 2. Of those that a mesh axis runs over, the one named last changes fastest.
Arguments:
- inputs: bfloat16 [64, 160, 768], P('dp'), may hold values from -6 to 6
- cotangent: bfloat16 [64, 160, 768], P('dp'), may hold values from -6 to 6
- chain_tags: int32 [64], P('dp'), may hold values 0 or 1
- chain_lengths: int32 [64], P('dp'), may hold values from 1 to 160, 6400 in all
- attn_in: float32 [2, 2, 768, 2304], P('section', None, 'dp'), may hold values from -0.3125 to 0.3125
- attn_out: float32 [2, 2, 768, 768], P('section', None, 'dp'), may hold values from -0.625 to 0.625
- ffn_in: float32 [2, 2, 768, 3072], P('section', None, 'dp'), may hold values from -0.21875 to 0.21875
- ffn_out: float32 [2, 2, 3072, 768], P('section', None, None, 'dp'), may hold values from -0.109375 to 0.109375
- proj_bias: float32 [2, 2, 4, 768], P('section', None, None, 'dp'), may hold values from -1.5 to 1.5
- ffn_bias: float32 [2, 2, 3072], P('section', None, 'dp'), may hold values from -1.5 to 1.5
- norm_gain: float32 [2, 2, 2, 768], P('section', None, None, 'dp'), may hold values from 0.25 to 1.75
- norm_shift: float32 [2, 2, 2, 768], P('section', None, None, 'dp'), may hold values from -1.5 to 1.5
Outputs:
- activations: bfloat16 [2, 64, 160, 768], P('section', 'dp')
- input_grads: float32 [2, 64, 160, 768], P('section', 'dp')
- grad_attn_in: float32 [2, 2, 768, 2304], P('section', None, 'dp')
- grad_attn_out: float32 [2, 2, 768, 768], P('section', None, 'dp')
- grad_ffn_in: float32 [2, 2, 768, 3072], P('section', None, 'dp')
- grad_ffn_out: float32 [2, 2, 3072, 768], P('section', None, None, 'dp')
- grad_proj_bias: float32 [2, 2, 4, 768], P('section', None, None, 'dp')
- grad_ffn_bias: float32 [2, 2, 3072], P('section', None, 'dp')
- grad_norm_gain: float32 [2, 2, 2, 768], P('section', None, None, 'dp')
- grad_norm_shift: float32 [2, 2, 2, 768], P('section', None, None, 'dp')
The draws below stay inside these ranges and needn't reach their ends.
Inputs may be any that keep to these rules, and one draw needn't show every extreme that they name: `chain_tags`: 1 marks a light chain, 0 a heavy one. `chain_lengths`: the longest chain has exactly 160 residues.
All inputs are finite; a program needn't handle non-finite values. No bound on the sum of `chain_tags` or of `chain_lengths` on one device may be relied on, other than what follows from the above.
Results may differ from the reference program's by a relative error of at most 0.035.
The reference program's roundings to bfloat16 on the way count: a program that leaves them out, or rounds other values in their place, can miss the bound.
Values may be sent and summed in bfloat16 or wider, within the bound.
No kernel may reach another device: no remote copies, remote signals or barrier semaphores. Data moves between devices by JAX's collectives and lax.ppermute only.
A program may use at most 384 MiB of HBM per device.

```python
import math
import jax
import jax.numpy as jnp
import numpy as np
from jax import lax

D = 768
HEADS = 12
HEAD_DIM = 64
FF = 3072
SEQ = 160
CH_MB = 2
MICRO = 2
CHAINS = 64
N_DP = 16


def with_ends(drawn, stream_key, smallest, high):
    spot = [jax.random.randint(jax.random.fold_in(stream_key, axis), (), 0, length) for axis, length in enumerate(drawn.shape)]
    main_axis = drawn.shape.index(max(drawn.shape))
    beside = spot[:main_axis] + [(spot[main_axis] + 1) % drawn.shape[main_axis]] + spot[main_axis + 1:]
    return drawn.at[tuple(spot)].set(smallest).at[tuple(beside)].set(high)


def raised(values, own_key, source, target, blocks, factor):
    def block_of(dim):
        return (jnp.arange(values.shape[dim]) // (values.shape[dim] // blocks)).reshape((-1,) + (1,) * (values.ndim - 1 - dim))

    one_side = jax.random.permutation(own_key, blocks)[block_of(target)]
    other_side = (block_of(target) + blocks // 2) % blocks
    return jnp.where((block_of(source) == one_side) | (block_of(source) == other_side), factor * values, values)


def levels(stream_key, dims, shards, low, top_value):
    level, own = 1.0, jax.random.fold_in(stream_key, 6)
    for axis_at, shards_of in shards:
        steps = jnp.exp(jax.random.uniform(jax.random.fold_in(own, axis_at), (shards_of,), jnp.float32, low / len(shards), top_value / len(shards)))
        level = level * jnp.repeat(steps, dims[axis_at] // shards_of).reshape([-1 if axis == axis_at else 1 for axis in range(len(dims))])
    return level


def profile(amount, total, bound, lean):
    loads = [(1 << 20) // math.isqrt(rank ** lean) + 1 for rank in range(2, amount + 1)]
    rest, given = total - bound - (amount - 1), [1] * (amount - 1)
    while rest > 0:
        candidates = [i for i in range(amount - 1) if given[i] < bound]
        pool, budget = sum([loads[i] for i in candidates]), rest
        for i in candidates:
            more = min(bound - given[i], max(1, budget * loads[i] // pool), rest)
            given[i] = given[i] + more
            rest = rest - more
    return np.array([bound] + given)


def uneven(stream_key, count, total, limit, slope):
    if count == 2:
        one = jax.random.randint(stream_key, (), max(1, total - limit), min(limit, total - 1) + 1)
        return jnp.stack([one, total - one])
    sizes = jnp.asarray(profile(count, total, limit, slope), jnp.int32)
    couples = (count - 1) // 2
    donor, sink = sizes[1:1 + 2 * couples:2], sizes[2:2 + 2 * couples:2]
    slack = jnp.minimum(donor - 1, limit - sink)
    passed = jax.random.randint(jax.random.fold_in(stream_key, 1), (couples,), 0, 1 << 20) % (slack + 1)
    sizes = sizes.at[1:1 + 2 * couples:2].set(donor - passed).at[2:2 + 2 * couples:2].set(sink + passed)
    return sizes[jax.random.permutation(jax.random.fold_in(stream_key, 2), count)]


def normal_values(key, dims, spread, most, cuts=(), held_as=jnp.bfloat16):
    level = levels(key, dims, cuts, -0.22, 0.18) if cuts else 1.0
    entries = jax.random.normal(key, dims, jnp.float32) * spread * level
    return jnp.minimum(jnp.maximum(entries, -most), most).astype(held_as)


def heavy_noise(stream_key, extent, deviation, limit, cuts, heavy, kind=jnp.bfloat16):
    entries = deviation * jax.random.normal(stream_key, extent, jnp.float32)
    if cuts:
        entries = entries * levels(stream_key, extent, cuts, -0.22, 0.18)
    return jnp.clip(raised(entries, jax.random.fold_in(stream_key, 3), *heavy), -limit, limit).astype(kind)


def setup_inputs(seed: int = 0) -> dict:
    splits = jax.random.split(jax.random.key(seed), 13)
    return {
        "inputs": normal_values(splits[0], (CHAINS, SEQ, D), 1.0, 6.0, ((0, 16),)),
        "cotangent": heavy_noise(splits[1], (CHAINS, SEQ, D), 1.0, 6.0, ((0, 16),), (0, 2, 16, 2.0)),
        "chain_tags": with_ends((jax.random.randint(splits[2], (CHAINS,), 0, 3) < 1).astype(jnp.int32), jax.random.fold_in(splits[2], 1), 0, 1),
        "chain_lengths": uneven(splits[3], CHAINS, CHAINS * SEQ * 5 // 8, SEQ, 1).astype(jnp.int32),
        "attn_in": normal_values(splits[4], (2, 2, D, 3 * D), (D // 2) ** -0.5, 0.3125, ((0, 2), (2, 16)), jnp.float32),
        "attn_out": normal_values(splits[5], (2, 2, D, D), (D // 8) ** -0.5, 0.625, ((0, 2), (2, 16)), jnp.float32),
        "ffn_in": normal_values(splits[6], (2, 2, D, FF), D ** -0.5, 0.21875, ((0, 2), (2, 16)), jnp.float32),
        "ffn_out": normal_values(splits[7], (2, 2, FF, D), FF ** -0.5, 0.109375, ((0, 2), (3, 16)), jnp.float32),
        "proj_bias": normal_values(splits[8], (2, 2, 4, D), 0.3, 1.5, ((0, 2), (3, 16)), jnp.float32),
        "ffn_bias": normal_values(splits[9], (2, 2, FF), 0.3, 1.5, ((0, 2), (2, 16)), jnp.float32),
        "norm_gain": jnp.clip(1.0 + 0.15 * jax.random.normal(splits[10], (2, 2, 2, D), jnp.float32), 0.25, 1.75),
        "norm_shift": normal_values(splits[11], (2, 2, 2, D), 0.3, 1.5, ((0, 2), (3, 16)), jnp.float32),
    }


@jax.custom_vjp
def low(v):
    return lax.optimization_barrier(v.astype(jnp.bfloat16)).astype(jnp.float32)

@jax.custom_vjp
def low_back(v):
    return v

def low_keep(v):
    return (low(v), None)

def low_pass(kept, grad):
    return (grad,)

def back_keep(v):
    return (v, None)

def back_low(kept, grad):
    return (low(grad),)
low.defvjp(low_keep, low_pass)
low_back.defvjp(back_keep, back_low)
EPS = 1e-05
NEG = -1e+30

def highest(form, left_op, right_op):
    return jnp.einsum(form, left_op, right_op, precision=lax.Precision.HIGHEST)

def layer_norm(summed, gain_row, shift_row):
    center = summed - lax.optimization_barrier(jnp.mean(summed, axis=-1, keepdims=True))
    inverse = lax.rsqrt(lax.optimization_barrier(jnp.mean(center * center, axis=-1, keepdims=True)) + EPS)
    return center * inverse * gain_row + shift_row

def one_model(chains, live_keys, w_qkv, w_out, w_up, w_down, biases, up_bias, gain_rows, shift_rows):
    count = chains.shape[0]
    zero_row = jnp.zeros_like(biases[0])
    qkv = highest('cld,de->cle', chains, w_qkv) + jnp.concatenate([biases[0], zero_row, biases[1]])
    qkv = low_back(low(qkv))
    queries = qkv[:, :, :D].reshape(count, SEQ, HEADS, HEAD_DIM)
    key_rows = qkv[:, :, D:2 * D].reshape(count, SEQ, HEADS, HEAD_DIM)
    values = qkv[:, :, 2 * D:].reshape(count, SEQ, HEADS, HEAD_DIM)
    raw_scores = low_back(highest('cqhd,ckhd->chqk', queries, key_rows))
    scores = jnp.where(live_keys[:, None, None, :], raw_scores * HEAD_DIM ** (-0.5), NEG)
    attn_probs = jax.nn.softmax(scores, axis=-1)
    context = highest('chqk,ckhd->cqhd', low(attn_probs), values).reshape(count, SEQ, D)
    context = low_back(low(context))
    attn_branch = low_back(highest('cld,de->cle', context, w_out) + biases[2])
    hidden = layer_norm(chains + attn_branch, gain_rows[0], shift_rows[0])
    pre_gelu = low_back(highest('cld,df->clf', low_back(low(hidden)), w_up) + up_bias)
    act_low = low(jax.nn.gelu(pre_gelu, approximate=False))
    ffn_branch = low_back(highest('clf,fd->cld', act_low, w_down) + biases[3])
    return layer_norm(hidden + ffn_branch, gain_rows[1], shift_rows[1])

def layer(chains, live_keys, select, params):
    rounded = [low(param) for param in params]
    heavy = one_model(chains, live_keys, *[item[0] for item in rounded])
    light = one_model(chains, live_keys, *[item[1] for item in rounded])
    return jnp.where(select[:, None, None], heavy, light)

def reference(inputs, cotangent, chain_tags, chain_lengths, attn_in, attn_out, ffn_in, ffn_out, proj_bias, ffn_bias, norm_gain, norm_shift):
    masters = (attn_in, attn_out, ffn_in, ffn_out, proj_bias, ffn_bias, norm_gain, norm_shift)
    group = CH_MB * MICRO

    def regroup(array):
        return array.reshape((N_DP, group) + array.shape[1:])

    def visit(totals, pieces):
        chains, cot_rows, chain_kind, chain_len = pieces
        live_keys = lax.broadcasted_iota(jnp.int32, (group, SEQ), 1) < chain_len[:, None]
        select = chain_kind == 0
        first_params = tuple((master[0] for master in masters))
        second_params = tuple((master[1] for master in masters))

        def run_layer(rows, params):
            return layer(rows, live_keys, select, params)
        middle, back_first = jax.vjp(run_layer, chains.astype(jnp.float32), first_params)
        top_rows, back_second = jax.vjp(run_layer, low(middle), second_params)
        grad_top = cot_rows.astype(jnp.float32) * live_keys[:, :, None].astype(jnp.float32)
        grad_middle, second_grads = back_second(grad_top)
        grad_input, first_grads = back_first(low(grad_middle))
        totals = tuple((total + jnp.stack([one_grad, two_grad]) for total, one_grad, two_grad in zip(totals, first_grads, second_grads)))
        outputs = jnp.stack([middle.astype(jnp.bfloat16), top_rows.astype(jnp.bfloat16)])
        return (totals, (outputs, jnp.stack([grad_input, grad_middle])))
    zeros = tuple((jnp.zeros(master.shape, jnp.float32) for master in masters))
    totals, (outputs, grads) = lax.scan(visit, zeros, (regroup(inputs), regroup(cotangent), regroup(chain_tags), regroup(chain_lengths)))
    outputs = jnp.transpose(outputs, (1, 0, 2, 3, 4)).reshape(2, CHAINS, SEQ, D)
    grads = jnp.transpose(grads, (1, 0, 2, 3, 4)).reshape(2, CHAINS, SEQ, D)
    return (outputs, grads, totals[0], totals[1], totals[2], totals[3], totals[4], totals[5], totals[6], totals[7])
```

```python
import functools

import jax
import jax.numpy as jnp
from jax import lax
from jax.experimental import pallas as pl
from jax.experimental.pallas import tpu as pltpu
from jax.sharding import PartitionSpec as P

D = 768
HEADS = 12
HEAD_DIM = 64
FF = 3072
SEQ = 160
PAIRS = HEADS // 2
BLOCKS = 16
ROWS = D // BLOCKS
WIDE = 3072
EXTRA = 128
CHUNK = 768

EPS = 1e-05
NEG = -1e30
SQRT_HALF = 0.7071067811865476
INV_ROOT = 0.3989422804014327
SCALE = HEAD_DIM**-0.5

ROTATIONS = ((0, 1, 2), (1, 2, 0), (2, 0, 1))
F32 = jnp.float32
BF16 = jnp.bfloat16


def unit_masks(unit):
    one, two, three = (1 << bit for bit in ROTATIONS[unit])
    base = [0, one, two, two | one]
    return [side | far | mask for side in (0, 8) for far in (0, three) for mask in base]


def grad_masks(unit):
    one, two, three = (1 << bit for bit in ROTATIONS[unit])
    return [
        (8 if p & 8 else 0) | (one if p & 4 else 0) | (two if p & 2 else 0) | (three if p & 1 else 0)
        for p in range(BLOCKS)
    ]


def dot_nn(a, b):
    return jnp.dot(a, b, preferred_element_type=F32)


def dot_nt(a, b):
    return lax.dot_general(a, b, (((1,), (1,)), ((), ())), preferred_element_type=F32)


def dot_tn(a, b):
    return lax.dot_general(a, b, (((0,), (0,)), ((), ())), preferred_element_type=F32)


def row_mean(a):
    return jnp.sum(a, axis=-1, keepdims=True) * (1.0 / D)


def norm(summed):
    center = summed - row_mean(summed)
    inverse = lax.rsqrt(row_mean(center * center) + EPS)
    return center * inverse, inverse


def norm_back(grad, normed, inverse, gain):
    scaled = grad * gain
    return inverse * (scaled - row_mean(scaled) - normed * row_mean(scaled * normed))


def col_sum(a):
    return jnp.sum(a.astype(F32), axis=0, keepdims=True)


def lanes(start, width):
    return pl.ds(pl.multiple_of(start, 128), width)


def layer_kernel(back, half, index, x_index, gy_index, masked, count, *refs):
    refs = list(refs)
    take = lambda n: [refs.pop(0) for _ in range(n)]
    (meta,) = take(1)
    rows_ref, fbias_ref = take(2)
    pieces = take(24)
    (x_hbm,) = take(1)
    if back:
        (gy_hbm,) = take(1)
    n_alias = len(refs)
    n_out = 11 if back else 2
    n_scratch = 23 if back else 12
    take(n_alias - n_out - n_scratch)
    outs = take(n_out)
    scr = take(n_scratch)
    win, wout, wfi, wfo, x_s, qkv, ctx, act, hl, y_s, acc, sems = scr[:12]
    if back:
        (gx16_o, y_o, gx_o, sum_o, fsum_o, sx_o, sctx_o, shid_o, sdf_o, sr0_o, sr1_o) = outs[:11]
        gy_s, probs, slope, n1_s, n2_s, dr0, dpre, dfn, gx_s, sum_s, fsum_s = scr[12:]
    else:
        y1_o, y_o = outs

    @pl.when(meta[0] == half)
    def _():
        tag = meta[1 + index]
        length = meta[1 + count + index]
        cp_x = pltpu.make_async_copy(x_hbm.at[x_index], x_s, sems.at[4, 0])
        cp_x.start()
        if back:
            cp_g = pltpu.make_async_copy(gy_hbm.at[gy_index], gy_s, sems.at[4, 1])
            cp_g.start()

        def load_from(model):
            def one(unit, col, width, dst, group):
                for q in range(4):
                    src = pieces[(model * 3 + unit) * 4 + q]

                    def body(e, carry):
                        k = q * 4 + e
                        row = pl.multiple_of(meta[1 + 2 * count + unit * BLOCKS + k] * ROWS, 16)
                        pltpu.make_async_copy(
                            src.at[e, :, col : col + width],
                            dst.at[pl.ds(row, ROWS)],
                            sems.at[group, k],
                        ).start()
                        return carry

                    lax.fori_loop(0, 4, body, 0)

            one(0, 0, 3 * D, win, 0)
            one(0, 3 * D, D, wout, 1)
            one(1, 0, FF, wfi, 2)
            one(2, 0, FF, wfo, 3)

        pl.when(tag == 0)(lambda: load_from(0))
        pl.when(tag != 0)(lambda: load_from(1))

        def landed(dst, group):
            def body(k, carry):
                part = dst.at[pl.ds(0, ROWS)]
                pltpu.make_async_copy(part, part, sems.at[group, k]).wait()
                return carry

            lax.fori_loop(0, BLOCKS, body, 0)

        def small(row):
            return rows_ref[tag, row : row + 1, :]

        cp_x.wait()
        landed(win, 0)
        x = x_s[...]
        zero_row = jnp.zeros((1, D), F32)
        for n, bias in enumerate((small(0), zero_row, small(1))):
            cols = slice(n * D, (n + 1) * D)
            qkv[:, cols] = (dot_nn(x, win[:, cols]) + bias).astype(BF16)

        low_half = lax.broadcasted_iota(jnp.int32, (1, 2 * HEAD_DIM), 1) < HEAD_DIM
        head_mask = (low_half.astype(F32).astype(BF16), (1 - low_half.astype(F32)).astype(BF16))
        live = lax.broadcasted_iota(jnp.int32, (SEQ, SEQ), 1) < length

        def heads_fwd(pair, carry):
            off = pair * 2 * HEAD_DIM
            q2 = qkv[:, lanes(off, 128)]
            k2 = qkv[:, lanes(D + off, 128)]
            v2 = qkv[:, lanes(2 * D + off, 128)]
            joined = None
            for side in range(2):
                raw = dot_nt(q2 * head_mask[side], k2)
                scores = jnp.where(live, raw * SCALE, NEG)
                expo = jnp.exp(scores - jnp.max(scores, axis=-1, keepdims=True))
                prob = expo * (1.0 / jnp.sum(expo, axis=-1, keepdims=True))
                if back:
                    probs[2 * pair + side] = prob
                part = dot_nn(prob.astype(BF16), v2 * head_mask[side])
                joined = part if joined is None else joined + part
            ctx[:, lanes(off, 128)] = joined.astype(BF16)
            return carry

        lax.fori_loop(0, PAIRS, heads_fwd, 0)

        landed(wout, 1)
        branch = dot_nn(ctx[...], wout[...]) + small(2)
        n1, i1 = norm(x.astype(F32) + branch)
        hidden = n1 * small(4) + small(6)
        if back:
            n1_s[...] = n1
        hl[...] = hidden.astype(BF16)
        acc[...] = hidden
        landed(wfi, 2)
        landed(wfo, 3)

        def ffn_fwd(n, carry):
            cols = lanes(n * CHUNK, CHUNK)
            pre = dot_nn(hl[...], wfi[:, cols]) + fbias_ref[tag, :, cols]
            phi = 0.5 * (1.0 + lax.erf(pre * SQRT_HALF))
            act[:, cols] = (pre * phi).astype(BF16)
            if back:
                slope[:, cols] = phi + pre * jnp.exp(-0.5 * pre * pre) * INV_ROOT
            return carry

        lax.fori_loop(0, FF // CHUNK, ffn_fwd, 0)
        branch = dot_nt(act[...], wfo[...]) + small(3)
        n2, i2 = norm(acc[...] + branch)
        y_s[...] = (n2 * small(5) + small(7)).astype(BF16)
        copies = []

        def put(src, dst, sem):
            copy = pltpu.make_async_copy(src, dst, sem)
            copy.start()
            copies.append(copy)

        put(y_s, y_o.at[index], sems.at[5, 0])
        if not back:
            put(y_s, y1_o.at[0], sems.at[5, 1])
        else:
            put(x_s, sx_o.at[index], sems.at[5, 2])
            put(ctx, sctx_o.at[index], sems.at[5, 3])
            put(hl, shid_o.at[index], sems.at[5, 4])
            put(act, sr1_o.at[1, index], sems.at[5, 5])
            cp_g.wait()
            gy = gy_s[...].astype(F32)
            if masked:
                alive = lax.broadcasted_iota(jnp.int32, (SEQ, D), 0) < length
                gy = jnp.where(alive, gy, 0.0)
            sum_s[5:6, :] = col_sum(gy * n2)
            sum_s[7:8, :] = col_sum(gy)
            gr2 = norm_back(gy, n2, i2, small(5))
            dfn[...] = gr2.astype(BF16)
            sum_s[3:4, :] = col_sum(dfn[...])
            put(dfn, sdf_o.at[index], sems.at[5, 6])
            n2_s[...] = gr2

            def ffn_back(n, carry):
                cols = lanes(n * CHUNK, CHUNK)
                d_act = dot_nn(dfn[...], wfo[:, cols])
                d_pre = (d_act * slope[:, cols]).astype(BF16)
                dpre[:, cols] = d_pre
                fsum_s[:, cols] = col_sum(d_pre)
                return carry

            lax.fori_loop(0, FF // CHUNK, ffn_back, 0)
            put(dpre, sr1_o.at[0, index], sems.at[5, 7])
            gh = n2_s[...] + dot_nt(dpre[...], wfi[...]).astype(BF16).astype(F32)
            n1 = n1_s[...]
            sum_s[4:5, :] = col_sum(gh * n1)
            sum_s[6:7, :] = col_sum(gh)
            gr1 = norm_back(gh, n1, i1, small(4))
            acc[...] = gr1
            d_attn = gr1.astype(BF16)
            dr0[:, 3 * D :] = d_attn
            sum_s[2:3, :] = col_sum(d_attn)
            gx_s[...] = dot_nt(d_attn, wout[...]).astype(BF16)

            def heads_back(pair, carry):
                off = pair * 2 * HEAD_DIM
                q2 = qkv[:, lanes(off, 128)]
                k2 = qkv[:, lanes(D + off, 128)]
                v2 = qkv[:, lanes(2 * D + off, 128)]
                dc2 = gx_s[:, lanes(off, 128)]
                dq = dk = dv = None
                for side in range(2):
                    prob = probs[2 * pair + side]
                    dch = dc2 * head_mask[side]
                    d_prob = dot_nt(dch, v2)
                    inner = jnp.sum(prob * d_prob, axis=-1, keepdims=True)
                    d_raw = (prob * (d_prob - inner) * SCALE).astype(BF16)
                    a = dot_nn(d_raw, k2 * head_mask[side])
                    b = dot_tn(d_raw, q2 * head_mask[side])
                    c = dot_tn(prob.astype(BF16), dch)
                    dq, dk, dv = (a, b, c) if dq is None else (dq + a, dk + b, dv + c)
                dr0[:, lanes(off, 128)] = dq.astype(BF16)
                dr0[:, lanes(D + off, 128)] = dk.astype(BF16)
                dr0[:, lanes(2 * D + off, 128)] = dv.astype(BF16)
                return carry

            lax.fori_loop(0, PAIRS, heads_back, 0)
            put(dr0, sr0_o.at[index], sems.at[5, 8])
            sum_s[0:1, :] = col_sum(dr0[:, :D])
            sum_s[1:2, :] = col_sum(dr0[:, 2 * D : 3 * D])
            grad_a = dot_nt(dr0[:, : 3 * D], win[...]) + acc[...]
            n1_s[...] = grad_a
            hl_out = grad_a.astype(BF16)
            gy_s[...] = hl_out
            put(sum_s, sum_o.at[index], sems.at[5, 11])
            put(fsum_s, fsum_o.at[index], sems.at[5, 12])
            put(n1_s, gx_o.at[index], sems.at[5, 9])
            put(gy_s, gx16_o.at[0], sems.at[5, 10])
        for copy in copies:
            copy.wait()


def grad_kernel(unit, meta, *refs):
    n_left = 2 if unit == 0 else 1
    left, (right,), outs, (turned, acc) = refs[:n_left], refs[n_left : n_left + 1], refs[n_left + 1 : n_left + 5], refs[-2:]
    n = pl.program_id(0)

    @pl.when(n == 0)
    def _():
        for i in range(n_left):
            for c in range(left[i].shape[0]):
                turned[i, c] = left[i][c].T

    pick = jnp.where(n == 3, 1, 0) if unit == 0 else 0
    acc[...] = jnp.zeros_like(acc)

    def add_chain(c, carry):
        tag = jnp.where(meta[1 + c] == 0, 0, 1)
        acc[tag] += dot_nn(turned[pick, c], right[c])
        return carry

    lax.fori_loop(0, right.shape[0], add_chain, 0)
    for model in range(2):
        for p in range(BLOCKS):
            row = pl.multiple_of(meta[1 + 2 * right.shape[0] + (3 + unit) * BLOCKS + p] * ROWS, 16)
            outs[2 * model + p // 8][p % 8] = acc[model, pl.ds(row, ROWS), :].astype(BF16)


ANY = pl.BlockSpec(memory_space=pl.ANY)
SMEM = pl.BlockSpec(memory_space=pltpu.SMEM)
VMEM = pl.BlockSpec(memory_space=pltpu.VMEM)


def shaped(shape, dtype):
    return jax.ShapeDtypeStruct(shape, dtype)


def saved_shapes(count):
    narrow = shaped((count, SEQ, D), BF16)
    return [
        narrow,
        shaped((count, SEQ, D), F32),
        shaped((count, 8, D), F32),
        shaped((count, 1, FF), F32),
        narrow,
        narrow,
        narrow,
        narrow,
        shaped((count, SEQ, WIDE), BF16),
        shaped((2, count, SEQ, WIDE), BF16),
    ]


def layer_call(back, half, index, masked, count, meta, rows, fbias, pieces, x, x_index, gy, gy_index, held):
    scratch = [
        pltpu.VMEM((D, 3 * D), BF16),
        pltpu.VMEM((D, D), BF16),
        pltpu.VMEM((D, FF), BF16),
        pltpu.VMEM((D, FF), BF16),
        pltpu.VMEM((SEQ, D), BF16),
        pltpu.VMEM((SEQ, 3 * D), BF16),
        pltpu.VMEM((SEQ, D), BF16),
        pltpu.VMEM((SEQ, FF), BF16),
        pltpu.VMEM((SEQ, D), BF16),
        pltpu.VMEM((SEQ, D), BF16),
        pltpu.VMEM((SEQ, D), F32),
        pltpu.SemaphoreType.DMA((6, BLOCKS)),
    ]
    if back:
        scratch += [
            pltpu.VMEM((SEQ, D), BF16),
            pltpu.VMEM((HEADS, SEQ, SEQ), F32),
            pltpu.VMEM((SEQ, FF), F32),
            pltpu.VMEM((SEQ, D), F32),
            pltpu.VMEM((SEQ, D), F32),
            pltpu.VMEM((SEQ, WIDE), BF16),
            pltpu.VMEM((SEQ, FF), BF16),
            pltpu.VMEM((SEQ, D), BF16),
            pltpu.VMEM((SEQ, D), BF16),
            pltpu.VMEM((8, D), F32),
            pltpu.VMEM((1, FF), F32),
        ]
    operands = [meta, rows, fbias, *pieces, x]
    specs = [SMEM, VMEM, VMEM] + [ANY] * (len(pieces) + 1)
    if back:
        operands.append(gy)
        specs.append(ANY)
    first = [shaped((1, SEQ, D), BF16)]
    kept = saved_shapes(count) if back else [shaped((count, SEQ, D), BF16)]
    aliases = {}
    for at, array in enumerate(held):
        if array is not None:
            aliases[len(operands)] = at + 1
            operands.append(array)
            specs.append(ANY)
    scale = 3 if back else 1
    outs = pl.pallas_call(
        functools.partial(layer_kernel, back, half, index, x_index, gy_index, masked, count),
        out_shape=first + kept,
        in_specs=specs,
        out_specs=[ANY] * (1 + len(kept)),
        scratch_shapes=scratch,
        input_output_aliases=aliases,
        compiler_params=pltpu.CompilerParams(vmem_limit_bytes=50 * 1024 * 1024),
        cost_estimate=pl.CostEstimate(
            flops=scale * 2 * SEQ * D * 9216, bytes_accessed=scale * D * 9216 * 2, transcendentals=0
        ),
        name="layer_back" if back else "layer_fwd",
    )(*operands)
    return outs[0], list(outs[1:])


def grad_call(unit, meta, left, right, which):
    count = left[0].shape[0]
    block = (count, SEQ, CHUNK)
    if right.ndim == 4:
        right_spec = pl.BlockSpec((None,) + block, lambda n, m: (which, 0, 0, n))
    else:
        right_spec = pl.BlockSpec(block, lambda n, m: (0, 0, n))
    out = shaped((8, ROWS, WIDE), BF16)
    return pl.pallas_call(
        functools.partial(grad_kernel, unit),
        out_shape=[out] * 4,
        grid_spec=pltpu.PrefetchScalarGridSpec(
            num_scalar_prefetch=1,
            grid=(WIDE // CHUNK,),
            in_specs=[pl.BlockSpec((count, SEQ, D), lambda n, m: (0, 0, 0))] * len(left) + [right_spec],
            out_specs=[pl.BlockSpec((8, ROWS, CHUNK), lambda n, m: (0, 0, n))] * 4,
            scratch_shapes=[
                pltpu.VMEM((len(left), count, D, SEQ), BF16),
                pltpu.VMEM((2, D, CHUNK), F32),
            ],
        ),
        compiler_params=pltpu.CompilerParams(vmem_limit_bytes=50 * 1024 * 1024),
        cost_estimate=pl.CostEstimate(
            flops=2 * count * SEQ * D * WIDE * 2, bytes_accessed=4 * 8 * ROWS * WIDE * 2, transcendentals=0
        ),
        name="layer_grad",
    )(meta, *left, right)


def swap_bit(array, bit):
    count = lax.axis_size("dp")
    return lax.ppermute(array, "dp", [(i, i ^ (1 << bit)) for i in range(count)])


def swap_section(array):
    return lax.ppermute(array, "section", [(0, 1), (1, 0)])


def along(array, pairs):
    count = lax.axis_size("dp")
    flat = [(s * count + i, t * count + k) for (s, i), (t, k) in pairs]
    return lax.ppermute(array, ("section", "dp"), flat)


def swap_crossed(array):
    near = lax.axis_size("dp") // 2
    pairs = []
    for j in range(near):
        pairs += [((1, j), (0, near + j)), ((0, near + j), (1, j))]
    return along(array, pairs)


def gather_pieces(own, unit):
    one, two, three = ROTATIONS[unit]
    pair = jnp.concatenate([own, swap_bit(own, one)], 0)
    four = jnp.concatenate([pair, swap_bit(pair, two)], 0)
    far = swap_bit(four, three)
    return [four, far, swap_section(four), swap_section(far)]


def both(first, second):
    return (first.astype(F32) + second.astype(F32)).astype(BF16)


def scatter_sums(keep, send, unit):
    got = swap_section(send)
    for step, bit in enumerate(ROTATIONS[unit]):
        width = 4 >> step
        send = both(keep[width:], got[width:])
        keep = both(keep[:width], got[:width])
        got = swap_bit(send, bit)
    return keep.astype(F32) + got.astype(F32)


def per_device(
    inputs,
    cotangent,
    chain_tags,
    chain_lengths,
    attn_in,
    attn_out,
    ffn_in,
    ffn_out,
    proj_bias,
    ffn_bias,
    norm_gain,
    norm_shift,
):
    n_dp = lax.axis_size("dp")
    near = n_dp // 2
    rows = attn_in.shape[2]
    count = inputs.shape[0]
    fast = near == 8 and rows == ROWS
    section = lax.axis_index("section")
    place = lax.axis_index("dp")
    half = place // near
    spot = place % near
    at_home = section == half
    crossing = []
    for j in range(near):
        crossing += [((1, near + j), (1, j)), ((0, j), (0, near + j))]

    moved = along(jnp.where(half == 1, inputs, cotangent), crossing)
    numbers = jnp.concatenate([chain_tags, chain_lengths])
    numbers = jnp.where(at_home, numbers, along(numbers, crossing))
    chains = jnp.where(at_home, inputs, moved)
    top_grad = jnp.where(at_home, cotangent, moved)

    gap = jnp.zeros((2, rows, EXTRA - 12), BF16)
    small = jnp.concatenate(
        [
            jnp.swapaxes(proj_bias[0], 1, 2),
            jnp.swapaxes(norm_gain[0], 1, 2),
            jnp.swapaxes(norm_shift[0], 1, 2),
            ffn_bias[0].reshape(2, rows, 4),
        ],
        -1,
    ).astype(BF16)
    units = [
        jnp.concatenate([attn_in[0].astype(BF16), attn_out[0].astype(BF16), small, gap], -1),
        ffn_in[0].astype(BF16),
        jnp.swapaxes(ffn_out[0].astype(BF16), 1, 2),
    ]
    shard = spot + section * near
    if fast:
        gathered = []
        for model in range(2):
            for unit in range(3):
                own = units[unit][model : model + 1]
                own = jnp.where(at_home, own, swap_crossed(own))
                gathered.append(gather_pieces(own, unit))
        tables = [shard ^ jnp.asarray(unit_masks(unit), jnp.int32) for unit in range(3)]
        tables += [shard ^ jnp.asarray(grad_masks(unit), jnp.int32) for unit in range(3)]
    else:
        order = jnp.arange(BLOCKS, dtype=jnp.int32)
        tables = [order] * 6
        whole = []
        for unit in range(3):
            full = lax.all_gather(units[unit], ("section", "dp"), axis=0)
            full = full.reshape((2, n_dp) + full.shape[1:])
            full = lax.dynamic_index_in_dim(full, half, 0, keepdims=False)
            full = jnp.swapaxes(full, 0, 1).reshape(2, BLOCKS, ROWS, full.shape[-1])
            whole.append(full)
        gathered = [
            [whole[unit][model, 4 * q : 4 * q + 4] for q in range(4)] for model in range(2) for unit in range(3)
        ]
    meta = jnp.concatenate([half[None].astype(jnp.int32), numbers] + tables)
    pieces = [array for group in gathered for array in group]

    pick = (tables[0][None, :] == jnp.arange(BLOCKS, dtype=jnp.int32)[:, None]).astype(BF16)
    row_list, fbias_list = [], []
    for model in range(2):
        cols = jnp.concatenate([array[:, :, WIDE : WIDE + 12] for array in gathered[3 * model]], 0)
        cols = dot_nn(pick, cols.reshape(BLOCKS, ROWS * 12)).reshape(D, 12)
        row_list.append(cols[:, :8].T)
        fbias_list.append(cols[:, 8:].reshape(1, FF))
    rows_all = jnp.stack(row_list)
    fbias_all = jnp.stack(fbias_list)

    call = functools.partial(layer_call, count=count, meta=meta, rows=rows_all, fbias=fbias_all, pieces=pieces)
    forward = [((0, j), (0, near + j)) for j in range(near)] + [((1, j), (1, near + j)) for j in range(near)]
    backward = [(b, a) for a, b in forward]
    acts, act_all = [], [None]
    for c in range(count):
        out, act_all = call(False, 0, c, False, x=chains, x_index=c, gy=None, gy_index=0, held=act_all)
        acts.append(along(out, forward))
    held = act_all + [None] * 9
    grads = []
    for c in range(count):
        out, held = call(True, 1, c, True, x=acts[c], x_index=0, gy=top_grad, gy_index=c, held=held)
        grads.append(along(out, backward))
    for c in range(count):
        out, held = call(True, 0, c, False, x=chains, x_index=c, gy=grads[c], gy_index=0, held=held)
    act_all, grad_all, sums, fsums, s_x, s_ctx, s_hid, s_dffn, s_r0, s_r1 = held

    totals = [
        grad_call(2, meta, [s_dffn], s_r1, 1),
        grad_call(1, meta, [s_hid], s_r1, 0),
        grad_call(0, meta, [s_x, s_ctx], s_r0, 0),
    ]
    chosen = (numbers[None, :count] == jnp.arange(2, dtype=jnp.int32)[:, None]).astype(F32)
    row_sums = jnp.sum(chosen[:, :, None, None] * sums[None], axis=1)
    fbias_sums = jnp.sum(chosen[:, :, None] * fsums[None, :, 0], axis=1)
    small_grads = jnp.concatenate([jnp.swapaxes(row_sums, 1, 2), fbias_sums.reshape(2, D, 4)], -1)

    results = {}
    if fast:
        for at, unit in enumerate((2, 1, 0)):
            for model in range(2):
                keep, send = totals[at][2 * model : 2 * model + 2]
                results[unit, model] = scatter_sums(keep, send, unit)[0]
        laid = jnp.concatenate([small_grads, jnp.zeros((2, D, EXTRA - 12), F32)], -1).astype(BF16)
        laid = jnp.swapaxes(laid.reshape(2, BLOCKS, ROWS, EXTRA), 0, 1)
        pick = (tables[3][:, None] == jnp.arange(BLOCKS, dtype=jnp.int32)[None, :]).astype(BF16)
        laid = dot_nn(pick, laid.reshape(BLOCKS, -1)).astype(BF16).reshape(BLOCKS, 2 * ROWS, EXTRA)
        small_out = scatter_sums(laid[:8], laid[8:], 0)[0].reshape(2, ROWS, EXTRA)

        def home(array):
            return jnp.where(at_home, array, swap_crossed(array.astype(BF16)).astype(F32))

        unit_out = [jnp.stack([home(results[unit, model]) for model in range(2)]) for unit in range(3)]
        small_out = home(small_out)
    else:

        def summed(array):
            layers = jnp.stack([jnp.where(half == layer, array, jnp.zeros_like(array)) for layer in range(2)])
            layers = jnp.swapaxes(layers, 1, 2).reshape(2 * n_dp, rows, 2, array.shape[-1])
            out = lax.psum_scatter(layers, ("section", "dp"), scatter_dimension=0, tiled=True)
            return jnp.swapaxes(out[0], 0, 1)

        unit_out = [None] * 3
        for at, unit in enumerate((2, 1, 0)):
            group = [
                jnp.concatenate(totals[at][2 * model : 2 * model + 2], 0).reshape(D, WIDE) for model in range(2)
            ]
            unit_out[unit] = summed(jnp.stack(group).astype(F32))
        small_out = summed(small_grads)

    pairs = []
    for j in range(near):
        pairs += [((1, near + j), (0, near + j)), ((0, near + j), (1, j))]
    other = along(jnp.where(section == 1, jnp.concatenate(acts, 0), act_all), pairs)
    act_out = jnp.where(at_home, act_all, other)
    pairs = []
    for j in range(near):
        pairs += [((0, j), (1, j)), ((1, j), (0, near + j))]
    other = along(jnp.where(section == 0, jnp.concatenate(grads, 0), grad_all.astype(BF16)), pairs)
    grad_out = jnp.where(at_home, grad_all, other.astype(F32))

    turned = jnp.swapaxes(small_out[:, :, :8], 1, 2)
    return (
        act_out[None],
        grad_out[None],
        unit_out[0][None, :, :, : 3 * D],
        unit_out[0][None, :, :, 3 * D :],
        unit_out[1][None],
        jnp.swapaxes(unit_out[2], 1, 2)[None],
        turned[None, :, 0:4],
        small_out[:, :, 8:12].reshape(1, 2, 4 * rows),
        turned[None, :, 4:6],
        turned[None, :, 6:8],
    )


def solution(mesh):
    in_specs = (
        P("dp", None, None),
        P("dp", None, None),
        P("dp"),
        P("dp"),
        P("section", None, "dp", None),
        P("section", None, "dp", None),
        P("section", None, "dp", None),
        P("section", None, None, "dp"),
        P("section", None, None, "dp"),
        P("section", None, "dp"),
        P("section", None, None, "dp"),
        P("section", None, None, "dp"),
    )
    out_specs = (
        P("section", "dp", None, None),
        P("section", "dp", None, None),
        P("section", None, "dp", None),
        P("section", None, "dp", None),
        P("section", None, "dp", None),
        P("section", None, None, "dp"),
        P("section", None, None, "dp"),
        P("section", None, "dp"),
        P("section", None, None, "dp"),
        P("section", None, None, "dp"),
    )
    return jax.shard_map(
        per_device, mesh=mesh, in_specs=in_specs, out_specs=out_specs, check_vma=False
    )
```

```python
import functools

import jax
import jax.numpy as jnp
from jax import lax
from jax.experimental import pallas as pl
from jax.experimental.pallas import tpu as pltpu
from jax.sharding import PartitionSpec as P

D = 768
HEADS = 12
HEAD_DIM = 64
FF = 3072
SEQ = 160
PAIRS = HEADS // 2
BLOCKS = 16
ROWS = D // BLOCKS
WIDE = 3072
EXTRA = 128
CHUNK = 768

EPS = 1e-05
NEG = -1e30
SQRT_HALF = 0.7071067811865476
INV_ROOT = 0.3989422804014327
SCALE = HEAD_DIM**-0.5

ROTATIONS = ((0, 1, 2), (1, 2, 0), (2, 0, 1))
F32 = jnp.float32
BF16 = jnp.bfloat16


def piece_masks(unit):
    one, two, three = (1 << bit for bit in ROTATIONS[unit])
    return [far | mask for far in (0, three) for mask in (0, one, two, two | one)]


def grad_masks(rotation):
    one, two, three = (1 << bit for bit in rotation)
    return [(one if p & 4 else 0) | (two if p & 2 else 0) | (three if p & 1 else 0) for p in range(8)]


def grad_place(mask, rotation):
    one, two, three = rotation
    return ((mask >> one) & 1) * 4 + ((mask >> two) & 1) * 2 + ((mask >> three) & 1)


def dot_nn(a, b):
    return jnp.dot(a, b, preferred_element_type=F32)


def dot_nt(a, b):
    return lax.dot_general(a, b, (((1,), (1,)), ((), ())), preferred_element_type=F32)


def dot_tn(a, b):
    return lax.dot_general(a, b, (((0,), (0,)), ((), ())), preferred_element_type=F32)


def row_mean(a):
    return jnp.sum(a, axis=-1, keepdims=True) * (1.0 / D)


def norm(summed):
    center = summed - row_mean(summed)
    inverse = lax.rsqrt(row_mean(center * center) + EPS)
    return center * inverse, inverse


def norm_back(grad, normed, inverse, gain):
    scaled = grad * gain
    return inverse * (scaled - row_mean(scaled) - normed * row_mean(scaled * normed))


def col_sum(a):
    return jnp.sum(a.astype(F32), axis=0, keepdims=True)


def lanes(start, width):
    return pl.ds(pl.multiple_of(start, 128), width)


def layer_kernel(back, slot, lead, count, *refs):
    refs = list(refs)
    take = lambda n: [refs.pop(0) for _ in range(n)]
    has_high, has_low = back and slot < count, not back or slot >= lead
    (meta,) = take(1)
    rows_ref, fbias_ref = take(2)
    own_pieces, twin_joined, twin_last = take(12), take(3), take(3)
    (chains_hbm,) = take(1)
    act_hbm, top_hbm = take(2) if has_high else (None, None)
    (grad_hbm,) = take(1) if back and has_low else (None,)
    n_out = 10 if back else 2
    n_scratch = 23 if back else 12
    take(len(refs) - n_out - n_scratch)
    outs = take(n_out)
    scr = take(n_scratch)
    win, wout, wfi, wfo, x_s, qkv, ctx, act, hl, y_s, acc, sems = scr[:12]
    if back:
        (gx16_o, y_o, gx_o, sum_o, fsum_o, sx_o, sctx_o, shid_o, sdf_o, sr_o) = outs
        gy_s, probs, slope, n1_s, n2_s, dr0, dpre, dfn, gx_s, sum_s, fsum_s = scr[12:]
    else:
        y1_o, y_o = outs
    high = meta[0] == 1
    low = meta[0] == 0
    active = (high | low) if has_high and has_low else (high if has_high else low)

    @pl.when(active)
    def _():
        shift = lead if back else 0
        index = jnp.where(high, slot, slot - shift)
        length = meta[1 + count + index]

        def fetch(src, dst, sem):
            pltpu.make_async_copy(src, dst, sem).start()

        if has_high:

            @pl.when(high)
            def _():
                fetch(act_hbm.at[0], x_s, sems.at[4, 0])
                fetch(top_hbm.at[slot], gy_s, sems.at[4, 1])

        if has_low:

            @pl.when(low)
            def _():
                fetch(chains_hbm.at[slot - shift], x_s, sems.at[4, 0])
                if back:
                    fetch(grad_hbm.at[0], gy_s, sems.at[4, 1])

        def load_from(side):
            def one(unit, col, width, dst, group):
                for q in range(4):
                    if side == 0:
                        src, first = own_pieces[unit * 4 + q], col
                    elif q < 3:
                        src, first = twin_joined[q], unit * WIDE + col
                    else:
                        src, first = twin_last[unit], col

                    def body(e, carry):
                        k = q * 4 + e
                        row = pl.multiple_of(meta[1 + 3 * count + unit * BLOCKS + k] * ROWS, 16)
                        fetch(src.at[e, :, first : first + width], dst.at[pl.ds(row, ROWS)], sems.at[group, k])
                        return carry

                    lax.fori_loop(0, 4, body, 0)

            one(0, 0, 3 * D, win, 0)
            one(0, 3 * D, D, wout, 1)
            one(1, 0, FF, wfi, 2)
            one(2, 0, FF, wfo, 3)

        side = meta[1 + 2 * count + index]
        pl.when(side == 0)(lambda: load_from(0))
        pl.when(side != 0)(lambda: load_from(1))

        def landed(dst, group):
            def body(k, carry):
                part = dst.at[pl.ds(0, ROWS)]
                pltpu.make_async_copy(part, part, sems.at[group, k]).wait()
                return carry

            lax.fori_loop(0, BLOCKS, body, 0)

        def small(row):
            return rows_ref[side, row : row + 1, :]

        pltpu.make_async_copy(x_s, x_s, sems.at[4, 0]).wait()
        landed(win, 0)
        x = x_s[...]
        zero_row = jnp.zeros((1, D), F32)
        for n, bias in enumerate((small(0), zero_row, small(1))):
            cols = slice(n * D, (n + 1) * D)
            qkv[:, cols] = (dot_nn(x, win[:, cols]) + bias).astype(BF16)

        low_half = lax.broadcasted_iota(jnp.int32, (1, 2 * HEAD_DIM), 1) < HEAD_DIM
        head_mask = (low_half.astype(F32).astype(BF16), (1 - low_half.astype(F32)).astype(BF16))
        live = lax.broadcasted_iota(jnp.int32, (SEQ, SEQ), 1) < length

        def heads_fwd(pair, carry):
            off = pair * 2 * HEAD_DIM
            q2 = qkv[:, lanes(off, 128)]
            k2 = qkv[:, lanes(D + off, 128)]
            v2 = qkv[:, lanes(2 * D + off, 128)]
            joined = None
            for side in range(2):
                raw = dot_nt(q2 * head_mask[side], k2)
                scores = jnp.where(live, raw * SCALE, NEG)
                expo = jnp.exp(scores - jnp.max(scores, axis=-1, keepdims=True))
                prob = expo * (1.0 / jnp.sum(expo, axis=-1, keepdims=True))
                if back:
                    probs[2 * pair + side] = prob
                part = dot_nn(prob.astype(BF16), v2 * head_mask[side])
                joined = part if joined is None else joined + part
            ctx[:, lanes(off, 128)] = joined.astype(BF16)
            return carry

        lax.fori_loop(0, PAIRS, heads_fwd, 0, unroll=True)

        landed(wout, 1)
        branch = dot_nn(ctx[...], wout[...]) + small(2)
        n1, i1 = norm(x.astype(F32) + branch)
        hidden = n1 * small(4) + small(6)
        if back:
            n1_s[...] = n1
        hl[...] = hidden.astype(BF16)
        acc[...] = hidden
        landed(wfi, 2)
        landed(wfo, 3)

        def ffn_fwd(n, carry):
            cols = lanes(n * CHUNK, CHUNK)
            pre = dot_nn(hl[...], wfi[:, cols]) + fbias_ref[side, :, cols]
            phi = 0.5 * (1.0 + lax.erf(pre * SQRT_HALF))
            act[:, cols] = (pre * phi).astype(BF16)
            if back:
                slope[:, cols] = phi + pre * jnp.exp(-0.5 * pre * pre) * INV_ROOT
            return carry

        lax.fori_loop(0, FF // CHUNK, ffn_fwd, 0, unroll=True)
        branch = dot_nt(act[...], wfo[...]) + small(3)
        n2, i2 = norm(acc[...] + branch)
        y_s[...] = (n2 * small(5) + small(7)).astype(BF16)
        copies = []

        def put(src, dst, sem):
            copy = pltpu.make_async_copy(src, dst, sem)
            copy.start()
            copies.append(copy)

        put(y_s, y_o.at[index], sems.at[5, 0])
        if not back:
            put(y_s, y1_o.at[0], sems.at[5, 1])
        else:
            put(x_s, sx_o.at[index], sems.at[5, 2])
            put(ctx, sctx_o.at[index], sems.at[5, 3])
            put(hl, shid_o.at[index], sems.at[5, 4])
            put(act, sr_o.at[2, index], sems.at[5, 5])
            pltpu.make_async_copy(gy_s, gy_s, sems.at[4, 1]).wait()
            alive = lax.broadcasted_iota(jnp.int32, (SEQ, D), 0) < jnp.where(high, length, SEQ)
            gy = jnp.where(alive, gy_s[...].astype(F32), 0.0)
            sum_s[5:6, :] = col_sum(gy * n2)
            sum_s[7:8, :] = col_sum(gy)
            gr2 = norm_back(gy, n2, i2, small(5))
            dfn[...] = gr2.astype(BF16)
            sum_s[3:4, :] = col_sum(dfn[...])
            put(dfn, sdf_o.at[index], sems.at[5, 6])
            n2_s[...] = gr2

            def ffn_back(n, carry):
                cols = lanes(n * CHUNK, CHUNK)
                d_act = dot_nn(dfn[...], wfo[:, cols])
                d_pre = (d_act * slope[:, cols]).astype(BF16)
                dpre[:, cols] = d_pre
                fsum_s[:, cols] = col_sum(d_pre)
                return carry

            lax.fori_loop(0, FF // CHUNK, ffn_back, 0, unroll=True)
            put(dpre, sr_o.at[1, index], sems.at[5, 7])
            gh = n2_s[...] + dot_nt(dpre[...], wfi[...]).astype(BF16).astype(F32)
            n1 = n1_s[...]
            sum_s[4:5, :] = col_sum(gh * n1)
            sum_s[6:7, :] = col_sum(gh)
            gr1 = norm_back(gh, n1, i1, small(4))
            acc[...] = gr1
            d_attn = gr1.astype(BF16)
            dr0[:, 3 * D :] = d_attn
            sum_s[2:3, :] = col_sum(d_attn)
            gx_s[...] = dot_nt(d_attn, wout[...]).astype(BF16)

            def heads_back(pair, carry):
                off = pair * 2 * HEAD_DIM
                q2 = qkv[:, lanes(off, 128)]
                k2 = qkv[:, lanes(D + off, 128)]
                v2 = qkv[:, lanes(2 * D + off, 128)]
                dc2 = gx_s[:, lanes(off, 128)]
                dq = dk = dv = None
                for side in range(2):
                    prob = probs[2 * pair + side]
                    dch = dc2 * head_mask[side]
                    d_prob = dot_nt(dch, v2)
                    inner = jnp.sum(prob * d_prob, axis=-1, keepdims=True)
                    d_raw = (prob * (d_prob - inner) * SCALE).astype(BF16)
                    a = dot_nn(d_raw, k2 * head_mask[side])
                    b = dot_tn(d_raw, q2 * head_mask[side])
                    c = dot_tn(prob.astype(BF16), dch)
                    dq, dk, dv = (a, b, c) if dq is None else (dq + a, dk + b, dv + c)
                dr0[:, lanes(off, 128)] = dq.astype(BF16)
                dr0[:, lanes(D + off, 128)] = dk.astype(BF16)
                dr0[:, lanes(2 * D + off, 128)] = dv.astype(BF16)
                return carry

            lax.fori_loop(0, PAIRS, heads_back, 0, unroll=True)
            put(dr0, sr_o.at[0, index], sems.at[5, 8])
            sum_s[0:1, :] = col_sum(dr0[:, :D])
            sum_s[1:2, :] = col_sum(dr0[:, 2 * D : 3 * D])
            grad_a = dot_nt(dr0[:, : 3 * D], win[...]) + acc[...]
            n1_s[...] = grad_a
            hl_out = grad_a.astype(BF16)
            gy_s[...] = hl_out
            put(sum_s, sum_o.at[index], sems.at[5, 11])
            put(fsum_s, fsum_o.at[index], sems.at[5, 12])
            put(n1_s, gx_o.at[index], sems.at[5, 9])
            put(gy_s, gx16_o.at[0], sems.at[5, 10])
        for copy in copies:
            copy.wait()


def grad_kernel(unit, at, meta, *refs):
    n_left = 2 if unit == 0 else 1
    left, (right,), outs, (turned,) = refs[:n_left], refs[n_left : n_left + 1], refs[n_left + 1 : n_left + 3], refs[-1:]
    count, half = right.shape[0], D // 2
    n = pl.program_id(0)

    @pl.when(n == 0)
    def _():
        for i in range(n_left):
            for side in range(2):
                chains = [jnp.where(meta[c] == side, left[i][c], jnp.zeros_like(left[i][c])) for c in range(count)]
                turned[i, side * half : (side + 1) * half, :] = jnp.concatenate(chains, 0).T

    pick = jnp.where(n == 3, 1, 0) if unit == 0 else 0
    total = dot_nn(turned[pick], right[...].reshape(count * SEQ, CHUNK)).astype(BF16)
    for side in range(2):
        for block in range(8):
            row = side * half + block * ROWS
            outs[side][meta[count + 2 + (unit * 2 + at) * 8 + block]] = total[row : row + ROWS]


ANY = pl.BlockSpec(memory_space=pl.ANY)
SMEM = pl.BlockSpec(memory_space=pltpu.SMEM)
VMEM = pl.BlockSpec(memory_space=pltpu.VMEM)


def shaped(shape, dtype):
    return jax.ShapeDtypeStruct(shape, dtype)


def saved_shapes(count):
    narrow = shaped((count, SEQ, D), BF16)
    return [
        narrow,
        shaped((count, SEQ, D), F32),
        shaped((count, 8, D), F32),
        shaped((count, 1, FF), F32),
        narrow,
        narrow,
        narrow,
        narrow,
        shaped((3, count, SEQ, WIDE), BF16),
    ]


def layer_call(back, slot, lead, count, meta, rows, fbias, pieces, sources, held):
    scratch = [
        pltpu.VMEM((D, 3 * D), BF16),
        pltpu.VMEM((D, D), BF16),
        pltpu.VMEM((D, FF), BF16),
        pltpu.VMEM((D, FF), BF16),
        pltpu.VMEM((SEQ, D), BF16),
        pltpu.VMEM((SEQ, 3 * D), BF16),
        pltpu.VMEM((SEQ, D), BF16),
        pltpu.VMEM((SEQ, FF), BF16),
        pltpu.VMEM((SEQ, D), BF16),
        pltpu.VMEM((SEQ, D), BF16),
        pltpu.VMEM((SEQ, D), F32),
        pltpu.SemaphoreType.DMA((6, BLOCKS)),
    ]
    if back:
        scratch += [
            pltpu.VMEM((SEQ, D), BF16),
            pltpu.VMEM((HEADS, SEQ, SEQ), F32),
            pltpu.VMEM((SEQ, FF), F32),
            pltpu.VMEM((SEQ, D), F32),
            pltpu.VMEM((SEQ, D), F32),
            pltpu.VMEM((SEQ, WIDE), BF16),
            pltpu.VMEM((SEQ, FF), BF16),
            pltpu.VMEM((SEQ, D), BF16),
            pltpu.VMEM((SEQ, D), BF16),
            pltpu.VMEM((8, D), F32),
            pltpu.VMEM((1, FF), F32),
        ]
    operands = [meta, rows, fbias, *pieces, *sources]
    specs = [SMEM, VMEM, VMEM] + [ANY] * (len(pieces) + len(sources))
    first = [shaped((1, SEQ, D), BF16)]
    kept = saved_shapes(count) if back else [shaped((count, SEQ, D), BF16)]
    aliases = {}
    for at, array in enumerate(held):
        if array is not None:
            aliases[len(operands)] = at + 1
            operands.append(array)
            specs.append(ANY)
    outs = pl.pallas_call(
        functools.partial(layer_kernel, back, slot, lead, count),
        out_shape=first + kept,
        in_specs=specs,
        out_specs=[ANY] * (1 + len(kept)),
        scratch_shapes=scratch,
        input_output_aliases=aliases,
        compiler_params=pltpu.CompilerParams(vmem_limit_bytes=50 * 1024 * 1024),
        cost_estimate=pl.CostEstimate(flops=1, bytes_accessed=1, transcendentals=0),
        name="layer_back" if back else "layer_fwd",
    )(*operands)
    return outs[0], list(outs[1:])


def grad_call(unit, at, meta, left, right):
    count = left[0].shape[0]
    right_spec = pl.BlockSpec((None, count, SEQ, CHUNK), lambda n, m: (unit, 0, 0, n))
    out = shaped((8, ROWS, WIDE), BF16)
    return pl.pallas_call(
        functools.partial(grad_kernel, unit, at),
        out_shape=[out] * 2,
        grid_spec=pltpu.PrefetchScalarGridSpec(
            num_scalar_prefetch=1,
            grid=(WIDE // CHUNK,),
            in_specs=[pl.BlockSpec((count, SEQ, D // 2), lambda n, m: (0, 0, m[count + at]))] * len(left)
            + [right_spec],
            out_specs=[pl.BlockSpec((8, ROWS, CHUNK), lambda n, m: (0, 0, n))] * 2,
            scratch_shapes=[
                pltpu.VMEM((len(left), D, count * SEQ), BF16),
            ],
        ),
        compiler_params=pltpu.CompilerParams(vmem_limit_bytes=50 * 1024 * 1024),
        cost_estimate=pl.CostEstimate(flops=1, bytes_accessed=1, transcendentals=0),
        name="layer_grad",
    )(meta, *left, right)


def swap_bit(array, bit):
    count = lax.axis_size("dp")
    return lax.ppermute(array, "dp", [(i, i ^ (1 << bit)) for i in range(count)])


def swap_section(array):
    return lax.ppermute(array, "section", [(0, 1), (1, 0)])


def along(array, pairs):
    count = lax.axis_size("dp")
    flat = [(s * count + i, t * count + k) for (s, i), (t, k) in pairs]
    return lax.ppermute(array, ("section", "dp"), flat)


def both(first, second):
    return (first.astype(F32) + second.astype(F32)).astype(BF16)


def after(array, *others):
    others = [other for other in others if other is not None]
    return lax.optimization_barrier((array, *others))[0] if others else array


class Waves:
    def __init__(self):
        self.before = ()

    def __call__(self, *sends):
        arrays = lax.optimization_barrier(tuple(array for array, _ in sends) + self.before)[: len(sends)]
        self.before = tuple(move(array) for array, (_, move) in zip(arrays, sends))
        return list(self.before)


def by_bit(bit):
    return lambda array: swap_bit(array, bit)


def by(pairs):
    return lambda array: along(array, pairs)


class Routes:
    def __init__(self, near):
        self.home_to_away = [((h, h * near + j), (1 - h, h * near + j)) for h in range(2) for j in range(near)]
        self.away_to_home = [(b, a) for a, b in self.home_to_away]
        self.straight = [((s, (1 - s) * near + j), (s, s * near + j)) for s in range(2) for j in range(near)]
        self.straight_back = [(b, a) for a, b in self.straight]
        self.crossed = [((s, (1 - s) * near + j), (1 - s, s * near + j)) for s in range(2) for j in range(near)]
        self.up = [((s, j), (s, near + j)) for s in range(2) for j in range(near)]
        self.down = [(b, a) for a, b in self.up]


def per_device(
    inputs,
    cotangent,
    chain_tags,
    chain_lengths,
    attn_in,
    attn_out,
    ffn_in,
    ffn_out,
    proj_bias,
    ffn_bias,
    norm_gain,
    norm_shift,
):
    n_dp = lax.axis_size("dp")
    near = n_dp // 2
    rows = attn_in.shape[2]
    count = inputs.shape[0]
    fast = near == 8 and rows == ROWS
    routes = Routes(near)
    section = lax.axis_index("section")
    place = lax.axis_index("dp")
    half = place // near
    spot = place % near
    at_home = section == half

    native = jnp.concatenate(
        [
            attn_in[0].astype(BF16),
            attn_out[0].astype(BF16),
            ffn_in[0].astype(BF16),
            jnp.swapaxes(ffn_out[0].astype(BF16), 1, 2),
        ],
        -1,
    )
    smalls = jnp.concatenate([proj_bias[0], norm_gain[0], norm_shift[0]], 1).astype(BF16)
    wides = ffn_bias[0].astype(BF16)
    numbers = jnp.concatenate([chain_tags, chain_lengths])
    crossing = routes.straight_back
    if fast:
        mine = jnp.where(section == 0, native[0], native[1])
        twin = jnp.where(section == 0, native[1], native[0])
        wave = Waves()
        cuts = (0, WIDE, 2 * WIDE, 3 * WIDE)

        def bits(held, step):
            return [(held[unit], by_bit(ROTATIONS[unit][step])) for unit in range(3)]

        def joined(held, got):
            return [jnp.concatenate([a, b], 0) for a, b in zip(held, got)]

        def own(blocks):
            return [blocks[None, :, cuts[unit] : cuts[unit + 1]] for unit in range(3)]

        def merged(held):
            return jnp.concatenate(held, -1)

        def one_bit(array, bit):
            return (array, by_bit(bit))

        small = jnp.pad(smalls, ((0, 0), (0, 0), (0, EXTRA - rows)))
        wide = jnp.pad(wides, ((0, 0), (0, 2 * EXTRA - 4 * rows))).reshape(2, 2, EXTRA)
        small = jnp.pad(jnp.concatenate([small, wide], 1), ((0, 0), (0, 6), (0, 0)))
        small_mine = jnp.where(section == 0, small[0], small[1])
        small_twin = jnp.where(section == 0, small[1], small[0])
        home, small_home = wave((twin, by(routes.home_to_away)), (small_twin, by(routes.home_to_away)))
        near_held = own(jnp.where(at_home, mine, home))
        *got, small_straight, cross_a = wave(
            *bits(near_held, 0), (small_mine, by(routes.straight)), (twin[:, : cuts[1]], by(routes.crossed))
        )
        near_held = joined(near_held, got)
        *got, small_crossed, cross_b = wave(
            *bits(near_held, 1), (small_twin, by(routes.crossed)), (twin[:, cuts[1] :], by(routes.crossed))
        )
        small_held = jnp.stack(
            [jnp.where(at_home, small_mine, small_home), jnp.where(at_home, small_straight, small_crossed)]
        )[None]
        near_held = joined(near_held, got)
        *near_far, small_got, straight = wave(
            *bits(near_held, 2), one_bit(small_held, 0), (mine, by(routes.straight))
        )
        small_held = jnp.concatenate([small_held, small_got], 0)
        away_held = own(jnp.where(at_home, straight, jnp.concatenate([cross_a, cross_b], -1)))
        *got, small_got, twin_near_held = wave(
            *bits(away_held, 0), one_bit(small_held, 1), (merged(near_held), swap_section)
        )
        small_held = jnp.concatenate([small_held, small_got], 0)
        away_held = joined(away_held, got)
        *got, small_got, twin_near_far = wave(
            *bits(away_held, 1), one_bit(small_held, 2), (merged(near_far), swap_section)
        )
        small_held = jnp.concatenate([small_held, small_got], 0)
        away_held = joined(away_held, got)
        *away_far, moved, twin_away_held = wave(
            *bits(away_held, 2),
            (jnp.where(half == 1, inputs, cotangent), by(crossing)),
            (merged(away_held), swap_section),
        )
        *twin_last, small_other, numbers_got = wave(
            *[(array, swap_section) for array in away_far], (small_held, swap_section), (numbers, by(crossing))
        )
        pieces = [array for group in zip(near_held, near_far, away_held, away_far) for array in group]
        pieces += [twin_near_held, twin_near_far, twin_away_held, *twin_last]

        def table(masks):
            near_ones = spot ^ jnp.asarray(masks, jnp.int32)
            return jnp.concatenate([near_ones + near * half, near_ones + near * (1 - half)])

        tables = [table(piece_masks(unit)) for unit in range(3)]
        places = [grad_place(spot ^ jnp.arange(8, dtype=jnp.int32), ROTATIONS[2 - unit]) for unit in range(3)]
        row_halves = [half, 1 - half]
        first_side = section
        small_order = (spot ^ jnp.arange(8, dtype=jnp.int32))
        small_order = jnp.stack([small_order + near * half, small_order + near * (1 - half)], 1).reshape(BLOCKS)
        pick = (small_order[None, :] == jnp.arange(BLOCKS, dtype=jnp.int32)[:, None]).astype(BF16)
        row_list, fbias_list = [], []
        for array in (small_held, small_other):
            laid = dot_nn(pick, array.reshape(BLOCKS, 16 * EXTRA)).reshape(BLOCKS, 16, EXTRA)
            row_list.append(jnp.swapaxes(laid[:, :8, :rows], 0, 1).reshape(8, D))
            fbias_list.append(laid[:, 8:10].reshape(BLOCKS, 2 * EXTRA)[:, : 4 * rows].reshape(1, FF))
        rows_all = jnp.stack(row_list)
        fbias_all = jnp.stack(fbias_list)
    else:
        tables = [jnp.arange(BLOCKS, dtype=jnp.int32)] * 3
        places = [jnp.arange(8, dtype=jnp.int32)] * 3
        row_halves = [jnp.int32(0), jnp.int32(1)]
        first_side = 0
        moved = along(jnp.where(half == 1, inputs, cotangent), crossing)
        numbers_got = along(numbers, crossing)

        def whole(array, dim):
            full = lax.all_gather(array, ("section", "dp"), axis=0).reshape((2, n_dp) + array.shape)
            full = lax.dynamic_index_in_dim(full, half, 0, keepdims=False)
            shape = array.shape[:dim] + (n_dp * array.shape[dim],) + array.shape[dim + 1 :]
            return jnp.moveaxis(full, 0, dim).reshape(shape)

        full = whole(native, 1).reshape(2, 4, 4, ROWS, 3 * WIDE)
        pieces = [full[0, q, :, :, unit * WIDE : (unit + 1) * WIDE] for unit in range(3) for q in range(4)]
        pieces += [full[1, q] for q in range(3)]
        pieces += [full[1, 3, :, :, unit * WIDE : (unit + 1) * WIDE] for unit in range(3)]
        rows_all = whole(smalls, 2).astype(F32)
        fbias_all = whole(wides, 1).astype(F32)[:, None, :]

    numbers = jnp.where(at_home, numbers, numbers_got)
    chains = jnp.where(at_home, inputs, moved)
    top_grad = jnp.where(at_home, cotangent, moved)
    sides = numbers[:count] ^ first_side
    meta = jnp.concatenate([half[None].astype(jnp.int32), numbers, sides.astype(jnp.int32)] + tables)
    grad_meta = jnp.concatenate(
        [sides.astype(jnp.int32)]
        + [value[None].astype(jnp.int32) for value in row_halves]
        + [place for unit in range(3) for place in (places[unit], places[unit])]
    )

    lead = 2
    call = functools.partial(layer_call, lead=lead, count=count, rows=rows_all, fbias=fbias_all, pieces=pieces)
    acts, grads, act_low, held = [None] * count, [None] * count, [None], [None] * 9
    token = None

    def forward(c):
        nonlocal token, act_low
        out, act_low = call(False, c, meta=after(meta, token), sources=[chains], held=act_low)
        acts[c], token = along(out, routes.up), out

    for c in range(count):
        forward(c)
    for slot in range(count + lead):
        sources = [chains]
        if slot < count:
            sources += [acts[slot], top_grad]
        if slot >= lead:
            sources.append(grads[slot - lead])
        out, held = call(True, slot, meta=after(meta, token), sources=sources, held=held)
        token = out
        if slot < count:
            grads[slot] = along(out, routes.down)
    act_high, grad_all, sums, fsums, s_x, s_ctx, s_hid, s_dffn, s_right = held
    act_all = jnp.where(half == 0, act_low[0], act_high)

    lefts = {2: [s_dffn], 1: [s_hid], 0: [s_x, s_ctx]}

    def gradient(unit, at, *others):
        return grad_call(unit, at, after(grad_meta, *others), lefts[unit], s_right)

    act_move = (
        jnp.where(section == 1, jnp.concatenate(acts, 0), act_all),
        by([pair for j in range(near) for pair in (((1, near + j), (0, near + j)), ((0, near + j), (1, j)))]),
    )
    grad_move = (
        jnp.where(section == 0, jnp.concatenate(grads, 0), grad_all.astype(BF16)),
        by([pair for j in range(near) for pair in (((0, j), (1, j)), ((1, j), (0, near + j)))]),
    )

    chosen = (sides[None, :] == jnp.arange(2, dtype=jnp.int32)[:, None]).astype(F32)
    row_sums = jnp.sum(chosen[:, :, None, None] * sums[None], axis=1)
    fbias_sums = jnp.sum(chosen[:, :, None] * fsums[None, :, 0], axis=1)
    small_grads = jnp.concatenate([jnp.swapaxes(row_sums, 1, 2), fbias_sums.reshape(2, D, 4)], -1)

    if fast:
        laid = jnp.concatenate([small_grads, jnp.zeros((2, D, EXTRA - 12), F32)], -1).astype(BF16)
        laid = jnp.swapaxes(laid.reshape(2, BLOCKS, ROWS, EXTRA), 0, 1)
        small_places = table(grad_masks(ROTATIONS[0]))
        pick = (small_places[:, None] == jnp.arange(BLOCKS, dtype=jnp.int32)[None, :]).astype(BF16)
        laid = dot_nn(pick, laid.reshape(BLOCKS, -1)).astype(BF16).reshape(2, 8, 2, ROWS, EXTRA)
        laid = jnp.transpose(laid, (2, 1, 0, 3, 4)).reshape(2, 8, 2 * ROWS, EXTRA)
        wave = Waves()

        def reduce_step(keep, got, step):
            width = 4 >> step
            send = [both(a[width:], b[width:]) for a, b in zip(keep, got)]
            return [both(a[:width], b[:width]) for a, b in zip(keep, got)], send

        def bits_out(send, step):
            return [(send[i], by_bit(ROTATIONS[i % 3][step])) for i in range(len(send))]

        units = (2, 1, 0)
        totals = {(unit, 1): gradient(unit, 1) for unit in units}
        keep = [totals[unit, 1][0] for unit in units] + [laid[0]]
        got = [swap_section(totals[unit, 1][1]) for unit in units] + [swap_section(laid[1])]
        near_got = []
        for step in range(3):
            if step == 0:
                totals[2, 0] = gradient(2, 0, totals[0, 1][0])
            keep, send = reduce_step(keep, got, step)
            if step == 0:
                totals[1, 0] = gradient(1, 0, *send)
                totals[0, 0] = gradient(0, 0, totals[1, 0][0])
            *got, other = wave(*bits_out(send, step), (totals[units[step], 0][1], swap_section))
            near_got.append(other)
        far_sum = [(a[0].astype(F32) + b[0].astype(F32)).astype(BF16) for a, b in zip(keep, got)]
        small_near = far_sum[3][:ROWS]
        far_sum = jnp.concatenate(far_sum[:3] + [far_sum[3][ROWS:]], -1)

        keep = [totals[unit, 0][0] for unit in units]
        keep, send = reduce_step(keep, near_got, 0)
        *got, straight, act_other = wave(*bits_out(send, 0), (far_sum, by(routes.straight_back)), act_move)
        keep, send = reduce_step(keep, got, 1)
        *got, cross_a, grad_other = wave(
            *bits_out(send, 1), (far_sum[:, : 2 * WIDE], by(routes.crossed)), grad_move
        )
        keep, send = reduce_step(keep, got, 2)
        *got, cross_b = wave(*bits_out(send, 2), (far_sum[:, 2 * WIDE :], by(routes.crossed)))
        near_sum = [a[0].astype(F32) + b[0].astype(F32) for a, b in zip(keep, got)] + [small_near.astype(F32)]
        (beside,) = wave((jnp.concatenate(near_sum, -1).astype(BF16), by(routes.away_to_home)))
        crossed = jnp.concatenate([cross_a, cross_b], -1)

        def settle(i, width):
            cols = slice(i * WIDE, i * WIDE + width)
            mine = jnp.where(at_home, near_sum[i], straight[:, cols].astype(F32))
            twin = jnp.where(at_home, beside[:, cols].astype(F32), crossed[:, cols].astype(F32))
            return jnp.stack([jnp.where(section == 0, mine, twin), jnp.where(section == 0, twin, mine)])

        unit_out = [None] * 3
        for i, unit in enumerate(units):
            unit_out[unit] = settle(i, WIDE)
        small_out = settle(3, EXTRA)
    else:

        def summed(array):
            layers = jnp.stack([jnp.where(half == layer, array, jnp.zeros_like(array)) for layer in range(2)])
            layers = jnp.swapaxes(layers, 1, 2).reshape(2 * n_dp, rows, 2, array.shape[-1])
            out = lax.psum_scatter(layers, ("section", "dp"), scatter_dimension=0, tiled=True)
            return jnp.swapaxes(out[0], 0, 1)

        unit_out = []
        totals = {(unit, at): gradient(unit, at) for unit in range(3) for at in range(2)}
        for unit in range(3):
            group = [
                jnp.concatenate([totals[unit, 0][side], totals[unit, 1][side]], 0).reshape(D, WIDE) for side in range(2)
            ]
            unit_out.append(summed(jnp.stack(group).astype(F32)))
        small_out = summed(small_grads)
        act_other, grad_other = act_move[1](act_move[0]), grad_move[1](grad_move[0])

    act_out = jnp.where(at_home, act_all, act_other)
    grad_out = jnp.where(at_home, grad_all, grad_other.astype(F32))

    turned = jnp.swapaxes(small_out[:, :, :8], 1, 2)
    return (
        act_out[None],
        grad_out[None],
        unit_out[0][None, :, :, : 3 * D],
        unit_out[0][None, :, :, 3 * D :],
        unit_out[1][None],
        jnp.swapaxes(unit_out[2], 1, 2)[None],
        turned[None, :, 0:4],
        small_out[:, :, 8:12].reshape(1, 2, 4 * rows),
        turned[None, :, 4:6],
        turned[None, :, 6:8],
    )


def solution(mesh):
    in_specs = (
        P("dp", None, None),
        P("dp", None, None),
        P("dp"),
        P("dp"),
        P("section", None, "dp", None),
        P("section", None, "dp", None),
        P("section", None, "dp", None),
        P("section", None, None, "dp"),
        P("section", None, None, "dp"),
        P("section", None, "dp"),
        P("section", None, None, "dp"),
        P("section", None, None, "dp"),
    )
    out_specs = (
        P("section", "dp", None, None),
        P("section", "dp", None, None),
        P("section", None, "dp", None),
        P("section", None, "dp", None),
        P("section", None, "dp", None),
        P("section", None, None, "dp"),
        P("section", None, None, "dp"),
        P("section", None, "dp"),
        P("section", None, None, "dp"),
        P("section", None, None, "dp"),
    )
    return jax.shard_map(
        per_device, mesh=mesh, in_specs=in_specs, out_specs=out_specs, check_vma=False
    )
```

```python
import functools

import jax
import jax.numpy as jnp
from jax import lax
from jax.experimental import pallas as pl
from jax.experimental.pallas import tpu as pltpu
from jax.sharding import PartitionSpec as P

D = 768
HEADS = 12
HEAD_DIM = 64
FF = 3072
SEQ = 160
PAIRS = HEADS // 2
BLOCKS = 16
ROWS = D // BLOCKS
WIDE = 3072
EXTRA = 128
CHUNK = 768

EPS = 1e-05
NEG = -1e30
SQRT_HALF = 0.7071067811865476
INV_ROOT = 0.3989422804014327
SCALE = HEAD_DIM**-0.5

ROTATIONS = ((0, 1, 2), (1, 2, 0), (2, 0, 1))
F32 = jnp.float32
BF16 = jnp.bfloat16


def piece_masks(unit):
    one, two, three = (1 << bit for bit in ROTATIONS[unit])
    return [far | mask for far in (0, three) for mask in (0, one, two, two | one)]


def grad_masks(rotation):
    one, two, three = (1 << bit for bit in rotation)
    return [(one if p & 4 else 0) | (two if p & 2 else 0) | (three if p & 1 else 0) for p in range(8)]


def grad_place(mask, rotation):
    one, two, three = rotation
    return ((mask >> one) & 1) * 4 + ((mask >> two) & 1) * 2 + ((mask >> three) & 1)


def dot_nn(a, b):
    return jnp.dot(a, b, preferred_element_type=F32)


def dot_nt(a, b):
    return lax.dot_general(a, b, (((1,), (1,)), ((), ())), preferred_element_type=F32)


def dot_tn(a, b):
    return lax.dot_general(a, b, (((0,), (0,)), ((), ())), preferred_element_type=F32)


def row_mean(a):
    return jnp.sum(a, axis=-1, keepdims=True) * (1.0 / D)


def norm(summed):
    center = summed - row_mean(summed)
    inverse = lax.rsqrt(row_mean(center * center) + EPS)
    return center * inverse, inverse


def norm_back(grad, normed, inverse, gain):
    scaled = grad * gain
    return inverse * (scaled - row_mean(scaled) - normed * row_mean(scaled * normed))


def col_sum(a):
    return jnp.sum(a.astype(F32), axis=0, keepdims=True)


def lanes(start, width):
    return pl.ds(pl.multiple_of(start, 128), width)


def layer_kernel(back, slot, lead, count, *refs):
    refs = list(refs)
    take = lambda n: [refs.pop(0) for _ in range(n)]
    has_high, has_low = back and slot < count, not back or slot >= lead
    (meta,) = take(1)
    rows_ref, fbias_ref = take(2)
    own_pieces, twin_joined, twin_last = take(12), take(3), take(3)
    (chains_hbm,) = take(1)
    act_hbm, top_hbm = take(2) if has_high else (None, None)
    (grad_hbm,) = take(1) if back and has_low else (None,)
    n_out = 10 if back else 2
    n_scratch = 23 if back else 12
    take(len(refs) - n_out - n_scratch)
    outs = take(n_out)
    scr = take(n_scratch)
    win, wout, wfi, wfo, x_s, qkv, ctx, act, hl, y_s, acc, sems = scr[:12]
    if back:
        (gx16_o, y_o, gx_o, sum_o, fsum_o, sx_o, sctx_o, shid_o, sdf_o, sr_o) = outs
        gy_s, probs, slope, n1_s, n2_s, dr0, dpre, dfn, gx_s, sum_s, fsum_s = scr[12:]
    else:
        y1_o, y_o = outs
    high = meta[0] == 1
    low = meta[0] == 0
    active = (high | low) if has_high and has_low else (high if has_high else low)

    @pl.when(active)
    def _():
        shift = lead if back else 0
        index = jnp.where(high, slot, slot - shift)
        length = meta[1 + count + index]

        def fetch(src, dst, sem):
            pltpu.make_async_copy(src, dst, sem).start()

        if has_high:

            @pl.when(high)
            def _():
                fetch(act_hbm.at[0], x_s, sems.at[4, 0])
                fetch(top_hbm.at[slot], gy_s, sems.at[4, 1])

        if has_low:

            @pl.when(low)
            def _():
                fetch(chains_hbm.at[slot - shift], x_s, sems.at[4, 0])
                if back:
                    fetch(grad_hbm.at[0], gy_s, sems.at[4, 1])

        def load_from(side):
            def one(unit, col, width, dst, group):
                for q in range(4):
                    if side == 0:
                        src, first = own_pieces[unit * 4 + q], col
                    elif q < 3:
                        src, first = twin_joined[q], unit * WIDE + col
                    else:
                        src, first = twin_last[unit], col

                    def body(e, carry):
                        k = q * 4 + e
                        row = pl.multiple_of(meta[1 + 3 * count + unit * BLOCKS + k] * ROWS, 16)
                        fetch(src.at[e, :, first : first + width], dst.at[pl.ds(row, ROWS)], sems.at[group, k])
                        return carry

                    lax.fori_loop(0, 4, body, 0)

            one(0, 0, 3 * D, win, 0)
            one(0, 3 * D, D, wout, 1)
            one(1, 0, FF, wfi, 2)
            one(2, 0, FF, wfo, 3)

        side = meta[1 + 2 * count + index]
        pl.when(side == 0)(lambda: load_from(0))
        pl.when(side != 0)(lambda: load_from(1))

        def landed(dst, group):
            def body(k, carry):
                part = dst.at[pl.ds(0, ROWS)]
                pltpu.make_async_copy(part, part, sems.at[group, k]).wait()
                return carry

            lax.fori_loop(0, BLOCKS, body, 0)

        def small(row):
            return rows_ref[side, row : row + 1, :]

        pltpu.make_async_copy(x_s, x_s, sems.at[4, 0]).wait()
        landed(win, 0)
        x = x_s[...]
        zero_row = jnp.zeros((1, D), F32)
        for n, bias in enumerate((small(0), zero_row, small(1))):
            cols = slice(n * D, (n + 1) * D)
            qkv[:, cols] = (dot_nn(x, win[:, cols]) + bias).astype(BF16)

        low_half = lax.broadcasted_iota(jnp.int32, (1, 2 * HEAD_DIM), 1) < HEAD_DIM
        head_mask = (low_half.astype(F32).astype(BF16), (1 - low_half.astype(F32)).astype(BF16))
        live = lax.broadcasted_iota(jnp.int32, (SEQ, SEQ), 1) < length

        def heads_fwd(pair, carry):
            off = pair * 2 * HEAD_DIM
            q2 = qkv[:, lanes(off, 128)]
            k2 = qkv[:, lanes(D + off, 128)]
            v2 = qkv[:, lanes(2 * D + off, 128)]
            joined = None
            for side in range(2):
                raw = dot_nt(q2 * head_mask[side], k2)
                scores = jnp.where(live, raw * SCALE, NEG)
                expo = jnp.exp(scores - jnp.max(scores, axis=-1, keepdims=True))
                prob = expo * (1.0 / jnp.sum(expo, axis=-1, keepdims=True))
                if back:
                    probs[2 * pair + side] = prob
                part = dot_nn(prob.astype(BF16), v2 * head_mask[side])
                joined = part if joined is None else joined + part
            ctx[:, lanes(off, 128)] = joined.astype(BF16)
            return carry

        lax.fori_loop(0, PAIRS, heads_fwd, 0, unroll=True)

        landed(wout, 1)
        branch = dot_nn(ctx[...], wout[...]) + small(2)
        n1, i1 = norm(x.astype(F32) + branch)
        hidden = n1 * small(4) + small(6)
        if back:
            n1_s[...] = n1
        hl[...] = hidden.astype(BF16)
        acc[...] = hidden
        landed(wfi, 2)
        landed(wfo, 3)

        def ffn_fwd(n, carry):
            cols = lanes(n * CHUNK, CHUNK)
            pre = dot_nn(hl[...], wfi[:, cols]) + fbias_ref[side, :, cols]
            phi = 0.5 * (1.0 + lax.erf(pre * SQRT_HALF))
            act[:, cols] = (pre * phi).astype(BF16)
            if back:
                slope[:, cols] = phi + pre * jnp.exp(-0.5 * pre * pre) * INV_ROOT
            return carry

        lax.fori_loop(0, FF // CHUNK, ffn_fwd, 0, unroll=True)
        branch = dot_nt(act[...], wfo[...]) + small(3)
        n2, i2 = norm(acc[...] + branch)
        y_s[...] = (n2 * small(5) + small(7)).astype(BF16)
        copies = []

        def put(src, dst, sem):
            copy = pltpu.make_async_copy(src, dst, sem)
            copy.start()
            copies.append(copy)

        put(y_s, y_o.at[index], sems.at[5, 0])
        if not back:
            put(y_s, y1_o.at[0], sems.at[5, 1])
        else:
            put(x_s, sx_o.at[index], sems.at[5, 2])
            put(ctx, sctx_o.at[index], sems.at[5, 3])
            put(hl, shid_o.at[index], sems.at[5, 4])
            put(act, sr_o.at[2, index], sems.at[5, 5])
            pltpu.make_async_copy(gy_s, gy_s, sems.at[4, 1]).wait()
            alive = lax.broadcasted_iota(jnp.int32, (SEQ, D), 0) < jnp.where(high, length, SEQ)
            gy = jnp.where(alive, gy_s[...].astype(F32), 0.0)
            sum_s[5:6, :] = col_sum(gy * n2)
            sum_s[7:8, :] = col_sum(gy)
            gr2 = norm_back(gy, n2, i2, small(5))
            dfn[...] = gr2.astype(BF16)
            sum_s[3:4, :] = col_sum(dfn[...])
            put(dfn, sdf_o.at[index], sems.at[5, 6])
            n2_s[...] = gr2

            def ffn_back(n, carry):
                cols = lanes(n * CHUNK, CHUNK)
                d_act = dot_nn(dfn[...], wfo[:, cols])
                d_pre = (d_act * slope[:, cols]).astype(BF16)
                dpre[:, cols] = d_pre
                fsum_s[:, cols] = col_sum(d_pre)
                return carry

            lax.fori_loop(0, FF // CHUNK, ffn_back, 0, unroll=True)
            put(dpre, sr_o.at[1, index], sems.at[5, 7])
            gh = n2_s[...] + dot_nt(dpre[...], wfi[...]).astype(BF16).astype(F32)
            n1 = n1_s[...]
            sum_s[4:5, :] = col_sum(gh * n1)
            sum_s[6:7, :] = col_sum(gh)
            gr1 = norm_back(gh, n1, i1, small(4))
            acc[...] = gr1
            d_attn = gr1.astype(BF16)
            dr0[:, 3 * D :] = d_attn
            sum_s[2:3, :] = col_sum(d_attn)
            gx_s[...] = dot_nt(d_attn, wout[...]).astype(BF16)

            def heads_back(pair, carry):
                off = pair * 2 * HEAD_DIM
                q2 = qkv[:, lanes(off, 128)]
                k2 = qkv[:, lanes(D + off, 128)]
                v2 = qkv[:, lanes(2 * D + off, 128)]
                dc2 = gx_s[:, lanes(off, 128)]
                dq = dk = dv = None
                for side in range(2):
                    prob = probs[2 * pair + side]
                    dch = dc2 * head_mask[side]
                    d_prob = dot_nt(dch, v2)
                    inner = jnp.sum(prob * d_prob, axis=-1, keepdims=True)
                    d_raw = (prob * (d_prob - inner) * SCALE).astype(BF16)
                    a = dot_nn(d_raw, k2 * head_mask[side])
                    b = dot_tn(d_raw, q2 * head_mask[side])
                    c = dot_tn(prob.astype(BF16), dch)
                    dq, dk, dv = (a, b, c) if dq is None else (dq + a, dk + b, dv + c)
                dr0[:, lanes(off, 128)] = dq.astype(BF16)
                dr0[:, lanes(D + off, 128)] = dk.astype(BF16)
                dr0[:, lanes(2 * D + off, 128)] = dv.astype(BF16)
                return carry

            lax.fori_loop(0, PAIRS, heads_back, 0, unroll=True)
            put(dr0, sr_o.at[0, index], sems.at[5, 8])
            sum_s[0:1, :] = col_sum(dr0[:, :D])
            sum_s[1:2, :] = col_sum(dr0[:, 2 * D : 3 * D])
            grad_a = dot_nt(dr0[:, : 3 * D], win[...]) + acc[...]
            n1_s[...] = grad_a
            hl_out = grad_a.astype(BF16)
            gy_s[...] = hl_out
            put(sum_s, sum_o.at[index], sems.at[5, 11])
            put(fsum_s, fsum_o.at[index], sems.at[5, 12])
            put(n1_s, gx_o.at[index], sems.at[5, 9])
            put(gy_s, gx16_o.at[0], sems.at[5, 10])
        for copy in copies:
            copy.wait()


def grad_kernel(unit, at, meta, *refs):
    n_left = 2 if unit == 0 else 1
    left, (right,), outs, (turned,) = refs[:n_left], refs[n_left : n_left + 1], refs[n_left + 1 : n_left + 3], refs[-1:]
    count = right.shape[0]
    n = pl.program_id(0)
    chain_of = [[meta[c] for c in range(count)], [meta[count - 1 - c] for c in range(count)]]

    @pl.when(n == 0)
    def _():
        for i in range(n_left):
            for side in range(2):
                turned[i, side] = jnp.concatenate([left[i][c] for c in chain_of[side]], 0).T

    pick = jnp.where(n == 3, 1, 0) if unit == 0 else 0

    def put(side, total):
        for block in range(8):
            place = meta[count + 3 + (unit * 2 + at) * 8 + block]
            outs[side][place] = total[block * ROWS : (block + 1) * ROWS]

    def with_first(first):
        @pl.when(meta[count] == first)
        def _():
            for side, many in ((0, first), (1, count - first)):
                if many:
                    rows = jnp.concatenate([right[c] for c in chain_of[side][:many]], 0)
                    put(side, dot_nn(turned[pick, side, :, : many * SEQ], rows).astype(BF16))
                else:
                    put(side, jnp.zeros((D // 2, CHUNK), BF16))

    for first in range(count + 1):
        with_first(first)


ANY = pl.BlockSpec(memory_space=pl.ANY)
SMEM = pl.BlockSpec(memory_space=pltpu.SMEM)
VMEM = pl.BlockSpec(memory_space=pltpu.VMEM)


def shaped(shape, dtype):
    return jax.ShapeDtypeStruct(shape, dtype)


def saved_shapes(count):
    narrow = shaped((count, SEQ, D), BF16)
    return [
        narrow,
        shaped((count, SEQ, D), F32),
        shaped((count, 8, D), F32),
        shaped((count, 1, FF), F32),
        narrow,
        narrow,
        narrow,
        narrow,
        shaped((3, count, SEQ, WIDE), BF16),
    ]


def layer_call(back, slot, lead, count, meta, rows, fbias, pieces, sources, held):
    scratch = [
        pltpu.VMEM((D, 3 * D), BF16),
        pltpu.VMEM((D, D), BF16),
        pltpu.VMEM((D, FF), BF16),
        pltpu.VMEM((D, FF), BF16),
        pltpu.VMEM((SEQ, D), BF16),
        pltpu.VMEM((SEQ, 3 * D), BF16),
        pltpu.VMEM((SEQ, D), BF16),
        pltpu.VMEM((SEQ, FF), BF16),
        pltpu.VMEM((SEQ, D), BF16),
        pltpu.VMEM((SEQ, D), BF16),
        pltpu.VMEM((SEQ, D), F32),
        pltpu.SemaphoreType.DMA((6, BLOCKS)),
    ]
    if back:
        scratch += [
            pltpu.VMEM((SEQ, D), BF16),
            pltpu.VMEM((HEADS, SEQ, SEQ), F32),
            pltpu.VMEM((SEQ, FF), F32),
            pltpu.VMEM((SEQ, D), F32),
            pltpu.VMEM((SEQ, D), F32),
            pltpu.VMEM((SEQ, WIDE), BF16),
            pltpu.VMEM((SEQ, FF), BF16),
            pltpu.VMEM((SEQ, D), BF16),
            pltpu.VMEM((SEQ, D), BF16),
            pltpu.VMEM((8, D), F32),
            pltpu.VMEM((1, FF), F32),
        ]
    operands = [meta, rows, fbias, *pieces, *sources]
    specs = [SMEM, VMEM, VMEM] + [ANY] * (len(pieces) + len(sources))
    first = [shaped((1, SEQ, D), BF16)]
    kept = saved_shapes(count) if back else [shaped((count, SEQ, D), BF16)]
    aliases = {}
    for at, array in enumerate(held):
        if array is not None:
            aliases[len(operands)] = at + 1
            operands.append(array)
            specs.append(ANY)
    outs = pl.pallas_call(
        functools.partial(layer_kernel, back, slot, lead, count),
        out_shape=first + kept,
        in_specs=specs,
        out_specs=[ANY] * (1 + len(kept)),
        scratch_shapes=scratch,
        input_output_aliases=aliases,
        compiler_params=pltpu.CompilerParams(vmem_limit_bytes=50 * 1024 * 1024),
        cost_estimate=pl.CostEstimate(flops=1, bytes_accessed=1, transcendentals=0),
        name="layer_back" if back else "layer_fwd",
    )(*operands)
    return outs[0], list(outs[1:])


def grad_call(unit, at, meta, left, right):
    count = left[0].shape[0]
    right_spec = pl.BlockSpec((None, count, SEQ, CHUNK), lambda n, m: (unit, 0, 0, n))
    out = shaped((8, ROWS, WIDE), BF16)
    return pl.pallas_call(
        functools.partial(grad_kernel, unit, at),
        out_shape=[out] * 2,
        grid_spec=pltpu.PrefetchScalarGridSpec(
            num_scalar_prefetch=1,
            grid=(WIDE // CHUNK,),
            in_specs=[pl.BlockSpec((count, SEQ, D // 2), lambda n, m: (0, 0, m[count + 1 + at]))] * len(left)
            + [right_spec],
            out_specs=[pl.BlockSpec((8, ROWS, CHUNK), lambda n, m: (0, 0, n))] * 2,
            scratch_shapes=[
                pltpu.VMEM((len(left), 2, D // 2, count * SEQ), BF16),
            ],
        ),
        compiler_params=pltpu.CompilerParams(vmem_limit_bytes=50 * 1024 * 1024),
        cost_estimate=pl.CostEstimate(flops=1, bytes_accessed=1, transcendentals=0),
        name="layer_grad",
    )(meta, *left, right)


def swap_bit(array, bit):
    count = lax.axis_size("dp")
    return lax.ppermute(array, "dp", [(i, i ^ (1 << bit)) for i in range(count)])


def swap_section(array):
    return lax.ppermute(array, "section", [(0, 1), (1, 0)])


def along(array, pairs):
    count = lax.axis_size("dp")
    flat = [(s * count + i, t * count + k) for (s, i), (t, k) in pairs]
    return lax.ppermute(array, ("section", "dp"), flat)


def both(first, second):
    return (first.astype(F32) + second.astype(F32)).astype(BF16)


def after(array, *others):
    others = [other for other in others if other is not None]
    return lax.optimization_barrier((array, *others))[0] if others else array


class Waves:
    def __init__(self):
        self.before = ()

    def __call__(self, *sends):
        arrays = lax.optimization_barrier(tuple(array for array, _ in sends) + self.before)[: len(sends)]
        self.before = tuple(move(array) for array, (_, move) in zip(arrays, sends))
        return list(self.before)


def by_bit(bit):
    return lambda array: swap_bit(array, bit)


def by(pairs):
    return lambda array: along(array, pairs)


class Routes:
    def __init__(self, near):
        self.home_to_away = [((h, h * near + j), (1 - h, h * near + j)) for h in range(2) for j in range(near)]
        self.away_to_home = [(b, a) for a, b in self.home_to_away]
        self.straight = [((s, (1 - s) * near + j), (s, s * near + j)) for s in range(2) for j in range(near)]
        self.straight_back = [(b, a) for a, b in self.straight]
        self.crossed = [((s, (1 - s) * near + j), (1 - s, s * near + j)) for s in range(2) for j in range(near)]
        self.up = [((s, j), (s, near + j)) for s in range(2) for j in range(near)]
        self.down = [(b, a) for a, b in self.up]


def per_device(
    inputs,
    cotangent,
    chain_tags,
    chain_lengths,
    attn_in,
    attn_out,
    ffn_in,
    ffn_out,
    proj_bias,
    ffn_bias,
    norm_gain,
    norm_shift,
):
    n_dp = lax.axis_size("dp")
    near = n_dp // 2
    rows = attn_in.shape[2]
    count = inputs.shape[0]
    fast = near == 8 and rows == ROWS
    routes = Routes(near)
    section = lax.axis_index("section")
    place = lax.axis_index("dp")
    half = place // near
    spot = place % near
    at_home = section == half

    native = jnp.concatenate(
        [
            attn_in[0].astype(BF16),
            attn_out[0].astype(BF16),
            ffn_in[0].astype(BF16),
            jnp.swapaxes(ffn_out[0].astype(BF16), 1, 2),
        ],
        -1,
    )
    smalls = jnp.concatenate([proj_bias[0], norm_gain[0], norm_shift[0]], 1).astype(BF16)
    wides = ffn_bias[0].astype(BF16)
    numbers = jnp.concatenate([chain_tags, chain_lengths])
    crossing = routes.straight_back
    if fast:
        mine = jnp.where(section == 0, native[0], native[1])
        twin = jnp.where(section == 0, native[1], native[0])
        wave = Waves()
        cuts = (0, WIDE, 2 * WIDE, 3 * WIDE)

        def bits(held, step):
            return [(held[unit], by_bit(ROTATIONS[unit][step])) for unit in range(3)]

        def joined(held, got):
            return [jnp.concatenate([a, b], 0) for a, b in zip(held, got)]

        def own(blocks):
            return [blocks[None, :, cuts[unit] : cuts[unit + 1]] for unit in range(3)]

        def merged(held):
            return jnp.concatenate(held, -1)

        def one_bit(array, bit):
            return (array, by_bit(bit))

        small = jnp.pad(smalls, ((0, 0), (0, 0), (0, EXTRA - rows)))
        wide = jnp.pad(wides, ((0, 0), (0, 2 * EXTRA - 4 * rows))).reshape(2, 2, EXTRA)
        small = jnp.pad(jnp.concatenate([small, wide], 1), ((0, 0), (0, 6), (0, 0)))
        small = small.at[:, 10, : 2 * count].set(numbers.astype(BF16)[None])
        small_mine = jnp.where(section == 0, small[0], small[1])
        small_twin = jnp.where(section == 0, small[1], small[0])
        home, small_home = wave((twin, by(routes.home_to_away)), (small_twin, by(routes.home_to_away)))
        near_held = own(jnp.where(at_home, mine, home))
        *got, small_straight, cross_a = wave(
            *bits(near_held, 0), (small_mine, by(routes.straight)), (twin[:, : cuts[1]], by(routes.crossed))
        )
        near_held = joined(near_held, got)
        *got, small_crossed, cross_b = wave(
            *bits(near_held, 1), (small_twin, by(routes.crossed)), (twin[:, cuts[1] :], by(routes.crossed))
        )
        small_held = jnp.stack(
            [jnp.where(at_home, small_mine, small_home), jnp.where(at_home, small_straight, small_crossed)]
        )[None]
        near_held = joined(near_held, got)
        *near_far, small_got, straight = wave(
            *bits(near_held, 2), one_bit(small_held, 0), (mine, by(routes.straight))
        )
        small_held = jnp.concatenate([small_held, small_got], 0)
        away_held = own(jnp.where(at_home, straight, jnp.concatenate([cross_a, cross_b], -1)))
        *got, small_got, twin_near_held = wave(
            *bits(away_held, 0), one_bit(small_held, 1), (merged(near_held), swap_section)
        )
        small_held = jnp.concatenate([small_held, small_got], 0)
        away_held = joined(away_held, got)
        *got, small_got, twin_near_far = wave(
            *bits(away_held, 1), one_bit(small_held, 2), (merged(near_far), swap_section)
        )
        small_held = jnp.concatenate([small_held, small_got], 0)
        away_held = joined(away_held, got)
        *away_far, moved, twin_away_held = wave(
            *bits(away_held, 2),
            (jnp.where(half == 1, inputs, cotangent), by(crossing)),
            (merged(away_held), swap_section),
        )
        *twin_last, small_other = wave(*[(array, swap_section) for array in away_far], (small_held, swap_section))
        numbers_got = small_crossed[10, : 2 * count].astype(F32).astype(jnp.int32)
        pieces = [array for group in zip(near_held, near_far, away_held, away_far) for array in group]
        pieces += [twin_near_held, twin_near_far, twin_away_held, *twin_last]

        def table(masks):
            near_ones = spot ^ jnp.asarray(masks, jnp.int32)
            return jnp.concatenate([near_ones + near * half, near_ones + near * (1 - half)])

        tables = [table(piece_masks(unit)) for unit in range(3)]
        places = [grad_place(spot ^ jnp.arange(8, dtype=jnp.int32), ROTATIONS[2 - unit]) for unit in range(3)]
        row_halves = [half, 1 - half]
        first_side = section
        small_order = (spot ^ jnp.arange(8, dtype=jnp.int32))
        small_order = jnp.stack([small_order + near * half, small_order + near * (1 - half)], 1).reshape(BLOCKS)
        pick = (small_order[None, :] == jnp.arange(BLOCKS, dtype=jnp.int32)[:, None]).astype(BF16)
        row_list, fbias_list = [], []
        for array in (small_held, small_other):
            laid = dot_nn(pick, array.reshape(BLOCKS, 16 * EXTRA)).reshape(BLOCKS, 16, EXTRA)
            row_list.append(jnp.swapaxes(laid[:, :8, :rows], 0, 1).reshape(8, D))
            fbias_list.append(laid[:, 8:10].reshape(BLOCKS, 2 * EXTRA)[:, : 4 * rows].reshape(1, FF))
        rows_all = jnp.stack(row_list)
        fbias_all = jnp.stack(fbias_list)
    else:
        tables = [jnp.arange(BLOCKS, dtype=jnp.int32)] * 3
        places = [jnp.arange(8, dtype=jnp.int32)] * 3
        row_halves = [jnp.int32(0), jnp.int32(1)]
        first_side = 0
        moved = along(jnp.where(half == 1, inputs, cotangent), crossing)
        numbers_got = along(numbers, crossing)

        def whole(array, dim):
            full = lax.all_gather(array, ("section", "dp"), axis=0).reshape((2, n_dp) + array.shape)
            full = lax.dynamic_index_in_dim(full, half, 0, keepdims=False)
            shape = array.shape[:dim] + (n_dp * array.shape[dim],) + array.shape[dim + 1 :]
            return jnp.moveaxis(full, 0, dim).reshape(shape)

        full = whole(native, 1).reshape(2, 4, 4, ROWS, 3 * WIDE)
        pieces = [full[0, q, :, :, unit * WIDE : (unit + 1) * WIDE] for unit in range(3) for q in range(4)]
        pieces += [full[1, q] for q in range(3)]
        pieces += [full[1, 3, :, :, unit * WIDE : (unit + 1) * WIDE] for unit in range(3)]
        rows_all = whole(smalls, 2).astype(F32)
        fbias_all = whole(wides, 1).astype(F32)[:, None, :]

    numbers = jnp.where(at_home, numbers, numbers_got)
    chains = jnp.where(at_home, inputs, moved)
    top_grad = jnp.where(at_home, cotangent, moved)
    sides = numbers[:count] ^ first_side
    meta = jnp.concatenate([half[None].astype(jnp.int32), numbers, sides.astype(jnp.int32)] + tables)
    later = jnp.arange(count)[:, None] < jnp.arange(count)[None, :]
    rank = jnp.sum((sides[:, None] > sides[None, :]) | ((sides[:, None] == sides[None, :]) & later.T), axis=1)
    sorted_chains = jnp.sum(
        jnp.where(rank[None, :] == jnp.arange(count)[:, None], jnp.arange(count)[None, :], 0), axis=1
    )
    grad_meta = jnp.concatenate(
        [sorted_chains.astype(jnp.int32), jnp.sum(1 - sides)[None].astype(jnp.int32)]
        + [value[None].astype(jnp.int32) for value in row_halves]
        + [place for unit in range(3) for place in (places[unit], places[unit])]
    )

    lead = 2
    call = functools.partial(layer_call, lead=lead, count=count, rows=rows_all, fbias=fbias_all, pieces=pieces)
    acts, grads, act_low, held = [None] * count, [None] * count, [None], [None] * 9
    token = None

    def forward(c):
        nonlocal token, act_low
        out, act_low = call(False, c, meta=after(meta, token), sources=[chains], held=act_low)
        acts[c], token = along(out, routes.up), out

    for c in range(count):
        forward(c)
    for slot in range(count + lead):
        sources = [chains]
        if slot < count:
            sources += [acts[slot], top_grad]
        if slot >= lead:
            sources.append(grads[slot - lead])
        out, held = call(True, slot, meta=after(meta, token), sources=sources, held=held)
        token = out
        if slot < count:
            grads[slot] = along(out, routes.down)
    act_high, grad_all, sums, fsums, s_x, s_ctx, s_hid, s_dffn, s_right = held
    act_all = jnp.where(half == 0, act_low[0], act_high)

    lefts = {2: [s_dffn], 1: [s_hid], 0: [s_x, s_ctx]}

    def gradient(unit, at, *others):
        return grad_call(unit, at, after(grad_meta, *others), lefts[unit], s_right)

    act_move = (
        jnp.where(section == 1, jnp.concatenate(acts, 0), act_all),
        by([pair for j in range(near) for pair in (((1, near + j), (0, near + j)), ((0, near + j), (1, j)))]),
    )
    grad_move = (
        jnp.where(section == 0, jnp.concatenate(grads, 0), grad_all.astype(BF16)),
        by([pair for j in range(near) for pair in (((0, j), (1, j)), ((1, j), (0, near + j)))]),
    )

    chosen = (sides[None, :] == jnp.arange(2, dtype=jnp.int32)[:, None]).astype(F32)
    row_sums = jnp.sum(chosen[:, :, None, None] * sums[None], axis=1)
    fbias_sums = jnp.sum(chosen[:, :, None] * fsums[None, :, 0], axis=1)
    small_grads = jnp.concatenate([jnp.swapaxes(row_sums, 1, 2), fbias_sums.reshape(2, D, 4)], -1)

    if fast:
        laid = jnp.concatenate([small_grads, jnp.zeros((2, D, EXTRA - 12), F32)], -1).astype(BF16)
        laid = jnp.swapaxes(laid.reshape(2, BLOCKS, ROWS, EXTRA), 0, 1)
        small_places = table(grad_masks(ROTATIONS[0]))
        pick = (small_places[:, None] == jnp.arange(BLOCKS, dtype=jnp.int32)[None, :]).astype(BF16)
        laid = dot_nn(pick, laid.reshape(BLOCKS, -1)).astype(BF16).reshape(2, 8, 2, ROWS, EXTRA)
        laid = jnp.transpose(laid, (2, 1, 0, 3, 4)).reshape(2, 8, 2 * ROWS, EXTRA)
        wave = Waves()

        def reduce_step(keep, got, step):
            width = 4 >> step
            send = [both(a[width:], b[width:]) for a, b in zip(keep, got)]
            return [both(a[:width], b[:width]) for a, b in zip(keep, got)], send

        def bits_out(send, step):
            return [(send[i], by_bit(ROTATIONS[i % 3][step])) for i in range(len(send))]

        units = (2, 1, 0)
        totals = {(unit, 1): gradient(unit, 1) for unit in units}
        keep = [totals[unit, 1][0] for unit in units]
        got = [swap_section(totals[unit, 1][1]) for unit in units]
        act_other, grad_other = act_move[1](act_move[0]), grad_move[1](grad_move[0])
        wave.before = (act_other, grad_other)
        near_got = []
        small_keep, small_extra = [laid[0]], (laid[1], swap_section)
        for step in range(3):
            if step == 0:
                totals[2, 0] = gradient(2, 0, totals[0, 1][0])
            keep, send = reduce_step(keep, got, step)
            if step == 0:
                totals[1, 0] = gradient(1, 0, *send)
                totals[0, 0] = gradient(0, 0, totals[1, 0][0])
            small_got, *got, other = wave(
                small_extra, *bits_out(send, step), (totals[units[step], 0][1], swap_section)
            )
            near_got.append(other)
            small_keep, (small_send,) = reduce_step(small_keep, [small_got], step)
            small_extra = (small_send, by_bit(ROTATIONS[0][step]))
        far_sum = jnp.concatenate([(a[0].astype(F32) + b[0].astype(F32)).astype(BF16) for a, b in zip(keep, got)], -1)

        keep = [totals[unit, 0][0] for unit in units]
        keep, send = reduce_step(keep, near_got, 0)
        small_got, *got, straight = wave(small_extra, *bits_out(send, 0), (far_sum, by(routes.straight_back)))
        small_end = (small_keep[0][0].astype(F32) + small_got[0].astype(F32)).astype(BF16)
        keep, send = reduce_step(keep, got, 1)
        small_straight, *got, cross_a = wave(
            (small_end[ROWS:], by(routes.straight_back)),
            *bits_out(send, 1),
            (far_sum[:, : 2 * WIDE], by(routes.crossed)),
        )
        keep, send = reduce_step(keep, got, 2)
        *got, cross_b = wave(
            *bits_out(send, 2),
            (jnp.concatenate([far_sum[:, 2 * WIDE :], small_end[ROWS:]], -1), by(routes.crossed)),
        )
        near_sum = [a[0].astype(F32) + b[0].astype(F32) for a, b in zip(keep, got)] + [small_end[:ROWS].astype(F32)]
        (beside,) = wave((jnp.concatenate(near_sum, -1).astype(BF16), by(routes.away_to_home)))
        crossed = jnp.concatenate([cross_a, cross_b], -1)
        straight = jnp.concatenate([straight, small_straight], -1)

        def settle(i, width):
            cols = slice(i * WIDE, i * WIDE + width)
            mine = jnp.where(at_home, near_sum[i], straight[:, cols].astype(F32))
            twin = jnp.where(at_home, beside[:, cols].astype(F32), crossed[:, cols].astype(F32))
            return jnp.stack([jnp.where(section == 0, mine, twin), jnp.where(section == 0, twin, mine)])

        unit_out = [None] * 3
        for i, unit in enumerate(units):
            unit_out[unit] = settle(i, WIDE)
        small_out = settle(3, EXTRA)
    else:

        def summed(array):
            layers = jnp.stack([jnp.where(half == layer, array, jnp.zeros_like(array)) for layer in range(2)])
            layers = jnp.swapaxes(layers, 1, 2).reshape(2 * n_dp, rows, 2, array.shape[-1])
            out = lax.psum_scatter(layers, ("section", "dp"), scatter_dimension=0, tiled=True)
            return jnp.swapaxes(out[0], 0, 1)

        unit_out = []
        totals = {(unit, at): gradient(unit, at) for unit in range(3) for at in range(2)}
        for unit in range(3):
            group = [
                jnp.concatenate([totals[unit, 0][side], totals[unit, 1][side]], 0).reshape(D, WIDE) for side in range(2)
            ]
            unit_out.append(summed(jnp.stack(group).astype(F32)))
        small_out = summed(small_grads)
        act_other, grad_other = act_move[1](act_move[0]), grad_move[1](grad_move[0])

    act_out = jnp.where(at_home, act_all, act_other)
    grad_out = jnp.where(at_home, grad_all, grad_other.astype(F32))

    turned = jnp.swapaxes(small_out[:, :, :8], 1, 2)
    return (
        act_out[None],
        grad_out[None],
        unit_out[0][None, :, :, : 3 * D],
        unit_out[0][None, :, :, 3 * D :],
        unit_out[1][None],
        jnp.swapaxes(unit_out[2], 1, 2)[None],
        turned[None, :, 0:4],
        small_out[:, :, 8:12].reshape(1, 2, 4 * rows),
        turned[None, :, 4:6],
        turned[None, :, 6:8],
    )


def solution(mesh):
    in_specs = (
        P("dp", None, None),
        P("dp", None, None),
        P("dp"),
        P("dp"),
        P("section", None, "dp", None),
        P("section", None, "dp", None),
        P("section", None, "dp", None),
        P("section", None, None, "dp"),
        P("section", None, None, "dp"),
        P("section", None, "dp"),
        P("section", None, None, "dp"),
        P("section", None, None, "dp"),
    )
    out_specs = (
        P("section", "dp", None, None),
        P("section", "dp", None, None),
        P("section", None, "dp", None),
        P("section", None, "dp", None),
        P("section", None, "dp", None),
        P("section", None, None, "dp"),
        P("section", None, None, "dp"),
        P("section", None, "dp"),
        P("section", None, None, "dp"),
        P("section", None, None, "dp"),
    )
    return jax.shard_map(
        per_device, mesh=mesh, in_specs=in_specs, out_specs=out_specs, check_vma=False
    )
```

```python
import functools

import jax
import jax.numpy as jnp
from jax import lax
from jax.experimental import pallas as pl
from jax.experimental.pallas import tpu as pltpu
from jax.sharding import PartitionSpec as P

D = 768
HEADS = 12
HEAD_DIM = 64
FF = 3072
SEQ = 160
PAIRS = HEADS // 2
BLOCKS = 16
ROWS = D // BLOCKS
WIDE = 3072
EXTRA = 128
CHUNK = 768

EPS = 1e-05
NEG = -1e30
SQRT_HALF = 0.7071067811865476
INV_ROOT = 0.3989422804014327
SCALE = HEAD_DIM**-0.5

ROTATIONS = ((0, 1, 2), (1, 2, 0), (2, 0, 1))
F32 = jnp.float32
BF16 = jnp.bfloat16


def piece_masks(unit):
    one, two, three = (1 << bit for bit in ROTATIONS[unit])
    return [far | mask for far in (0, three) for mask in (0, one, two, two | one)]


def grad_masks(rotation):
    one, two, three = (1 << bit for bit in rotation)
    return [(one if p & 4 else 0) | (two if p & 2 else 0) | (three if p & 1 else 0) for p in range(8)]


def grad_place(mask, rotation):
    one, two, three = rotation
    return ((mask >> one) & 1) * 4 + ((mask >> two) & 1) * 2 + ((mask >> three) & 1)


def dot_nn(a, b):
    return jnp.dot(a, b, preferred_element_type=F32)


def dot_nt(a, b):
    return lax.dot_general(a, b, (((1,), (1,)), ((), ())), preferred_element_type=F32)


def dot_tn(a, b):
    return lax.dot_general(a, b, (((0,), (0,)), ((), ())), preferred_element_type=F32)


def row_mean(a):
    return jnp.sum(a, axis=-1, keepdims=True) * (1.0 / D)


def norm(summed):
    center = summed - row_mean(summed)
    inverse = lax.rsqrt(row_mean(center * center) + EPS)
    return center * inverse, inverse


def norm_back(grad, normed, inverse, gain):
    scaled = grad * gain
    return inverse * (scaled - row_mean(scaled) - normed * row_mean(scaled * normed))


def col_sum(a):
    return jnp.sum(a.astype(F32), axis=0, keepdims=True)


def lanes(start, width):
    return pl.ds(pl.multiple_of(start, 128), width)


def layer_kernel(back, slot, lead, count, *refs):
    refs = list(refs)
    take = lambda n: [refs.pop(0) for _ in range(n)]
    has_high, has_low = back and slot < count, not back or slot >= lead
    (meta,) = take(1)
    rows_ref, fbias_ref = take(2)
    own_pieces, twin_joined, twin_last = take(12), take(3), take(3)
    (chains_hbm,) = take(1)
    act_hbm, top_hbm = take(2) if has_high else (None, None)
    (grad_hbm,) = take(1) if back and has_low else (None,)
    n_out = 8 if back else 1
    n_scratch = 24 if back else 12
    take(len(refs) - n_out - n_scratch)
    outs = take(n_out)
    scr = take(n_scratch)
    win, wout, wfi, wfo, x_s, qkv, ctx, act, hl, y_s, acc, sems = scr[:12]
    if back:
        (gx16_o, y_o, gx_o, sum_o, fsum_o, sl_o, sr_o, give_o) = outs
        gy_s, probs, slope, n1_s, n2_s, dr0, dpre, dfn, gx_s, sum_s, fsum_s, low_s = scr[12:]
    else:
        (y1_o,) = outs
    high = meta[0] == 1
    low = meta[0] == 0
    active = (high | low) if has_high and has_low else (high if has_high else low)

    @pl.when(active)
    def _():
        shift = lead if back else 0
        index = jnp.where(high, slot, slot - shift)
        length = meta[1 + count + index]

        def fetch(src, dst, sem):
            pltpu.make_async_copy(src, dst, sem).start()

        if has_high:

            @pl.when(high)
            def _():
                fetch(act_hbm.at[0], x_s, sems.at[4, 0])
                fetch(top_hbm.at[slot], gy_s, sems.at[4, 1])

        if has_low:

            @pl.when(low)
            def _():
                fetch(chains_hbm.at[slot - shift], x_s, sems.at[4, 0])
                if back:
                    fetch(grad_hbm.at[0], gy_s, sems.at[4, 1])

        def load_from(side):
            def one(unit, col, width, dst, group):
                for q in range(4):
                    if side == 0:
                        src, first = own_pieces[unit * 4 + q], col
                    elif q < 3:
                        src, first = twin_joined[q], unit * WIDE + col
                    else:
                        src, first = twin_last[unit], col

                    def body(e, carry):
                        k = q * 4 + e
                        row = pl.multiple_of(meta[1 + 3 * count + unit * BLOCKS + k] * ROWS, 16)
                        fetch(src.at[e, :, first : first + width], dst.at[pl.ds(row, ROWS)], sems.at[group, k])
                        return carry

                    lax.fori_loop(0, 4, body, 0)

            one(0, 0, 3 * D, win, 0)
            one(0, 3 * D, D, wout, 1)
            one(1, 0, FF, wfi, 2)
            one(2, 0, FF, wfo, 3)

        side = meta[1 + 2 * count + index]
        pl.when(side == 0)(lambda: load_from(0))
        pl.when(side != 0)(lambda: load_from(1))

        def landed(dst, group):
            def body(k, carry):
                part = dst.at[pl.ds(0, ROWS)]
                pltpu.make_async_copy(part, part, sems.at[group, k]).wait()
                return carry

            lax.fori_loop(0, BLOCKS, body, 0)

        def small(row):
            return rows_ref[side, row : row + 1, :]

        pltpu.make_async_copy(x_s, x_s, sems.at[4, 0]).wait()
        landed(win, 0)
        x = x_s[...]
        zero_row = jnp.zeros((1, D), F32)
        for n, bias in enumerate((small(0), zero_row, small(1))):
            cols = slice(n * D, (n + 1) * D)
            qkv[:, cols] = (dot_nn(x, win[:, cols]) + bias).astype(BF16)

        low_half = lax.broadcasted_iota(jnp.int32, (1, 2 * HEAD_DIM), 1) < HEAD_DIM
        head_mask = (low_half.astype(F32).astype(BF16), (1 - low_half.astype(F32)).astype(BF16))
        live = lax.broadcasted_iota(jnp.int32, (SEQ, SEQ), 1) < length

        def heads_fwd(pair, carry):
            off = pair * 2 * HEAD_DIM
            q2 = qkv[:, lanes(off, 128)]
            k2 = qkv[:, lanes(D + off, 128)]
            v2 = qkv[:, lanes(2 * D + off, 128)]
            joined = None
            for side in range(2):
                raw = dot_nt(q2 * head_mask[side], k2)
                scores = jnp.where(live, raw * SCALE, NEG)
                expo = jnp.exp(scores - jnp.max(scores, axis=-1, keepdims=True))
                prob = expo * (1.0 / jnp.sum(expo, axis=-1, keepdims=True))
                if back:
                    probs[2 * pair + side] = prob
                part = dot_nn(prob.astype(BF16), v2 * head_mask[side])
                joined = part if joined is None else joined + part
            ctx[:, lanes(off, 128)] = joined.astype(BF16)
            return carry

        lax.fori_loop(0, PAIRS, heads_fwd, 0, unroll=True)

        landed(wout, 1)
        branch = dot_nn(ctx[...], wout[...]) + small(2)
        n1, i1 = norm(x.astype(F32) + branch)
        hidden = n1 * small(4) + small(6)
        if back:
            n1_s[...] = n1
        hl[...] = hidden.astype(BF16)
        acc[...] = hidden
        landed(wfi, 2)
        landed(wfo, 3)

        def ffn_fwd(n, carry):
            cols = lanes(n * CHUNK, CHUNK)
            pre = dot_nn(hl[...], wfi[:, cols]) + fbias_ref[side, :, cols]
            phi = 0.5 * (1.0 + lax.erf(pre * SQRT_HALF))
            act[:, cols] = (pre * phi).astype(BF16)
            if back:
                slope[:, cols] = phi + pre * jnp.exp(-0.5 * pre * pre) * INV_ROOT
            return carry

        lax.fori_loop(0, FF // CHUNK, ffn_fwd, 0, unroll=True)
        branch = dot_nt(act[...], wfo[...]) + small(3)
        n2, i2 = norm(acc[...] + branch)
        y_s[...] = (n2 * small(5) + small(7)).astype(BF16)
        copies = []

        def put(src, dst, sem):
            copy = pltpu.make_async_copy(src, dst, sem)
            copy.start()
            copies.append(copy)

        if not back:
            put(y_s, y1_o.at[0], sems.at[5, 1])
        else:
            put(y_s, y_o.at[index], sems.at[5, 0])
            put(x_s, sl_o.at[2, index], sems.at[5, 2])
            put(ctx, sl_o.at[3, index], sems.at[5, 3])
            put(hl, sl_o.at[1, index], sems.at[5, 4])
            put(act, sr_o.at[2, index], sems.at[5, 5])
            pltpu.make_async_copy(gy_s, gy_s, sems.at[4, 1]).wait()
            alive = lax.broadcasted_iota(jnp.int32, (SEQ, D), 0) < jnp.where(high, length, SEQ)
            gy = jnp.where(alive, gy_s[...].astype(F32), 0.0)
            sum_s[5:6, :] = col_sum(gy * n2)
            sum_s[7:8, :] = col_sum(gy)
            gr2 = norm_back(gy, n2, i2, small(5))
            dfn[...] = gr2.astype(BF16)
            sum_s[3:4, :] = col_sum(dfn[...])
            put(dfn, sl_o.at[0, index], sems.at[5, 6])
            n2_s[...] = gr2

            def ffn_back(n, carry):
                cols = lanes(n * CHUNK, CHUNK)
                d_act = dot_nn(dfn[...], wfo[:, cols])
                d_pre = (d_act * slope[:, cols]).astype(BF16)
                dpre[:, cols] = d_pre
                fsum_s[:, cols] = col_sum(d_pre)
                return carry

            lax.fori_loop(0, FF // CHUNK, ffn_back, 0, unroll=True)
            put(dpre, sr_o.at[1, index], sems.at[5, 7])
            gh = n2_s[...] + dot_nt(dpre[...], wfi[...]).astype(BF16).astype(F32)
            n1 = n1_s[...]
            sum_s[4:5, :] = col_sum(gh * n1)
            sum_s[6:7, :] = col_sum(gh)
            gr1 = norm_back(gh, n1, i1, small(4))
            acc[...] = gr1
            d_attn = gr1.astype(BF16)
            dr0[:, 3 * D :] = d_attn
            sum_s[2:3, :] = col_sum(d_attn)
            gx_s[...] = dot_nt(d_attn, wout[...]).astype(BF16)

            def heads_back(pair, carry):
                off = pair * 2 * HEAD_DIM
                q2 = qkv[:, lanes(off, 128)]
                k2 = qkv[:, lanes(D + off, 128)]
                v2 = qkv[:, lanes(2 * D + off, 128)]
                dc2 = gx_s[:, lanes(off, 128)]
                dq = dk = dv = None
                for side in range(2):
                    prob = probs[2 * pair + side]
                    dch = dc2 * head_mask[side]
                    d_prob = dot_nt(dch, v2)
                    inner = jnp.sum(prob * d_prob, axis=-1, keepdims=True)
                    d_raw = (prob * (d_prob - inner) * SCALE).astype(BF16)
                    a = dot_nn(d_raw, k2 * head_mask[side])
                    b = dot_tn(d_raw, q2 * head_mask[side])
                    c = dot_tn(prob.astype(BF16), dch)
                    dq, dk, dv = (a, b, c) if dq is None else (dq + a, dk + b, dv + c)
                dr0[:, lanes(off, 128)] = dq.astype(BF16)
                dr0[:, lanes(D + off, 128)] = dk.astype(BF16)
                dr0[:, lanes(2 * D + off, 128)] = dv.astype(BF16)
                return carry

            lax.fori_loop(0, PAIRS, heads_back, 0, unroll=True)
            put(dr0, sr_o.at[0, index], sems.at[5, 8])
            sum_s[0:1, :] = col_sum(dr0[:, :D])
            sum_s[1:2, :] = col_sum(dr0[:, 2 * D : 3 * D])
            grad_a = dot_nt(dr0[:, : 3 * D], win[...]) + acc[...]
            n1_s[...] = grad_a
            low_s[...] = grad_a.astype(BF16)
            put(sum_s, sum_o.at[index], sems.at[5, 11])
            put(fsum_s, fsum_o.at[index], sems.at[5, 12])
            put(n1_s, gx_o.at[index], sems.at[5, 9])
            put(low_s, gx16_o.at[0], sems.at[5, 10])
            section = meta[1 + 3 * count + 3 * BLOCKS]
            for here, core, source in ((high, 1, x_s), (high, 0, y_s), (low, 0, gy_s), (low, 1, low_s)):
                pl.when(here & (section == core))(functools.partial(fetch, source, give_o.at[index], sems.at[5, 13]))
            pltpu.make_async_copy(low_s, low_s, sems.at[5, 13]).wait()
        for copy in copies:
            copy.wait()


def grad_kernel(unit, at, meta, *refs):
    n_left = 2 if unit == 0 else 1
    left, (right,), outs, (turned,) = refs[:n_left], refs[n_left : n_left + 1], refs[n_left + 1 : n_left + 3], refs[-1:]
    count = right.shape[0]
    n = pl.program_id(0)
    chain_of = [[meta[c] for c in range(count)], [meta[count - 1 - c] for c in range(count)]]

    @pl.when(n == 0)
    def _():
        for i in range(n_left):
            for side in range(2):
                turned[i, side] = jnp.concatenate([left[i][c] for c in chain_of[side]], 0).T

    pick = jnp.where(n == 3, 1, 0) if unit == 0 else 0

    def put(side, total):
        for block in range(8):
            place = meta[count + 1 + (2 - unit) * 8 + block]
            outs[side][place] = total[block * ROWS : (block + 1) * ROWS]

    def with_first(first):
        @pl.when(meta[count] == first)
        def _():
            for side, many in ((0, first), (1, count - first)):
                if many:
                    rows = jnp.concatenate([right[c] for c in chain_of[side][:many]], 0)
                    put(side, dot_nn(turned[pick, side, :, : many * SEQ], rows).astype(BF16))
                else:
                    put(side, jnp.zeros((D // 2, CHUNK), BF16))

    for first in range(count + 1):
        with_first(first)


ANY = pl.BlockSpec(memory_space=pl.ANY)
SMEM = pl.BlockSpec(memory_space=pltpu.SMEM)
VMEM = pl.BlockSpec(memory_space=pltpu.VMEM)


def shaped(shape, dtype):
    return jax.ShapeDtypeStruct(shape, dtype)


def saved_shapes(count):
    narrow = shaped((count, SEQ, D), BF16)
    return [
        narrow,
        shaped((count, SEQ, D), F32),
        shaped((count, 8, D), F32),
        shaped((count, 1, FF), F32),
        shaped((4, count, SEQ, D), BF16),
        shaped((3, count, SEQ, WIDE), BF16),
        narrow,
    ]


def layer_call(back, slot, lead, count, meta, rows, fbias, pieces, sources, held):
    scratch = [
        pltpu.VMEM((D, 3 * D), BF16),
        pltpu.VMEM((D, D), BF16),
        pltpu.VMEM((D, FF), BF16),
        pltpu.VMEM((D, FF), BF16),
        pltpu.VMEM((SEQ, D), BF16),
        pltpu.VMEM((SEQ, 3 * D), BF16),
        pltpu.VMEM((SEQ, D), BF16),
        pltpu.VMEM((SEQ, FF), BF16),
        pltpu.VMEM((SEQ, D), BF16),
        pltpu.VMEM((SEQ, D), BF16),
        pltpu.VMEM((SEQ, D), F32),
        pltpu.SemaphoreType.DMA((6, BLOCKS)),
    ]
    if back:
        scratch += [
            pltpu.VMEM((SEQ, D), BF16),
            pltpu.VMEM((HEADS, SEQ, SEQ), F32),
            pltpu.VMEM((SEQ, FF), F32),
            pltpu.VMEM((SEQ, D), F32),
            pltpu.VMEM((SEQ, D), F32),
            pltpu.VMEM((SEQ, WIDE), BF16),
            pltpu.VMEM((SEQ, FF), BF16),
            pltpu.VMEM((SEQ, D), BF16),
            pltpu.VMEM((SEQ, D), BF16),
            pltpu.VMEM((8, D), F32),
            pltpu.VMEM((1, FF), F32),
            pltpu.VMEM((SEQ, D), BF16),
        ]
    operands = [meta, rows, fbias, *pieces, *sources]
    specs = [SMEM, VMEM, VMEM] + [ANY] * (len(pieces) + len(sources))
    first = [shaped((1, SEQ, D), BF16)]
    kept = saved_shapes(count) if back else []
    aliases = {}
    for at, array in enumerate(held):
        if array is not None:
            aliases[len(operands)] = at + 1
            operands.append(array)
            specs.append(ANY)
    outs = pl.pallas_call(
        functools.partial(layer_kernel, back, slot, lead, count),
        out_shape=first + kept,
        in_specs=specs,
        out_specs=[ANY] * (1 + len(kept)),
        scratch_shapes=scratch,
        input_output_aliases=aliases,
        compiler_params=pltpu.CompilerParams(vmem_limit_bytes=50 * 1024 * 1024),
        cost_estimate=pl.CostEstimate(flops=1, bytes_accessed=1, transcendentals=0),
        name="layer_back" if back else "layer_fwd",
    )(*operands)
    return outs[0], list(outs[1:])


def grad_call(unit, at, meta, left, right):
    count = left.shape[1]
    which = {2: [0], 1: [1], 0: [2, 3]}[unit]

    def left_of(which):
        return pl.BlockSpec((None, count, SEQ, D // 2), lambda n, m: (which, 0, 0, m[count + 1 + 24 + at]))

    return pl.pallas_call(
        functools.partial(grad_kernel, unit, at),
        out_shape=[shaped((8, ROWS, WIDE), BF16)] * 2,
        grid_spec=pltpu.PrefetchScalarGridSpec(
            num_scalar_prefetch=1,
            grid=(WIDE // CHUNK,),
            in_specs=[left_of(i) for i in which]
            + [pl.BlockSpec((None, count, SEQ, CHUNK), lambda n, m: (unit, 0, 0, n))],
            out_specs=[pl.BlockSpec((8, ROWS, CHUNK), lambda n, m: (0, 0, n))] * 2,
            scratch_shapes=[pltpu.VMEM((len(which), 2, D // 2, count * SEQ), BF16)],
        ),
        compiler_params=pltpu.CompilerParams(vmem_limit_bytes=50 * 1024 * 1024),
        cost_estimate=pl.CostEstimate(flops=1, bytes_accessed=1, transcendentals=0),
        name="layer_grad",
    )(meta, *[left] * len(which), right)


def swap_bit(array, bit):
    count = lax.axis_size("dp")
    return lax.ppermute(array, "dp", [(i, i ^ (1 << bit)) for i in range(count)])


def swap_section(array):
    return lax.ppermute(array, "section", [(0, 1), (1, 0)])


def along(array, pairs):
    count = lax.axis_size("dp")
    flat = [(s * count + i, t * count + k) for (s, i), (t, k) in pairs]
    return lax.ppermute(array, ("section", "dp"), flat)


def both(first, second):
    return (first.astype(F32) + second.astype(F32)).astype(BF16)


def after(array, *others):
    others = [other for other in others if other is not None]
    return lax.optimization_barrier((array, *others))[0] if others else array


class Waves:
    def __init__(self):
        self.before = ()

    def __call__(self, *sends):
        arrays = lax.optimization_barrier(tuple(array for array, _ in sends) + self.before)[: len(sends)]
        self.before = tuple(move(array) for array, (_, move) in zip(arrays, sends))
        return list(self.before)


def by_bit(bit):
    return lambda array: swap_bit(array, bit)


def by(pairs):
    return lambda array: along(array, pairs)


class Routes:
    def __init__(self, near):
        self.home_to_away = [((h, h * near + j), (1 - h, h * near + j)) for h in range(2) for j in range(near)]
        self.away_to_home = [(b, a) for a, b in self.home_to_away]
        self.straight = [((s, (1 - s) * near + j), (s, s * near + j)) for s in range(2) for j in range(near)]
        self.straight_back = [(b, a) for a, b in self.straight]
        self.crossed = [((s, (1 - s) * near + j), (1 - s, s * near + j)) for s in range(2) for j in range(near)]
        self.up = [((s, j), (s, near + j)) for s in range(2) for j in range(near)]
        self.down = [(b, a) for a, b in self.up]


def per_device(
    inputs,
    cotangent,
    chain_tags,
    chain_lengths,
    attn_in,
    attn_out,
    ffn_in,
    ffn_out,
    proj_bias,
    ffn_bias,
    norm_gain,
    norm_shift,
):
    n_dp = lax.axis_size("dp")
    near = n_dp // 2
    rows = attn_in.shape[2]
    count = inputs.shape[0]
    fast = near == 8 and rows == ROWS
    routes = Routes(near)
    section = lax.axis_index("section")
    place = lax.axis_index("dp")
    half = place // near
    spot = place % near
    at_home = section == half

    native = jnp.concatenate(
        [
            attn_in[0].astype(BF16),
            attn_out[0].astype(BF16),
            ffn_in[0].astype(BF16),
            jnp.swapaxes(ffn_out[0].astype(BF16), 1, 2),
        ],
        -1,
    )
    smalls = jnp.concatenate([proj_bias[0], norm_gain[0], norm_shift[0]], 1).astype(BF16)
    wides = ffn_bias[0].astype(BF16)
    numbers = jnp.concatenate([chain_tags, chain_lengths])
    crossing = routes.straight_back
    if fast:
        mine = jnp.where(section == 0, native[0], native[1])
        twin = jnp.where(section == 0, native[1], native[0])
        wave = Waves()
        cuts = (0, WIDE, 2 * WIDE, 3 * WIDE)

        def bits(held, step):
            return [(held[unit], by_bit(ROTATIONS[unit][step])) for unit in range(3)]

        def joined(held, got):
            return [jnp.concatenate([a, b], 0) for a, b in zip(held, got)]

        def own(blocks):
            return [blocks[None, :, cuts[unit] : cuts[unit + 1]] for unit in range(3)]

        def merged(held):
            return jnp.concatenate(held, -1)

        def one_bit(array, bit):
            return (array, by_bit(bit))

        small = jnp.pad(smalls, ((0, 0), (0, 0), (0, EXTRA - rows)))
        wide = jnp.pad(wides, ((0, 0), (0, 2 * EXTRA - 4 * rows))).reshape(2, 2, EXTRA)
        small = jnp.pad(jnp.concatenate([small, wide], 1), ((0, 0), (0, 6), (0, 0)))
        small = small.at[:, 10, : 2 * count].set(numbers.astype(BF16)[None])
        small_mine = jnp.where(section == 0, small[0], small[1])
        small_twin = jnp.where(section == 0, small[1], small[0])
        home, small_home = wave((twin, by(routes.home_to_away)), (small_twin, by(routes.home_to_away)))
        near_held = own(jnp.where(at_home, mine, home))
        *got, small_straight, cross_a = wave(
            *bits(near_held, 0), (small_mine, by(routes.straight)), (twin[:, : cuts[1]], by(routes.crossed))
        )
        near_held = joined(near_held, got)
        *got, small_crossed, cross_b = wave(
            *bits(near_held, 1), (small_twin, by(routes.crossed)), (twin[:, cuts[1] :], by(routes.crossed))
        )
        small_held = jnp.stack(
            [jnp.where(at_home, small_mine, small_home), jnp.where(at_home, small_straight, small_crossed)]
        )[None]
        near_held = joined(near_held, got)
        *near_far, small_got, straight = wave(
            *bits(near_held, 2), one_bit(small_held, 0), (mine, by(routes.straight))
        )
        small_held = jnp.concatenate([small_held, small_got], 0)
        away_held = own(jnp.where(at_home, straight, jnp.concatenate([cross_a, cross_b], -1)))
        *got, small_got, twin_near_held = wave(
            *bits(away_held, 0), one_bit(small_held, 1), (merged(near_held), swap_section)
        )
        small_held = jnp.concatenate([small_held, small_got], 0)
        away_held = joined(away_held, got)
        *got, small_got, twin_near_far = wave(
            *bits(away_held, 1), one_bit(small_held, 2), (merged(near_far), swap_section)
        )
        small_held = jnp.concatenate([small_held, small_got], 0)
        away_held = joined(away_held, got)
        *away_far, moved, twin_away_held = wave(
            *bits(away_held, 2),
            (jnp.where(half == 1, inputs, cotangent), by(crossing)),
            (merged(away_held), swap_section),
        )
        *twin_last, small_other = wave(*[(array, swap_section) for array in away_far], (small_held, swap_section))
        numbers_got = small_crossed[10, : 2 * count].astype(F32).astype(jnp.int32)
        pieces = [array for group in zip(near_held, near_far, away_held, away_far) for array in group]
        pieces += [twin_near_held, twin_near_far, twin_away_held, *twin_last]

        def table(masks):
            near_ones = spot ^ jnp.asarray(masks, jnp.int32)
            return jnp.concatenate([near_ones + near * half, near_ones + near * (1 - half)])

        tables = [table(piece_masks(unit)) for unit in range(3)]
        places = [grad_place(spot ^ jnp.arange(8, dtype=jnp.int32), ROTATIONS[2 - unit]) for unit in range(3)]
        row_halves = [half, 1 - half]
        first_side = section
        small_order = (spot ^ jnp.arange(8, dtype=jnp.int32))
        small_order = jnp.stack([small_order + near * half, small_order + near * (1 - half)], 1).reshape(BLOCKS)
        pick = (small_order[None, :] == jnp.arange(BLOCKS, dtype=jnp.int32)[:, None]).astype(BF16)
        row_list, fbias_list = [], []
        for array in (small_held, small_other):
            laid = dot_nn(pick, array.reshape(BLOCKS, 16 * EXTRA)).reshape(BLOCKS, 16, EXTRA)
            row_list.append(jnp.swapaxes(laid[:, :8, :rows], 0, 1).reshape(8, D))
            fbias_list.append(laid[:, 8:10].reshape(BLOCKS, 2 * EXTRA)[:, : 4 * rows].reshape(1, FF))
        rows_all = jnp.stack(row_list)
        fbias_all = jnp.stack(fbias_list)
    else:
        tables = [jnp.arange(BLOCKS, dtype=jnp.int32)] * 3
        places = [jnp.arange(8, dtype=jnp.int32)] * 3
        row_halves = [jnp.int32(0), jnp.int32(1)]
        first_side = 0
        moved = along(jnp.where(half == 1, inputs, cotangent), crossing)
        numbers_got = along(numbers, crossing)

        def whole(array, dim):
            full = lax.all_gather(array, ("section", "dp"), axis=0).reshape((2, n_dp) + array.shape)
            full = lax.dynamic_index_in_dim(full, half, 0, keepdims=False)
            shape = array.shape[:dim] + (n_dp * array.shape[dim],) + array.shape[dim + 1 :]
            return jnp.moveaxis(full, 0, dim).reshape(shape)

        full = whole(native, 1).reshape(2, 4, 4, ROWS, 3 * WIDE)
        pieces = [full[0, q, :, :, unit * WIDE : (unit + 1) * WIDE] for unit in range(3) for q in range(4)]
        pieces += [full[1, q] for q in range(3)]
        pieces += [full[1, 3, :, :, unit * WIDE : (unit + 1) * WIDE] for unit in range(3)]
        rows_all = whole(smalls, 2).astype(F32)
        fbias_all = whole(wides, 1).astype(F32)[:, None, :]

    numbers = jnp.where(at_home, numbers, numbers_got)
    chains = jnp.where(at_home, inputs, moved)
    top_grad = jnp.where(at_home, cotangent, moved)
    sides = numbers[:count] ^ first_side
    meta = [half[None].astype(jnp.int32), numbers, sides.astype(jnp.int32)] + tables
    meta = jnp.concatenate(meta + [section[None].astype(jnp.int32)])
    later = jnp.arange(count)[:, None] < jnp.arange(count)[None, :]
    rank = jnp.sum((sides[:, None] > sides[None, :]) | ((sides[:, None] == sides[None, :]) & later.T), axis=1)
    sorted_chains = jnp.sum(
        jnp.where(rank[None, :] == jnp.arange(count)[:, None], jnp.arange(count)[None, :], 0), axis=1
    )
    grad_meta = jnp.concatenate(
        [sorted_chains.astype(jnp.int32), jnp.sum(1 - sides)[None].astype(jnp.int32)]
        + [places[unit] for unit in (2, 1, 0)]
        + [value[None].astype(jnp.int32) for value in row_halves]
    )

    lead = 2
    call = functools.partial(layer_call, lead=lead, count=count, rows=rows_all, fbias=fbias_all, pieces=pieces)
    acts, grads, held = [None] * count, [None] * count, [None] * 7
    token = None

    def forward(c):
        nonlocal token
        out, _ = call(False, c, meta=after(meta, token), sources=[chains], held=[])
        acts[c], token = along(out, routes.up), out

    for c in range(count):
        forward(c)
    for slot in range(count + lead):
        sources = [chains]
        if slot < count:
            sources += [acts[slot], top_grad]
        if slot >= lead:
            sources.append(grads[slot - lead])
        out, held = call(True, slot, meta=after(meta, token), sources=sources, held=held)
        token = out
        if slot < count:
            grads[slot] = along(out, routes.down)
    act_all, grad_all, sums, fsums, s_left, s_right, give = held


    def gradient(unit, at, *others):
        return grad_call(unit, at, after(grad_meta, *others), s_left, s_right)

    act_move = by([pair for j in range(near) for pair in (((1, near + j), (0, near + j)), ((0, near + j), (1, j)))])
    grad_move = by([pair for j in range(near) for pair in (((0, j), (1, j)), ((1, j), (0, near + j)))])
    act_other, grad_other = act_move(give), grad_move(give)

    chosen = (sides[None, :] == jnp.arange(2, dtype=jnp.int32)[:, None]).astype(F32)
    row_sums = jnp.sum(chosen[:, :, None, None] * sums[None], axis=1)
    fbias_sums = jnp.sum(chosen[:, :, None] * fsums[None, :, 0], axis=1)
    small_grads = jnp.concatenate([jnp.swapaxes(row_sums, 1, 2), fbias_sums.reshape(2, D, 4)], -1)

    if fast:
        laid = jnp.concatenate([small_grads, jnp.zeros((2, D, EXTRA - 12), F32)], -1).astype(BF16)
        laid = jnp.swapaxes(laid.reshape(2, BLOCKS, ROWS, EXTRA), 0, 1)
        small_places = table(grad_masks(ROTATIONS[0]))
        pick = (small_places[:, None] == jnp.arange(BLOCKS, dtype=jnp.int32)[None, :]).astype(BF16)
        laid = dot_nn(pick, laid.reshape(BLOCKS, -1)).astype(BF16).reshape(2, 8, 2, ROWS, EXTRA)
        laid = jnp.transpose(laid, (2, 1, 0, 3, 4)).reshape(2, 8, 2 * ROWS, EXTRA)
        wave = Waves()

        def reduce_step(keep, got, step):
            width = 4 >> step
            send = [both(a[width:], b[width:]) for a, b in zip(keep, got)]
            return [both(a[:width], b[:width]) for a, b in zip(keep, got)], send

        def bits_out(send, step):
            return [(send[i], by_bit(ROTATIONS[i % 3][step])) for i in range(len(send))]

        units = (2, 1, 0)
        terms = [gradient(unit, 1) for unit in units]
        keep = [own for own, _ in terms]
        got = [swap_section(other) for _, other in terms]
        wave.before = (act_other, grad_other)
        near_terms = [gradient(2, 0, keep[2])]
        send = [both(a[4:], b[4:]) for a, b in zip(keep, got)]
        near_terms += [gradient(1, 0, *send)]
        near_terms += [gradient(0, 0, near_terms[1][0])]
        near_keep = [own for own, _ in near_terms]
        small_got, *far_got, other = wave((laid[1], swap_section), *bits_out(send, 0), (near_terms[0][1], swap_section))
        near_got = [other]
        keep = [both(after(a, *send)[:4], b[:4]) for a, b in zip(keep, got)]
        got = far_got
        small_keep = [laid[0]]
        for step in (1, 2):
            small_keep, small_send = reduce_step(small_keep, [small_got], step - 1)
            keep, send = reduce_step(keep, got, step)
            small_got, *got, other = wave(
                one_bit(small_send[0], step - 1), *bits_out(send, step), (near_terms[step][1], swap_section)
            )
            near_got.append(other)
        far_sum = jnp.concatenate([(a[0].astype(F32) + b[0].astype(F32)).astype(BF16) for a, b in zip(keep, got)], -1)

        keep, send = reduce_step(near_keep, near_got, 0)
        small_keep, small_send = reduce_step(small_keep, [small_got], 2)
        small_got, *got, straight = wave(
            one_bit(small_send[0], 2), *bits_out(send, 0), (far_sum, by(routes.straight_back))
        )
        small_end = (small_keep[0][0].astype(F32) + small_got[0].astype(F32)).astype(BF16)
        keep, send = reduce_step(keep, got, 1)
        small_straight, *got, cross_a = wave(
            (small_end[ROWS:], by(routes.straight_back)),
            *bits_out(send, 1),
            (far_sum[:, : 2 * WIDE], by(routes.crossed)),
        )
        keep, send = reduce_step(keep, got, 2)
        *got, cross_b = wave(
            *bits_out(send, 2),
            (jnp.concatenate([far_sum[:, 2 * WIDE :], small_end[ROWS:]], -1), by(routes.crossed)),
        )
        near_sum = [a[0].astype(F32) + b[0].astype(F32) for a, b in zip(keep, got)] + [small_end[:ROWS].astype(F32)]
        (beside,) = wave((jnp.concatenate(near_sum, -1).astype(BF16), by(routes.away_to_home)))
        crossed = jnp.concatenate([cross_a, cross_b], -1)
        straight = jnp.concatenate([straight, small_straight], -1)

        def settle(i, width):
            cols = slice(i * WIDE, i * WIDE + width)
            mine = jnp.where(at_home, near_sum[i], straight[:, cols].astype(F32))
            twin = jnp.where(at_home, beside[:, cols].astype(F32), crossed[:, cols].astype(F32))
            return jnp.stack([jnp.where(section == 0, mine, twin), jnp.where(section == 0, twin, mine)])

        unit_out = [None] * 3
        for i, unit in enumerate(units):
            unit_out[unit] = settle(i, WIDE)
        small_out = settle(3, EXTRA)
    else:

        def summed(array):
            layers = jnp.stack([jnp.where(half == layer, array, jnp.zeros_like(array)) for layer in range(2)])
            layers = jnp.swapaxes(layers, 1, 2).reshape(2 * n_dp, rows, 2, array.shape[-1])
            out = lax.psum_scatter(layers, ("section", "dp"), scatter_dimension=0, tiled=True)
            return jnp.swapaxes(out[0], 0, 1)

        unit_out = []
        for unit in range(3):
            terms = [gradient(unit, at) for at in range(2)]
            group = [jnp.concatenate([part[side] for part in terms], 0).reshape(D, WIDE) for side in range(2)]
            unit_out.append(summed(jnp.stack(group).astype(F32)))
        small_out = summed(small_grads)

    act_out = jnp.where(at_home, act_all, act_other)
    grad_out = jnp.where(at_home, grad_all, grad_other.astype(F32))

    turned = jnp.swapaxes(small_out[:, :, :8], 1, 2)
    return (
        act_out[None],
        grad_out[None],
        unit_out[0][None, :, :, : 3 * D],
        unit_out[0][None, :, :, 3 * D :],
        unit_out[1][None],
        jnp.swapaxes(unit_out[2], 1, 2)[None],
        turned[None, :, 0:4],
        small_out[:, :, 8:12].reshape(1, 2, 4 * rows),
        turned[None, :, 4:6],
        turned[None, :, 6:8],
    )


def solution(mesh):
    in_specs = (
        P("dp", None, None),
        P("dp", None, None),
        P("dp"),
        P("dp"),
        P("section", None, "dp", None),
        P("section", None, "dp", None),
        P("section", None, "dp", None),
        P("section", None, None, "dp"),
        P("section", None, None, "dp"),
        P("section", None, "dp"),
        P("section", None, None, "dp"),
        P("section", None, None, "dp"),
    )
    out_specs = (
        P("section", "dp", None, None),
        P("section", "dp", None, None),
        P("section", None, "dp", None),
        P("section", None, "dp", None),
        P("section", None, "dp", None),
        P("section", None, None, "dp"),
        P("section", None, None, "dp"),
        P("section", None, "dp"),
        P("section", None, None, "dp"),
        P("section", None, None, "dp"),
    )
    return jax.shard_map(
        per_device, mesh=mesh, in_specs=in_specs, out_specs=out_specs, check_vma=False
    )
```

```python
import functools

import jax
import jax.numpy as jnp
from jax import lax
from jax.experimental import pallas as pl
from jax.experimental.pallas import tpu as pltpu
from jax.sharding import PartitionSpec as P

D = 768
HEADS = 12
HEAD_DIM = 64
FF = 3072
SEQ = 160
PAIRS = HEADS // 2
BLOCKS = 16
ROWS = D // BLOCKS
WIDE = 3072
EXTRA = 128
CHUNK = 768

EPS = 1e-05
NEG = -1e30
SQRT_HALF = 0.7071067811865476
INV_ROOT = 0.3989422804014327
SCALE = HEAD_DIM**-0.5

ROTATIONS = ((0, 1, 2), (1, 2, 0), (2, 0, 1))
F32 = jnp.float32
BF16 = jnp.bfloat16


def piece_masks(unit):
    one, two, three = (1 << bit for bit in ROTATIONS[unit])
    return [far | mask for far in (0, three) for mask in (0, one, two, two | one)]


def grad_masks(rotation):
    one, two, three = (1 << bit for bit in rotation)
    return [(one if p & 4 else 0) | (two if p & 2 else 0) | (three if p & 1 else 0) for p in range(8)]


def grad_place(mask, rotation):
    one, two, three = rotation
    return ((mask >> one) & 1) * 4 + ((mask >> two) & 1) * 2 + ((mask >> three) & 1)


def dot_nn(a, b):
    return jnp.dot(a, b, preferred_element_type=F32)


def dot_nt(a, b):
    return lax.dot_general(a, b, (((1,), (1,)), ((), ())), preferred_element_type=F32)


def dot_tn(a, b):
    return lax.dot_general(a, b, (((0,), (0,)), ((), ())), preferred_element_type=F32)


def row_mean(a):
    return jnp.sum(a, axis=-1, keepdims=True) * (1.0 / D)


def norm(summed):
    center = summed - row_mean(summed)
    inverse = lax.rsqrt(row_mean(center * center) + EPS)
    return center * inverse, inverse


def norm_back(grad, normed, inverse, gain):
    scaled = grad * gain
    return inverse * (scaled - row_mean(scaled) - normed * row_mean(scaled * normed))


def col_sum(a):
    return jnp.sum(a.astype(F32), axis=0, keepdims=True)


def lanes(start, width):
    return pl.ds(pl.multiple_of(start, 128), width)


def layer_kernel(back, slot, lead, count, *refs):
    refs = list(refs)
    take = lambda n: [refs.pop(0) for _ in range(n)]
    has_high, has_low = back and slot < count, not back or slot >= lead
    (meta,) = take(1)
    rows_ref, fbias_ref = take(2)
    own_pieces, twin_joined, twin_last = take(12), take(3), take(3)
    (chains_hbm,) = take(1)
    act_hbm, top_hbm = take(2) if has_high else (None, None)
    (grad_hbm,) = take(1) if back and has_low else (None,)
    n_out = 8 if back else 1
    n_scratch = 24 if back else 12
    take(len(refs) - n_out - n_scratch)
    outs = take(n_out)
    scr = take(n_scratch)
    win, wout, wfi, wfo, x_s, qkv, ctx, act, hl, y_s, acc, sems = scr[:12]
    if back:
        (gx16_o, y_o, gx_o, sum_o, fsum_o, sl_o, sr_o, give_o) = outs
        gy_s, probs, slope, n1_s, n2_s, dr0, dpre, dfn, gx_s, sum_s, fsum_s, low_s = scr[12:]
    else:
        (y1_o,) = outs
    high = meta[0] == 1
    low = meta[0] == 0
    active = (high | low) if has_high and has_low else (high if has_high else low)

    @pl.when(active)
    def _():
        shift = lead if back else 0
        index = jnp.where(high, slot, slot - shift)
        length = meta[1 + count + index]

        def fetch(src, dst, sem):
            pltpu.make_async_copy(src, dst, sem).start()

        if has_high:

            @pl.when(high)
            def _():
                fetch(act_hbm.at[0], x_s, sems.at[4, 0])
                fetch(top_hbm.at[slot], gy_s, sems.at[4, 1])

        if has_low:

            @pl.when(low)
            def _():
                fetch(chains_hbm.at[slot - shift], x_s, sems.at[4, 0])
                if back:
                    fetch(grad_hbm.at[0], gy_s, sems.at[4, 1])

        def load_from(side):
            def one(unit, col, width, dst, group):
                for q in range(4):
                    if side == 0:
                        src, first = own_pieces[unit * 4 + q], col
                    elif q < 3:
                        src, first = twin_joined[q], unit * WIDE + col
                    else:
                        src, first = twin_last[unit], col

                    def body(e, carry):
                        k = q * 4 + e
                        row = pl.multiple_of(meta[1 + 3 * count + unit * BLOCKS + k] * ROWS, 16)
                        fetch(src.at[e, :, first : first + width], dst.at[pl.ds(row, ROWS)], sems.at[group, k])
                        return carry

                    lax.fori_loop(0, 4, body, 0)

            one(0, 0, 3 * D, win, 0)
            one(0, 3 * D, D, wout, 1)
            one(1, 0, FF, wfi, 2)
            one(2, 0, FF, wfo, 3)

        side = meta[1 + 2 * count + index]
        pl.when(side == 0)(lambda: load_from(0))
        pl.when(side != 0)(lambda: load_from(1))

        def landed(dst, group):
            def body(k, carry):
                part = dst.at[pl.ds(0, ROWS)]
                pltpu.make_async_copy(part, part, sems.at[group, k]).wait()
                return carry

            lax.fori_loop(0, BLOCKS, body, 0)

        def small(row):
            return rows_ref[side, row : row + 1, :]

        pltpu.make_async_copy(x_s, x_s, sems.at[4, 0]).wait()
        landed(win, 0)
        x = x_s[...]
        zero_row = jnp.zeros((1, D), F32)
        for n, bias in enumerate((small(0), zero_row, small(1))):
            cols = slice(n * D, (n + 1) * D)
            qkv[:, cols] = (dot_nn(x, win[:, cols]) + bias).astype(BF16)

        low_half = lax.broadcasted_iota(jnp.int32, (1, 2 * HEAD_DIM), 1) < HEAD_DIM
        head_mask = (low_half.astype(F32).astype(BF16), (1 - low_half.astype(F32)).astype(BF16))
        live = lax.broadcasted_iota(jnp.int32, (SEQ, SEQ), 1) < length

        def heads_fwd(pair, carry):
            off = pair * 2 * HEAD_DIM
            q2 = qkv[:, lanes(off, 128)]
            k2 = qkv[:, lanes(D + off, 128)]
            v2 = qkv[:, lanes(2 * D + off, 128)]
            joined = None
            for side in range(2):
                raw = dot_nt(q2 * head_mask[side], k2)
                scores = jnp.where(live, raw * SCALE, NEG)
                expo = jnp.exp(scores - jnp.max(scores, axis=-1, keepdims=True))
                prob = expo * (1.0 / jnp.sum(expo, axis=-1, keepdims=True))
                if back:
                    probs[2 * pair + side] = prob
                part = dot_nn(prob.astype(BF16), v2 * head_mask[side])
                joined = part if joined is None else joined + part
            ctx[:, lanes(off, 128)] = joined.astype(BF16)
            return carry

        lax.fori_loop(0, PAIRS, heads_fwd, 0, unroll=True)

        landed(wout, 1)
        branch = dot_nn(ctx[...], wout[...]) + small(2)
        n1, i1 = norm(x.astype(F32) + branch)
        hidden = n1 * small(4) + small(6)
        if back:
            n1_s[...] = n1
        hl[...] = hidden.astype(BF16)
        acc[...] = hidden
        landed(wfi, 2)
        landed(wfo, 3)

        def ffn_fwd(n, carry):
            cols = lanes(n * CHUNK, CHUNK)
            pre = dot_nn(hl[...], wfi[:, cols]) + fbias_ref[side, :, cols]
            phi = 0.5 * (1.0 + lax.erf(pre * SQRT_HALF))
            act[:, cols] = (pre * phi).astype(BF16)
            if back:
                slope[:, cols] = phi + pre * jnp.exp(-0.5 * pre * pre) * INV_ROOT
            return carry

        lax.fori_loop(0, FF // CHUNK, ffn_fwd, 0, unroll=True)
        branch = dot_nt(act[...], wfo[...]) + small(3)
        n2, i2 = norm(acc[...] + branch)
        y_s[...] = (n2 * small(5) + small(7)).astype(BF16)
        copies = []

        def put(src, dst, sem):
            copy = pltpu.make_async_copy(src, dst, sem)
            copy.start()
            copies.append(copy)

        if not back:
            put(y_s, y1_o.at[0], sems.at[5, 1])
        else:
            put(y_s, y_o.at[index], sems.at[5, 0])
            put(x_s, sl_o.at[2, index], sems.at[5, 2])
            put(ctx, sl_o.at[3, index], sems.at[5, 3])
            put(hl, sl_o.at[1, index], sems.at[5, 4])
            put(act, sr_o.at[2, index], sems.at[5, 5])
            pltpu.make_async_copy(gy_s, gy_s, sems.at[4, 1]).wait()
            alive = lax.broadcasted_iota(jnp.int32, (SEQ, D), 0) < jnp.where(high, length, SEQ)
            gy = jnp.where(alive, gy_s[...].astype(F32), 0.0)
            sum_s[5:6, :] = col_sum(gy * n2)
            sum_s[7:8, :] = col_sum(gy)
            gr2 = norm_back(gy, n2, i2, small(5))
            dfn[...] = gr2.astype(BF16)
            sum_s[3:4, :] = col_sum(dfn[...])
            put(dfn, sl_o.at[0, index], sems.at[5, 6])
            n2_s[...] = gr2

            def ffn_back(n, carry):
                cols = lanes(n * CHUNK, CHUNK)
                d_act = dot_nn(dfn[...], wfo[:, cols])
                d_pre = (d_act * slope[:, cols]).astype(BF16)
                dpre[:, cols] = d_pre
                fsum_s[:, cols] = col_sum(d_pre)
                return carry

            lax.fori_loop(0, FF // CHUNK, ffn_back, 0, unroll=True)
            put(dpre, sr_o.at[1, index], sems.at[5, 7])
            gh = n2_s[...] + dot_nt(dpre[...], wfi[...]).astype(BF16).astype(F32)
            n1 = n1_s[...]
            sum_s[4:5, :] = col_sum(gh * n1)
            sum_s[6:7, :] = col_sum(gh)
            gr1 = norm_back(gh, n1, i1, small(4))
            acc[...] = gr1
            d_attn = gr1.astype(BF16)
            dr0[:, 3 * D :] = d_attn
            sum_s[2:3, :] = col_sum(d_attn)
            gx_s[...] = dot_nt(d_attn, wout[...]).astype(BF16)

            def heads_back(pair, carry):
                off = pair * 2 * HEAD_DIM
                q2 = qkv[:, lanes(off, 128)]
                k2 = qkv[:, lanes(D + off, 128)]
                v2 = qkv[:, lanes(2 * D + off, 128)]
                dc2 = gx_s[:, lanes(off, 128)]
                dq = dk = dv = None
                for side in range(2):
                    prob = probs[2 * pair + side]
                    dch = dc2 * head_mask[side]
                    d_prob = dot_nt(dch, v2)
                    inner = jnp.sum(prob * d_prob, axis=-1, keepdims=True)
                    d_raw = (prob * (d_prob - inner) * SCALE).astype(BF16)
                    a = dot_nn(d_raw, k2 * head_mask[side])
                    b = dot_tn(d_raw, q2 * head_mask[side])
                    c = dot_tn(prob.astype(BF16), dch)
                    dq, dk, dv = (a, b, c) if dq is None else (dq + a, dk + b, dv + c)
                dr0[:, lanes(off, 128)] = dq.astype(BF16)
                dr0[:, lanes(D + off, 128)] = dk.astype(BF16)
                dr0[:, lanes(2 * D + off, 128)] = dv.astype(BF16)
                return carry

            lax.fori_loop(0, PAIRS, heads_back, 0, unroll=True)
            put(dr0, sr_o.at[0, index], sems.at[5, 8])
            sum_s[0:1, :] = col_sum(dr0[:, :D])
            sum_s[1:2, :] = col_sum(dr0[:, 2 * D : 3 * D])
            grad_a = dot_nt(dr0[:, : 3 * D], win[...]) + acc[...]
            n1_s[...] = grad_a
            low_s[...] = grad_a.astype(BF16)
            put(sum_s, sum_o.at[index], sems.at[5, 11])
            put(fsum_s, fsum_o.at[index], sems.at[5, 12])
            put(n1_s, gx_o.at[index], sems.at[5, 9])
            put(low_s, gx16_o.at[0], sems.at[5, 10])
            section = meta[1 + 3 * count + 3 * BLOCKS]
            for here, core, source in ((high, 1, x_s), (high, 0, y_s), (low, 0, gy_s), (low, 1, low_s)):
                pl.when(here & (section == core))(functools.partial(fetch, source, give_o.at[index], sems.at[5, 13]))
            pltpu.make_async_copy(low_s, low_s, sems.at[5, 13]).wait()
        for copy in copies:
            copy.wait()


def grad_kernel(unit, at, meta, *refs):
    n_left = 2 if unit == 0 else 1
    left, (right,), outs, (turned,) = refs[:n_left], refs[n_left : n_left + 1], refs[n_left + 1 : n_left + 3], refs[-1:]
    count = right.shape[0]
    n = pl.program_id(0)
    chain_of = [[meta[c] for c in range(count)], [meta[count - 1 - c] for c in range(count)]]

    @pl.when(n == 0)
    def _():
        for i in range(n_left):
            for side in range(2):
                turned[i, side] = jnp.concatenate([left[i][c] for c in chain_of[side]], 0).T

    pick = jnp.where(n == 3, 1, 0) if unit == 0 else 0

    def put(side, total):
        for block in range(8):
            place = meta[count + 1 + (2 - unit) * 8 + block]
            outs[side][place] = total[block * ROWS : (block + 1) * ROWS]

    def with_first(first):
        @pl.when(meta[count] == first)
        def _():
            for side, many in ((0, first), (1, count - first)):
                if many:
                    rows = jnp.concatenate([right[c] for c in chain_of[side][:many]], 0)
                    put(side, dot_nn(turned[pick, side, :, : many * SEQ], rows).astype(BF16))
                else:
                    put(side, jnp.zeros((D // 2, CHUNK), BF16))

    for first in range(count + 1):
        with_first(first)


ANY = pl.BlockSpec(memory_space=pl.ANY)
SMEM = pl.BlockSpec(memory_space=pltpu.SMEM)
VMEM = pl.BlockSpec(memory_space=pltpu.VMEM)


def shaped(shape, dtype):
    return jax.ShapeDtypeStruct(shape, dtype)


def saved_shapes(count):
    narrow = shaped((count, SEQ, D), BF16)
    return [
        narrow,
        shaped((count, SEQ, D), F32),
        shaped((count, 8, D), F32),
        shaped((count, 1, FF), F32),
        shaped((4, count, SEQ, D), BF16),
        shaped((3, count, SEQ, WIDE), BF16),
        narrow,
    ]


def layer_call(back, slot, lead, count, meta, rows, fbias, pieces, sources, held):
    scratch = [
        pltpu.VMEM((D, 3 * D), BF16),
        pltpu.VMEM((D, D), BF16),
        pltpu.VMEM((D, FF), BF16),
        pltpu.VMEM((D, FF), BF16),
        pltpu.VMEM((SEQ, D), BF16),
        pltpu.VMEM((SEQ, 3 * D), BF16),
        pltpu.VMEM((SEQ, D), BF16),
        pltpu.VMEM((SEQ, FF), BF16),
        pltpu.VMEM((SEQ, D), BF16),
        pltpu.VMEM((SEQ, D), BF16),
        pltpu.VMEM((SEQ, D), F32),
        pltpu.SemaphoreType.DMA((6, BLOCKS)),
    ]
    if back:
        scratch += [
            pltpu.VMEM((SEQ, D), BF16),
            pltpu.VMEM((HEADS, SEQ, SEQ), F32),
            pltpu.VMEM((SEQ, FF), F32),
            pltpu.VMEM((SEQ, D), F32),
            pltpu.VMEM((SEQ, D), F32),
            pltpu.VMEM((SEQ, WIDE), BF16),
            pltpu.VMEM((SEQ, FF), BF16),
            pltpu.VMEM((SEQ, D), BF16),
            pltpu.VMEM((SEQ, D), BF16),
            pltpu.VMEM((8, D), F32),
            pltpu.VMEM((1, FF), F32),
            pltpu.VMEM((SEQ, D), BF16),
        ]
    operands = [meta, rows, fbias, *pieces, *sources]
    specs = [SMEM, VMEM, VMEM] + [ANY] * (len(pieces) + len(sources))
    first = [shaped((1, SEQ, D), BF16)]
    kept = saved_shapes(count) if back else []
    aliases = {}
    for at, array in enumerate(held):
        if array is not None:
            aliases[len(operands)] = at + 1
            operands.append(array)
            specs.append(ANY)
    outs = pl.pallas_call(
        functools.partial(layer_kernel, back, slot, lead, count),
        out_shape=first + kept,
        in_specs=specs,
        out_specs=[ANY] * (1 + len(kept)),
        scratch_shapes=scratch,
        input_output_aliases=aliases,
        compiler_params=pltpu.CompilerParams(vmem_limit_bytes=50 * 1024 * 1024),
        cost_estimate=pl.CostEstimate(flops=1, bytes_accessed=1, transcendentals=0),
        name="layer_back" if back else "layer_fwd",
    )(*operands)
    return outs[0], list(outs[1:])


def grad_call(unit, at, meta, left, right):
    count = left.shape[1]
    which = {2: [0], 1: [1], 0: [2, 3]}[unit]

    def left_of(which):
        return pl.BlockSpec((None, count, SEQ, D // 2), lambda n, m: (which, 0, 0, m[count + 1 + 24 + at]))

    return pl.pallas_call(
        functools.partial(grad_kernel, unit, at),
        out_shape=[shaped((8, ROWS, WIDE), BF16)] * 2,
        grid_spec=pltpu.PrefetchScalarGridSpec(
            num_scalar_prefetch=1,
            grid=(WIDE // CHUNK,),
            in_specs=[left_of(i) for i in which]
            + [pl.BlockSpec((None, count, SEQ, CHUNK), lambda n, m: (unit, 0, 0, n))],
            out_specs=[pl.BlockSpec((8, ROWS, CHUNK), lambda n, m: (0, 0, n))] * 2,
            scratch_shapes=[pltpu.VMEM((len(which), 2, D // 2, count * SEQ), BF16)],
        ),
        compiler_params=pltpu.CompilerParams(vmem_limit_bytes=50 * 1024 * 1024),
        cost_estimate=pl.CostEstimate(flops=1, bytes_accessed=1, transcendentals=0),
        name="layer_grad",
    )(meta, *[left] * len(which), right)


def swap_bit(array, bit):
    count = lax.axis_size("dp")
    return lax.ppermute(array, "dp", [(i, i ^ (1 << bit)) for i in range(count)])


def swap_section(array):
    return lax.ppermute(array, "section", [(0, 1), (1, 0)])


def along(array, pairs):
    count = lax.axis_size("dp")
    flat = [(s * count + i, t * count + k) for (s, i), (t, k) in pairs]
    return lax.ppermute(array, ("section", "dp"), flat)


def both(first, second):
    return (first.astype(F32) + second.astype(F32)).astype(BF16)


def after(array, *others):
    others = [other for other in others if other is not None]
    return lax.optimization_barrier((array, *others))[0] if others else array


class Waves:
    def __init__(self):
        self.before = ()

    def __call__(self, *sends):
        arrays = lax.optimization_barrier(tuple(array for array, _ in sends) + self.before)[: len(sends)]
        self.before = tuple(move(array) for array, (_, move) in zip(arrays, sends))
        return list(self.before)


def by_bit(bit):
    return lambda array: swap_bit(array, bit)


def by(pairs):
    return lambda array: along(array, pairs)


class Routes:
    def __init__(self, near):
        self.home_to_away = [((h, h * near + j), (1 - h, h * near + j)) for h in range(2) for j in range(near)]
        self.away_to_home = [(b, a) for a, b in self.home_to_away]
        self.straight = [((s, (1 - s) * near + j), (s, s * near + j)) for s in range(2) for j in range(near)]
        self.straight_back = [(b, a) for a, b in self.straight]
        self.crossed = [((s, (1 - s) * near + j), (1 - s, s * near + j)) for s in range(2) for j in range(near)]
        self.up = [((s, j), (s, near + j)) for s in range(2) for j in range(near)]
        self.down = [(b, a) for a, b in self.up]


def per_device(
    inputs,
    cotangent,
    chain_tags,
    chain_lengths,
    attn_in,
    attn_out,
    ffn_in,
    ffn_out,
    proj_bias,
    ffn_bias,
    norm_gain,
    norm_shift,
):
    n_dp = lax.axis_size("dp")
    near = n_dp // 2
    rows = attn_in.shape[2]
    count = inputs.shape[0]
    fast = near == 8 and rows == ROWS
    routes = Routes(near)
    section = lax.axis_index("section")
    place = lax.axis_index("dp")
    half = place // near
    spot = place % near
    at_home = section == half

    native = jnp.concatenate(
        [
            attn_in[0].astype(BF16),
            attn_out[0].astype(BF16),
            ffn_in[0].astype(BF16),
            jnp.swapaxes(ffn_out[0].astype(BF16), 1, 2),
        ],
        -1,
    )
    smalls = jnp.concatenate([proj_bias[0], norm_gain[0], norm_shift[0]], 1).astype(BF16)
    wides = ffn_bias[0].astype(BF16)
    numbers = jnp.concatenate([chain_tags, chain_lengths])
    crossing = routes.straight_back
    if fast:
        mine = jnp.where(section == 0, native[0], native[1])
        twin = jnp.where(section == 0, native[1], native[0])
        wave = Waves()
        cuts = (0, WIDE, 2 * WIDE, 3 * WIDE)

        def bits(held, step):
            return [(held[unit], by_bit(ROTATIONS[unit][step])) for unit in range(3)]

        def joined(held, got):
            return [jnp.concatenate([a, b], 0) for a, b in zip(held, got)]

        def own(blocks):
            return [blocks[None, :, cuts[unit] : cuts[unit + 1]] for unit in range(3)]

        def merged(held):
            return jnp.concatenate(held, -1)

        def one_bit(array, bit):
            return (array, by_bit(bit))

        small = jnp.pad(smalls, ((0, 0), (0, 0), (0, EXTRA - rows)))
        wide = jnp.pad(wides, ((0, 0), (0, 2 * EXTRA - 4 * rows))).reshape(2, 2, EXTRA)
        small = jnp.pad(jnp.concatenate([small, wide], 1), ((0, 0), (0, 6), (0, 0)))
        small = small.at[:, 10, : 2 * count].set(numbers.astype(BF16)[None])
        home, small_home = wave((twin, by(routes.home_to_away)), (small, by(routes.home_to_away)))
        near_held = own(jnp.where(at_home, mine, home))
        *got, small_straight, cross_a = wave(
            *bits(near_held, 0), (small, by(routes.straight)), (twin[:, : cuts[1]], by(routes.crossed))
        )
        near_held = joined(near_held, got)
        *got, small_crossed, cross_b = wave(
            *bits(near_held, 1), (small, by(routes.crossed)), (twin[:, cuts[1] :], by(routes.crossed))
        )
        small_held = jnp.stack(
            [jnp.where(at_home, small, small_home), jnp.where(at_home, small_straight, small_crossed)]
        )[None]
        near_held = joined(near_held, got)
        *near_far, small_got, straight = wave(
            *bits(near_held, 2), one_bit(small_held, 0), (mine, by(routes.straight))
        )
        small_held = jnp.concatenate([small_held, small_got], 0)
        away_held = own(jnp.where(at_home, straight, jnp.concatenate([cross_a, cross_b], -1)))
        *got, small_got, twin_near_held = wave(
            *bits(away_held, 0), one_bit(small_held, 1), (merged(near_held), swap_section)
        )
        small_held = jnp.concatenate([small_held, small_got], 0)
        away_held = joined(away_held, got)
        *got, moved, twin_near_far = wave(
            *bits(away_held, 1),
            (jnp.where(half == 1, inputs, cotangent), by(crossing)),
            (merged(near_far), swap_section),
        )
        away_held = joined(away_held, got)
        *away_far, small_got, twin_away_held = wave(
            *bits(away_held, 2), one_bit(small_held, 2), (merged(away_held), swap_section)
        )
        small_held = jnp.concatenate([small_held, small_got], 0)
        twin_last = wave(*[(array, swap_section) for array in away_far])
        numbers_got = small_crossed[0, 10, : 2 * count].astype(F32).astype(jnp.int32)
        pieces = [array for group in zip(near_held, near_far, away_held, away_far) for array in group]
        pieces += [twin_near_held, twin_near_far, twin_away_held, *twin_last]

        def table(masks):
            near_ones = spot ^ jnp.asarray(masks, jnp.int32)
            return jnp.concatenate([near_ones + near * half, near_ones + near * (1 - half)])

        tables = [table(piece_masks(unit)) for unit in range(3)]
        places = [grad_place(spot ^ jnp.arange(8, dtype=jnp.int32), ROTATIONS[2 - unit]) for unit in range(3)]
        row_halves = [half, 1 - half]
        first_side = section
        small_order = (spot ^ jnp.arange(8, dtype=jnp.int32))
        small_order = jnp.stack([small_order + near * half, small_order + near * (1 - half)], 1).reshape(BLOCKS)
        pick = (small_order[None, :] == jnp.arange(BLOCKS, dtype=jnp.int32)[:, None]).astype(BF16)
        row_list, fbias_list = [], []
        laid = dot_nn(pick, small_held.reshape(BLOCKS, 2 * 16 * EXTRA)).reshape(BLOCKS, 2, 16, EXTRA)
        laid = jnp.where(section == 0, laid, laid[:, ::-1])
        for side in range(2):
            row_list.append(jnp.swapaxes(laid[:, side, :8, :rows], 0, 1).reshape(8, D))
            fbias_list.append(laid[:, side, 8:10].reshape(BLOCKS, 2 * EXTRA)[:, : 4 * rows].reshape(1, FF))
        rows_all = jnp.stack(row_list)
        fbias_all = jnp.stack(fbias_list)
    else:
        tables = [jnp.arange(BLOCKS, dtype=jnp.int32)] * 3
        places = [jnp.arange(8, dtype=jnp.int32)] * 3
        row_halves = [jnp.int32(0), jnp.int32(1)]
        first_side = 0
        moved = along(jnp.where(half == 1, inputs, cotangent), crossing)
        numbers_got = along(numbers, crossing)

        def whole(array, dim):
            full = lax.all_gather(array, ("section", "dp"), axis=0).reshape((2, n_dp) + array.shape)
            full = lax.dynamic_index_in_dim(full, half, 0, keepdims=False)
            shape = array.shape[:dim] + (n_dp * array.shape[dim],) + array.shape[dim + 1 :]
            return jnp.moveaxis(full, 0, dim).reshape(shape)

        full = whole(native, 1).reshape(2, 4, 4, ROWS, 3 * WIDE)
        pieces = [full[0, q, :, :, unit * WIDE : (unit + 1) * WIDE] for unit in range(3) for q in range(4)]
        pieces += [full[1, q] for q in range(3)]
        pieces += [full[1, 3, :, :, unit * WIDE : (unit + 1) * WIDE] for unit in range(3)]
        rows_all = whole(smalls, 2).astype(F32)
        fbias_all = whole(wides, 1).astype(F32)[:, None, :]

    numbers = jnp.where(at_home, numbers, numbers_got)
    chains = jnp.where(at_home, inputs, moved)
    top_grad = jnp.where(at_home, cotangent, moved)
    sides = numbers[:count] ^ first_side
    meta = [half[None].astype(jnp.int32), numbers, sides.astype(jnp.int32)] + tables
    meta = jnp.concatenate(meta + [section[None].astype(jnp.int32)])
    later = jnp.arange(count)[:, None] < jnp.arange(count)[None, :]
    rank = jnp.sum((sides[:, None] > sides[None, :]) | ((sides[:, None] == sides[None, :]) & later.T), axis=1)
    sorted_chains = jnp.sum(
        jnp.where(rank[None, :] == jnp.arange(count)[:, None], jnp.arange(count)[None, :], 0), axis=1
    )
    grad_meta = jnp.concatenate(
        [sorted_chains.astype(jnp.int32), jnp.sum(1 - sides)[None].astype(jnp.int32)]
        + [places[unit] for unit in (2, 1, 0)]
        + [value[None].astype(jnp.int32) for value in row_halves]
    )

    lead = 2
    call = functools.partial(layer_call, lead=lead, count=count, rows=rows_all, fbias=fbias_all, pieces=pieces)
    acts, grads, held = [None] * count, [None] * count, [None] * 7
    token = None

    def forward(c):
        nonlocal token
        out, _ = call(False, c, meta=after(meta, token), sources=[chains], held=[])
        acts[c], token = along(out, routes.up), out

    for c in range(count):
        forward(c)
    for slot in range(count + lead):
        sources = [chains]
        if slot < count:
            sources += [acts[slot], top_grad]
        if slot >= lead:
            sources.append(grads[slot - lead])
        out, held = call(True, slot, meta=after(meta, token), sources=sources, held=held)
        token = out
        if slot < count:
            grads[slot] = along(out, routes.down)
    act_all, grad_all, sums, fsums, s_left, s_right, give = held


    def gradient(unit, at, *others):
        return grad_call(unit, at, after(grad_meta, *others), s_left, s_right)

    act_move = by([pair for j in range(near) for pair in (((1, near + j), (0, near + j)), ((0, near + j), (1, j)))])
    grad_move = by([pair for j in range(near) for pair in (((0, j), (1, j)), ((1, j), (0, near + j)))])
    act_other, grad_other = act_move(give), grad_move(give)

    chosen = (sides[None, :] == jnp.arange(2, dtype=jnp.int32)[:, None]).astype(F32)
    row_sums = jnp.sum(chosen[:, :, None, None] * sums[None], axis=1)
    fbias_sums = jnp.sum(chosen[:, :, None] * fsums[None, :, 0], axis=1)
    small_grads = jnp.concatenate([jnp.swapaxes(row_sums, 1, 2), fbias_sums.reshape(2, D, 4)], -1)

    if fast:
        laid = jnp.concatenate([small_grads, jnp.zeros((2, D, EXTRA - 12), F32)], -1).astype(BF16)
        laid = jnp.swapaxes(laid.reshape(2, BLOCKS, ROWS, EXTRA), 0, 1)
        small_places = table(grad_masks(ROTATIONS[0]))
        pick = (small_places[:, None] == jnp.arange(BLOCKS, dtype=jnp.int32)[None, :]).astype(BF16)
        laid = dot_nn(pick, laid.reshape(BLOCKS, -1)).astype(BF16).reshape(2, 8, 2, ROWS, EXTRA)
        laid = jnp.transpose(laid, (2, 1, 0, 3, 4)).reshape(2, 8, 2 * ROWS, EXTRA)
        wave = Waves()

        def reduce_step(keep, got, step):
            width = 4 >> step
            send = [both(a[width:], b[width:]) for a, b in zip(keep, got)]
            return [both(a[:width], b[:width]) for a, b in zip(keep, got)], send

        def bits_out(send, step):
            return [(send[i], by_bit(ROTATIONS[i % 3][step])) for i in range(len(send))]

        units = (2, 1, 0)
        terms = [gradient(unit, 1) for unit in units]
        keep = [own for own, _ in terms]
        got = [swap_section(other) for _, other in terms]
        wave.before = (act_other, grad_other)
        near_terms = [gradient(2, 0, keep[2])]
        send = [both(a[4:], b[4:]) for a, b in zip(keep, got)]
        near_terms += [gradient(1, 0, *send)]
        near_terms += [gradient(0, 0, near_terms[1][0])]
        near_keep = [own for own, _ in near_terms]
        small_got, *far_got, other = wave((laid[1], swap_section), *bits_out(send, 0), (near_terms[0][1], swap_section))
        near_got = [other]
        keep = [both(after(a, *send)[:4], b[:4]) for a, b in zip(keep, got)]
        got = far_got
        small_keep = [laid[0]]
        for step in (1, 2):
            small_keep, small_send = reduce_step(small_keep, [small_got], step - 1)
            keep, send = reduce_step(keep, got, step)
            small_got, *got, other = wave(
                one_bit(small_send[0], step - 1), *bits_out(send, step), (near_terms[step][1], swap_section)
            )
            near_got.append(other)
        far_sum = jnp.concatenate([(a[0].astype(F32) + b[0].astype(F32)).astype(BF16) for a, b in zip(keep, got)], -1)

        keep, send = reduce_step(near_keep, near_got, 0)
        small_keep, small_send = reduce_step(small_keep, [small_got], 2)
        small_got, *got, straight = wave(
            one_bit(small_send[0], 2), *bits_out(send, 0), (far_sum, by(routes.straight_back))
        )
        small_end = (small_keep[0][0].astype(F32) + small_got[0].astype(F32)).astype(BF16)
        keep, send = reduce_step(keep, got, 1)
        small_straight, *got, cross_a = wave(
            (small_end[ROWS:], by(routes.straight_back)),
            *bits_out(send, 1),
            (far_sum[:, : 2 * WIDE], by(routes.crossed)),
        )
        keep, send = reduce_step(keep, got, 2)
        *got, cross_b = wave(
            *bits_out(send, 2),
            (jnp.concatenate([far_sum[:, 2 * WIDE :], small_end[ROWS:]], -1), by(routes.crossed)),
        )
        near_sum = [a[0].astype(F32) + b[0].astype(F32) for a, b in zip(keep, got)] + [small_end[:ROWS].astype(F32)]
        (beside,) = wave((jnp.concatenate(near_sum, -1).astype(BF16), by(routes.away_to_home)))
        crossed = jnp.concatenate([cross_a, cross_b], -1)
        straight = jnp.concatenate([straight, small_straight], -1)

        def settle(i, width):
            cols = slice(i * WIDE, i * WIDE + width)
            mine = jnp.where(at_home, near_sum[i], straight[:, cols].astype(F32))
            twin = jnp.where(at_home, beside[:, cols].astype(F32), crossed[:, cols].astype(F32))
            return jnp.stack([jnp.where(section == 0, mine, twin), jnp.where(section == 0, twin, mine)])

        unit_out = [None] * 3
        for i, unit in enumerate(units):
            unit_out[unit] = settle(i, WIDE)
        small_out = settle(3, EXTRA)
    else:

        def summed(array):
            layers = jnp.stack([jnp.where(half == layer, array, jnp.zeros_like(array)) for layer in range(2)])
            layers = jnp.swapaxes(layers, 1, 2).reshape(2 * n_dp, rows, 2, array.shape[-1])
            out = lax.psum_scatter(layers, ("section", "dp"), scatter_dimension=0, tiled=True)
            return jnp.swapaxes(out[0], 0, 1)

        unit_out = []
        for unit in range(3):
            terms = [gradient(unit, at) for at in range(2)]
            group = [jnp.concatenate([part[side] for part in terms], 0).reshape(D, WIDE) for side in range(2)]
            unit_out.append(summed(jnp.stack(group).astype(F32)))
        small_out = summed(small_grads)

    act_out = jnp.where(at_home, act_all, act_other)
    grad_out = jnp.where(at_home, grad_all, grad_other.astype(F32))

    turned = jnp.swapaxes(small_out[:, :, :8], 1, 2)
    return (
        act_out[None],
        grad_out[None],
        unit_out[0][None, :, :, : 3 * D],
        unit_out[0][None, :, :, 3 * D :],
        unit_out[1][None],
        jnp.swapaxes(unit_out[2], 1, 2)[None],
        turned[None, :, 0:4],
        small_out[:, :, 8:12].reshape(1, 2, 4 * rows),
        turned[None, :, 4:6],
        turned[None, :, 6:8],
    )


def solution(mesh):
    in_specs = (
        P("dp", None, None),
        P("dp", None, None),
        P("dp"),
        P("dp"),
        P("section", None, "dp", None),
        P("section", None, "dp", None),
        P("section", None, "dp", None),
        P("section", None, None, "dp"),
        P("section", None, None, "dp"),
        P("section", None, "dp"),
        P("section", None, None, "dp"),
        P("section", None, None, "dp"),
    )
    out_specs = (
        P("section", "dp", None, None),
        P("section", "dp", None, None),
        P("section", None, "dp", None),
        P("section", None, "dp", None),
        P("section", None, "dp", None),
        P("section", None, None, "dp"),
        P("section", None, None, "dp"),
        P("section", None, "dp"),
        P("section", None, None, "dp"),
        P("section", None, None, "dp"),
    )
    return jax.shard_map(
        per_device, mesh=mesh, in_specs=in_specs, out_specs=out_specs, check_vma=False
    )
```

```python
import functools

import jax
import jax.numpy as jnp
from jax import lax
from jax.experimental import pallas as pl
from jax.experimental.pallas import tpu as pltpu
from jax.sharding import PartitionSpec as P

D = 768
HEADS = 12
HEAD_DIM = 64
FF = 3072
SEQ = 160
PAIRS = HEADS // 2
BLOCKS = 16
ROWS = D // BLOCKS
WIDE = 3072
EXTRA = 128
CHUNK = 768

EPS = 1e-05
NEG = -1e30
SQRT_HALF = 0.7071067811865476
INV_ROOT = 0.3989422804014327
SCALE = HEAD_DIM**-0.5

ROTATIONS = ((0, 1, 2), (1, 2, 0), (2, 0, 1))
F32 = jnp.float32
BF16 = jnp.bfloat16


def piece_masks(unit):
    one, two, three = (1 << bit for bit in ROTATIONS[unit])
    return [far | mask for far in (0, three) for mask in (0, one, two, two | one)]


def grad_masks(rotation):
    one, two, three = (1 << bit for bit in rotation)
    return [(one if p & 4 else 0) | (two if p & 2 else 0) | (three if p & 1 else 0) for p in range(8)]


def grad_place(mask, rotation):
    one, two, three = rotation
    return ((mask >> one) & 1) * 4 + ((mask >> two) & 1) * 2 + ((mask >> three) & 1)


def dot_nn(a, b):
    return jnp.dot(a, b, preferred_element_type=F32)


def dot_nt(a, b):
    return lax.dot_general(a, b, (((1,), (1,)), ((), ())), preferred_element_type=F32)


def dot_tn(a, b):
    return lax.dot_general(a, b, (((0,), (0,)), ((), ())), preferred_element_type=F32)


def row_mean(a):
    return jnp.sum(a, axis=-1, keepdims=True) * (1.0 / D)


def norm(summed):
    center = summed - row_mean(summed)
    inverse = lax.rsqrt(row_mean(center * center) + EPS)
    return center * inverse, inverse


def norm_back(grad, normed, inverse, gain):
    scaled = grad * gain
    return inverse * (scaled - row_mean(scaled) - normed * row_mean(scaled * normed))


def col_sum(a):
    return jnp.sum(a.astype(F32), axis=0, keepdims=True)


def lanes(start, width):
    return pl.ds(pl.multiple_of(start, 128), width)


def layer_kernel(back, slot, lead, count, *refs):
    refs = list(refs)
    take = lambda n: [refs.pop(0) for _ in range(n)]
    has_high, has_low = back and slot < count, not back or slot >= lead
    (meta,) = take(1)
    rows_ref, fbias_ref = take(2)
    own_pieces, twin_joined, twin_last = take(12), take(3), take(3)
    (chains_hbm,) = take(1)
    act_hbm, top_hbm = take(2) if has_high else (None, None)
    (grad_hbm,) = take(1) if back and has_low else (None,)
    n_out = 8 if back else 1
    n_scratch = 24 if back else 12
    take(len(refs) - n_out - n_scratch)
    outs = take(n_out)
    scr = take(n_scratch)
    win, wout, wfi, wfo, x_s, qkv, ctx, act, hl, y_s, acc, sems = scr[:12]
    if back:
        (gx16_o, y_o, gx_o, sum_o, fsum_o, sl_o, sr_o, give_o) = outs
        gy_s, probs, slope, n1_s, n2_s, dr0, dpre, dfn, gx_s, sum_s, fsum_s, low_s = scr[12:]
    else:
        (y1_o,) = outs
    high = meta[0] == 1
    low = meta[0] == 0
    active = (high | low) if has_high and has_low else (high if has_high else low)

    @pl.when(active)
    def _():
        shift = lead if back else 0
        index = jnp.where(high, slot, slot - shift)
        length = meta[1 + count + index]

        def fetch(src, dst, sem):
            pltpu.make_async_copy(src, dst, sem).start()

        if has_high:

            @pl.when(high)
            def _():
                fetch(act_hbm.at[0], x_s, sems.at[4, 0])
                fetch(top_hbm.at[slot], gy_s, sems.at[4, 1])

        if has_low:

            @pl.when(low)
            def _():
                fetch(chains_hbm.at[slot - shift], x_s, sems.at[4, 0])
                if back:
                    fetch(grad_hbm.at[0], gy_s, sems.at[4, 1])

        def load_from(side):
            def one(unit, col, width, dst, group):
                for q in range(4):
                    if side == 0:
                        src, first = own_pieces[unit * 4 + q], col
                    elif q < 3:
                        src, first = twin_joined[q], unit * WIDE + col
                    else:
                        src, first = twin_last[unit], col

                    def body(e, carry):
                        k = q * 4 + e
                        row = pl.multiple_of(meta[1 + 3 * count + unit * BLOCKS + k] * ROWS, 16)
                        fetch(src.at[e, :, first : first + width], dst.at[pl.ds(row, ROWS)], sems.at[group, k])
                        return carry

                    lax.fori_loop(0, 4, body, 0)

            one(0, 0, 3 * D, win, 0)
            one(0, 3 * D, D, wout, 1)
            one(1, 0, FF, wfi, 2)
            one(2, 0, FF, wfo, 3)

        side = meta[1 + 2 * count + index]
        pl.when(side == 0)(lambda: load_from(0))
        pl.when(side != 0)(lambda: load_from(1))

        def landed(dst, group):
            def body(k, carry):
                part = dst.at[pl.ds(0, ROWS)]
                pltpu.make_async_copy(part, part, sems.at[group, k]).wait()
                return carry

            lax.fori_loop(0, BLOCKS, body, 0)

        def small(row):
            return rows_ref[side, row : row + 1, :]

        pltpu.make_async_copy(x_s, x_s, sems.at[4, 0]).wait()
        landed(win, 0)
        x = x_s[...]
        zero_row = jnp.zeros((1, D), F32)
        for n, bias in enumerate((small(0), zero_row, small(1))):
            cols = slice(n * D, (n + 1) * D)
            qkv[:, cols] = (dot_nn(x, win[:, cols]) + bias).astype(BF16)

        low_half = lax.broadcasted_iota(jnp.int32, (1, 2 * HEAD_DIM), 1) < HEAD_DIM
        head_mask = (low_half.astype(F32).astype(BF16), (1 - low_half.astype(F32)).astype(BF16))
        live = lax.broadcasted_iota(jnp.int32, (SEQ, SEQ), 1) < length

        def heads_fwd(pair, carry):
            off = pair * 2 * HEAD_DIM
            q2 = qkv[:, lanes(off, 128)]
            k2 = qkv[:, lanes(D + off, 128)]
            v2 = qkv[:, lanes(2 * D + off, 128)]
            joined = None
            for side in range(2):
                raw = dot_nt(q2 * head_mask[side], k2)
                scores = jnp.where(live, raw * SCALE, NEG)
                expo = jnp.exp(scores - jnp.max(scores, axis=-1, keepdims=True))
                prob = expo * (1.0 / jnp.sum(expo, axis=-1, keepdims=True))
                if back:
                    probs[2 * pair + side] = prob
                part = dot_nn(prob.astype(BF16), v2 * head_mask[side])
                joined = part if joined is None else joined + part
            ctx[:, lanes(off, 128)] = joined.astype(BF16)
            return carry

        lax.fori_loop(0, PAIRS, heads_fwd, 0, unroll=True)

        landed(wout, 1)
        branch = dot_nn(ctx[...], wout[...]) + small(2)
        n1, i1 = norm(x.astype(F32) + branch)
        hidden = n1 * small(4) + small(6)
        if back:
            n1_s[...] = n1
        hl[...] = hidden.astype(BF16)
        acc[...] = hidden
        landed(wfi, 2)
        landed(wfo, 3)

        def ffn_fwd(n, carry):
            cols = lanes(n * CHUNK, CHUNK)
            pre = dot_nn(hl[...], wfi[:, cols]) + fbias_ref[side, :, cols]
            phi = 0.5 * (1.0 + lax.erf(pre * SQRT_HALF))
            act[:, cols] = (pre * phi).astype(BF16)
            if back:
                slope[:, cols] = phi + pre * jnp.exp(-0.5 * pre * pre) * INV_ROOT
            return carry

        lax.fori_loop(0, FF // CHUNK, ffn_fwd, 0, unroll=True)
        branch = dot_nt(act[...], wfo[...]) + small(3)
        n2, i2 = norm(acc[...] + branch)
        y_s[...] = (n2 * small(5) + small(7)).astype(BF16)
        copies = []

        def put(src, dst, sem):
            copy = pltpu.make_async_copy(src, dst, sem)
            copy.start()
            copies.append(copy)

        if not back:
            put(y_s, y1_o.at[0], sems.at[5, 1])
        else:
            put(y_s, y_o.at[index], sems.at[5, 0])
            put(x_s, sl_o.at[2, index], sems.at[5, 2])
            put(ctx, sl_o.at[3, index], sems.at[5, 3])
            put(hl, sl_o.at[1, index], sems.at[5, 4])
            put(act, sr_o.at[2, index], sems.at[5, 5])
            pltpu.make_async_copy(gy_s, gy_s, sems.at[4, 1]).wait()
            alive = lax.broadcasted_iota(jnp.int32, (SEQ, D), 0) < jnp.where(high, length, SEQ)
            gy = jnp.where(alive, gy_s[...].astype(F32), 0.0)
            sum_s[5:6, :] = col_sum(gy * n2)
            sum_s[7:8, :] = col_sum(gy)
            gr2 = norm_back(gy, n2, i2, small(5))
            dfn[...] = gr2.astype(BF16)
            sum_s[3:4, :] = col_sum(dfn[...])
            put(dfn, sl_o.at[0, index], sems.at[5, 6])
            n2_s[...] = gr2

            def ffn_back(n, carry):
                cols = lanes(n * CHUNK, CHUNK)
                d_act = dot_nn(dfn[...], wfo[:, cols])
                d_pre = (d_act * slope[:, cols]).astype(BF16)
                dpre[:, cols] = d_pre
                fsum_s[:, cols] = col_sum(d_pre)
                return carry

            lax.fori_loop(0, FF // CHUNK, ffn_back, 0, unroll=True)
            put(dpre, sr_o.at[1, index], sems.at[5, 7])
            gh = n2_s[...] + dot_nt(dpre[...], wfi[...]).astype(BF16).astype(F32)
            n1 = n1_s[...]
            sum_s[4:5, :] = col_sum(gh * n1)
            sum_s[6:7, :] = col_sum(gh)
            gr1 = norm_back(gh, n1, i1, small(4))
            acc[...] = gr1
            d_attn = gr1.astype(BF16)
            dr0[:, 3 * D :] = d_attn
            sum_s[2:3, :] = col_sum(d_attn)
            gx_s[...] = dot_nt(d_attn, wout[...]).astype(BF16)

            def heads_back(pair, carry):
                off = pair * 2 * HEAD_DIM
                q2 = qkv[:, lanes(off, 128)]
                k2 = qkv[:, lanes(D + off, 128)]
                v2 = qkv[:, lanes(2 * D + off, 128)]
                dc2 = gx_s[:, lanes(off, 128)]
                dq = dk = dv = None
                for side in range(2):
                    prob = probs[2 * pair + side]
                    dch = dc2 * head_mask[side]
                    d_prob = dot_nt(dch, v2)
                    inner = jnp.sum(prob * d_prob, axis=-1, keepdims=True)
                    d_raw = (prob * (d_prob - inner) * SCALE).astype(BF16)
                    a = dot_nn(d_raw, k2 * head_mask[side])
                    b = dot_tn(d_raw, q2 * head_mask[side])
                    c = dot_tn(prob.astype(BF16), dch)
                    dq, dk, dv = (a, b, c) if dq is None else (dq + a, dk + b, dv + c)
                dr0[:, lanes(off, 128)] = dq.astype(BF16)
                dr0[:, lanes(D + off, 128)] = dk.astype(BF16)
                dr0[:, lanes(2 * D + off, 128)] = dv.astype(BF16)
                return carry

            lax.fori_loop(0, PAIRS, heads_back, 0, unroll=True)
            put(dr0, sr_o.at[0, index], sems.at[5, 8])
            sum_s[0:1, :] = col_sum(dr0[:, :D])
            sum_s[1:2, :] = col_sum(dr0[:, 2 * D : 3 * D])
            grad_a = dot_nt(dr0[:, : 3 * D], win[...]) + acc[...]
            n1_s[...] = grad_a
            low_s[...] = grad_a.astype(BF16)
            put(sum_s, sum_o.at[index], sems.at[5, 11])
            put(fsum_s, fsum_o.at[index], sems.at[5, 12])
            put(n1_s, gx_o.at[index], sems.at[5, 9])
            put(low_s, gx16_o.at[0], sems.at[5, 10])
            section = meta[1 + 3 * count + 3 * BLOCKS]
            for here, core, source in ((high, 1, x_s), (high, 0, y_s), (low, 0, gy_s), (low, 1, low_s)):
                pl.when(here & (section == core))(functools.partial(fetch, source, give_o.at[index], sems.at[5, 13]))
            pltpu.make_async_copy(low_s, low_s, sems.at[5, 13]).wait()
        for copy in copies:
            copy.wait()


def grad_kernel(unit, at, meta, *refs):
    n_left = 2 if unit == 0 else 1
    left, (right,), outs, (turned,) = refs[:n_left], refs[n_left : n_left + 1], refs[n_left + 1 : n_left + 3], refs[-1:]
    count = right.shape[0]
    n = pl.program_id(0)
    chain_of = [[meta[c] for c in range(count)], [meta[count - 1 - c] for c in range(count)]]

    @pl.when(n == 0)
    def _():
        for i in range(n_left):
            for side in range(2):
                turned[i, side] = jnp.concatenate([left[i][c] for c in chain_of[side]], 0).T

    pick = jnp.where(n == 3, 1, 0) if unit == 0 else 0

    def put(side, total):
        for block in range(8):
            place = meta[count + 1 + (2 - unit) * 8 + block]
            outs[side][place] = total[block * ROWS : (block + 1) * ROWS]

    def with_first(first):
        @pl.when(meta[count] == first)
        def _():
            for side, many in ((0, first), (1, count - first)):
                if many:
                    rows = jnp.concatenate([right[c] for c in chain_of[side][:many]], 0)
                    put(side, dot_nn(turned[pick, side, :, : many * SEQ], rows).astype(BF16))
                else:
                    put(side, jnp.zeros((D // 2, CHUNK), BF16))

    for first in range(count + 1):
        with_first(first)


ANY = pl.BlockSpec(memory_space=pl.ANY)
SMEM = pl.BlockSpec(memory_space=pltpu.SMEM)
VMEM = pl.BlockSpec(memory_space=pltpu.VMEM)


def shaped(shape, dtype):
    return jax.ShapeDtypeStruct(shape, dtype)


def saved_shapes(count):
    narrow = shaped((count, SEQ, D), BF16)
    return [
        narrow,
        shaped((count, SEQ, D), F32),
        shaped((count, 8, D), F32),
        shaped((count, 1, FF), F32),
        shaped((4, count, SEQ, D), BF16),
        shaped((3, count, SEQ, WIDE), BF16),
        narrow,
    ]


def layer_call(back, slot, lead, count, meta, rows, fbias, pieces, sources, held):
    scratch = [
        pltpu.VMEM((D, 3 * D), BF16),
        pltpu.VMEM((D, D), BF16),
        pltpu.VMEM((D, FF), BF16),
        pltpu.VMEM((D, FF), BF16),
        pltpu.VMEM((SEQ, D), BF16),
        pltpu.VMEM((SEQ, 3 * D), BF16),
        pltpu.VMEM((SEQ, D), BF16),
        pltpu.VMEM((SEQ, FF), BF16),
        pltpu.VMEM((SEQ, D), BF16),
        pltpu.VMEM((SEQ, D), BF16),
        pltpu.VMEM((SEQ, D), F32),
        pltpu.SemaphoreType.DMA((6, BLOCKS)),
    ]
    if back:
        scratch += [
            pltpu.VMEM((SEQ, D), BF16),
            pltpu.VMEM((HEADS, SEQ, SEQ), F32),
            pltpu.VMEM((SEQ, FF), F32),
            pltpu.VMEM((SEQ, D), F32),
            pltpu.VMEM((SEQ, D), F32),
            pltpu.VMEM((SEQ, WIDE), BF16),
            pltpu.VMEM((SEQ, FF), BF16),
            pltpu.VMEM((SEQ, D), BF16),
            pltpu.VMEM((SEQ, D), BF16),
            pltpu.VMEM((8, D), F32),
            pltpu.VMEM((1, FF), F32),
            pltpu.VMEM((SEQ, D), BF16),
        ]
    operands = [meta, rows, fbias, *pieces, *sources]
    specs = [SMEM, VMEM, VMEM] + [ANY] * (len(pieces) + len(sources))
    first = [shaped((1, SEQ, D), BF16)]
    kept = saved_shapes(count) if back else []
    aliases = {}
    for at, array in enumerate(held):
        if array is not None:
            aliases[len(operands)] = at + 1
            operands.append(array)
            specs.append(ANY)
    outs = pl.pallas_call(
        functools.partial(layer_kernel, back, slot, lead, count),
        out_shape=first + kept,
        in_specs=specs,
        out_specs=[ANY] * (1 + len(kept)),
        scratch_shapes=scratch,
        input_output_aliases=aliases,
        compiler_params=pltpu.CompilerParams(vmem_limit_bytes=50 * 1024 * 1024),
        cost_estimate=pl.CostEstimate(flops=1, bytes_accessed=1, transcendentals=0),
        name="layer_back" if back else "layer_fwd",
    )(*operands)
    return outs[0], list(outs[1:])


def grad_call(unit, at, meta, left, right):
    count = left.shape[1]
    which = {2: [0], 1: [1], 0: [2, 3]}[unit]

    def left_of(which):
        return pl.BlockSpec((None, count, SEQ, D // 2), lambda n, m: (which, 0, 0, m[count + 1 + 24 + at]))

    return pl.pallas_call(
        functools.partial(grad_kernel, unit, at),
        out_shape=[shaped((8, ROWS, WIDE), BF16)] * 2,
        grid_spec=pltpu.PrefetchScalarGridSpec(
            num_scalar_prefetch=1,
            grid=(WIDE // CHUNK,),
            in_specs=[left_of(i) for i in which]
            + [pl.BlockSpec((None, count, SEQ, CHUNK), lambda n, m: (unit, 0, 0, n))],
            out_specs=[pl.BlockSpec((8, ROWS, CHUNK), lambda n, m: (0, 0, n))] * 2,
            scratch_shapes=[pltpu.VMEM((len(which), 2, D // 2, count * SEQ), BF16)],
        ),
        compiler_params=pltpu.CompilerParams(vmem_limit_bytes=50 * 1024 * 1024),
        cost_estimate=pl.CostEstimate(flops=1, bytes_accessed=1, transcendentals=0),
        name="layer_grad",
    )(meta, *[left] * len(which), right)


def swap_bit(array, bit):
    count = lax.axis_size("dp")
    return lax.ppermute(array, "dp", [(i, i ^ (1 << bit)) for i in range(count)])


def swap_section(array):
    return lax.ppermute(array, "section", [(0, 1), (1, 0)])


def along(array, pairs):
    count = lax.axis_size("dp")
    flat = [(s * count + i, t * count + k) for (s, i), (t, k) in pairs]
    return lax.ppermute(array, ("section", "dp"), flat)


def both(first, second):
    return (first.astype(F32) + second.astype(F32)).astype(BF16)


def after(array, *others):
    others = [other for other in others if other is not None]
    return lax.optimization_barrier((array, *others))[0] if others else array


class Waves:
    def __init__(self):
        self.before = ()

    def __call__(self, *sends):
        arrays = lax.optimization_barrier(tuple(array for array, _ in sends) + self.before)[: len(sends)]
        self.before = tuple(move(array) for array, (_, move) in zip(arrays, sends))
        return list(self.before)


def by_bit(bit):
    return lambda array: swap_bit(array, bit)


def by(pairs):
    return lambda array: along(array, pairs)


class Routes:
    def __init__(self, near):
        self.home_to_away = [((h, h * near + j), (1 - h, h * near + j)) for h in range(2) for j in range(near)]
        self.away_to_home = [(b, a) for a, b in self.home_to_away]
        self.straight = [((s, (1 - s) * near + j), (s, s * near + j)) for s in range(2) for j in range(near)]
        self.straight_back = [(b, a) for a, b in self.straight]
        self.crossed = [((s, (1 - s) * near + j), (1 - s, s * near + j)) for s in range(2) for j in range(near)]
        self.up = [((s, j), (s, near + j)) for s in range(2) for j in range(near)]
        self.down = [(b, a) for a, b in self.up]


def per_device(
    inputs,
    cotangent,
    chain_tags,
    chain_lengths,
    attn_in,
    attn_out,
    ffn_in,
    ffn_out,
    proj_bias,
    ffn_bias,
    norm_gain,
    norm_shift,
):
    n_dp = lax.axis_size("dp")
    near = n_dp // 2
    rows = attn_in.shape[2]
    count = inputs.shape[0]
    fast = near == 8 and rows == ROWS
    routes = Routes(near)
    section = lax.axis_index("section")
    place = lax.axis_index("dp")
    half = place // near
    spot = place % near
    at_home = section == half

    native = jnp.concatenate(
        [
            attn_in[0].astype(BF16),
            attn_out[0].astype(BF16),
            ffn_in[0].astype(BF16),
            jnp.swapaxes(ffn_out[0].astype(BF16), 1, 2),
        ],
        -1,
    )
    smalls = jnp.concatenate([proj_bias[0], norm_gain[0], norm_shift[0]], 1).astype(BF16)
    wides = ffn_bias[0].astype(BF16)
    numbers = jnp.concatenate([chain_tags, chain_lengths])
    crossing = routes.straight_back
    if fast:
        mine = jnp.where(section == 0, native[0], native[1])
        twin = jnp.where(section == 0, native[1], native[0])
        wave = Waves()
        cuts = (0, WIDE, 2 * WIDE, 3 * WIDE)

        def bits(held, step):
            return [(held[unit], by_bit(ROTATIONS[unit][step])) for unit in range(3)]

        def joined(held, got):
            return [jnp.concatenate([a, b], 0) for a, b in zip(held, got)]

        def own(blocks):
            return [blocks[None, :, cuts[unit] : cuts[unit + 1]] for unit in range(3)]

        def merged(held):
            return jnp.concatenate(held, -1)

        def one_bit(array, bit):
            return (array, by_bit(bit))

        small = jnp.pad(smalls, ((0, 0), (0, 0), (0, EXTRA - rows)))
        wide = jnp.pad(wides, ((0, 0), (0, 2 * EXTRA - 4 * rows))).reshape(2, 2, EXTRA)
        small = jnp.pad(jnp.concatenate([small, wide], 1), ((0, 0), (0, 6), (0, 0)))
        small = small.at[:, 10, : 2 * count].set(numbers.astype(BF16)[None])
        home, small_home = wave((twin, by(routes.home_to_away)), (small, by(routes.home_to_away)))
        near_held = own(jnp.where(at_home, mine, home))
        *got, small_straight, cross_a = wave(
            *bits(near_held, 0), (small, by(routes.straight)), (twin[:, : cuts[1]], by(routes.crossed))
        )
        near_held = joined(near_held, got)
        *got, small_crossed, cross_b = wave(
            *bits(near_held, 1), (small, by(routes.crossed)), (twin[:, cuts[1] :], by(routes.crossed))
        )
        small_held = jnp.stack(
            [jnp.where(at_home, small, small_home), jnp.where(at_home, small_straight, small_crossed)]
        )[None]
        near_held = joined(near_held, got)
        *near_far, small_got, straight = wave(
            *bits(near_held, 2), one_bit(small_held, 0), (mine, by(routes.straight))
        )
        small_held = jnp.concatenate([small_held, small_got], 0)
        away_held = own(jnp.where(at_home, straight, jnp.concatenate([cross_a, cross_b], -1)))
        *got, small_got, twin_near_held = wave(
            *bits(away_held, 0), one_bit(small_held, 1), (merged(near_held), swap_section)
        )
        small_held = jnp.concatenate([small_held, small_got], 0)
        away_held = joined(away_held, got)
        *got, moved, twin_near_far = wave(
            *bits(away_held, 1),
            (jnp.where(half == 1, inputs, cotangent), by(crossing)),
            (merged(near_far), swap_section),
        )
        away_held = joined(away_held, got)
        *away_far, small_got, twin_away_held = wave(
            *bits(away_held, 2), one_bit(small_held, 2), (merged(away_held), swap_section)
        )
        small_held = jnp.concatenate([small_held, small_got], 0)
        twin_last = wave(*[(array, swap_section) for array in away_far])
        numbers_got = small_crossed[0, 10, : 2 * count].astype(F32).astype(jnp.int32)
        pieces = [array for group in zip(near_held, near_far, away_held, away_far) for array in group]
        pieces += [twin_near_held, twin_near_far, twin_away_held, *twin_last]

        def table(masks):
            near_ones = spot ^ jnp.asarray(masks, jnp.int32)
            return jnp.concatenate([near_ones + near * half, near_ones + near * (1 - half)])

        tables = [table(piece_masks(unit)) for unit in range(3)]
        places = [grad_place(spot ^ jnp.arange(8, dtype=jnp.int32), ROTATIONS[2 - unit]) for unit in range(3)]
        row_halves = [half, 1 - half]
        first_side = section
        small_order = (spot ^ jnp.arange(8, dtype=jnp.int32))
        small_order = jnp.stack([small_order + near * half, small_order + near * (1 - half)], 1).reshape(BLOCKS)
        pick = (small_order[None, :] == jnp.arange(BLOCKS, dtype=jnp.int32)[:, None]).astype(BF16)
        row_list, fbias_list = [], []
        laid = dot_nn(pick, small_held.reshape(BLOCKS, 2 * 16 * EXTRA)).reshape(BLOCKS, 2, 16, EXTRA)
        laid = jnp.where(section == 0, laid, laid[:, ::-1])
        for side in range(2):
            row_list.append(jnp.swapaxes(laid[:, side, :8, :rows], 0, 1).reshape(8, D))
            fbias_list.append(laid[:, side, 8:10].reshape(BLOCKS, 2 * EXTRA)[:, : 4 * rows].reshape(1, FF))
        rows_all = jnp.stack(row_list)
        fbias_all = jnp.stack(fbias_list)
    else:
        tables = [jnp.arange(BLOCKS, dtype=jnp.int32)] * 3
        places = [jnp.arange(8, dtype=jnp.int32)] * 3
        row_halves = [jnp.int32(0), jnp.int32(1)]
        first_side = 0
        moved = along(jnp.where(half == 1, inputs, cotangent), crossing)
        numbers_got = along(numbers, crossing)

        def whole(array, dim):
            full = lax.all_gather(array, ("section", "dp"), axis=0).reshape((2, n_dp) + array.shape)
            full = lax.dynamic_index_in_dim(full, half, 0, keepdims=False)
            shape = array.shape[:dim] + (n_dp * array.shape[dim],) + array.shape[dim + 1 :]
            return jnp.moveaxis(full, 0, dim).reshape(shape)

        full = whole(native, 1).reshape(2, 4, 4, ROWS, 3 * WIDE)
        pieces = [full[0, q, :, :, unit * WIDE : (unit + 1) * WIDE] for unit in range(3) for q in range(4)]
        pieces += [full[1, q] for q in range(3)]
        pieces += [full[1, 3, :, :, unit * WIDE : (unit + 1) * WIDE] for unit in range(3)]
        rows_all = whole(smalls, 2).astype(F32)
        fbias_all = whole(wides, 1).astype(F32)[:, None, :]

    numbers = jnp.where(at_home, numbers, numbers_got)
    chains = jnp.where(at_home, inputs, moved)
    top_grad = jnp.where(at_home, cotangent, moved)
    sides = numbers[:count] ^ first_side
    meta = [half[None].astype(jnp.int32), numbers, sides.astype(jnp.int32)] + tables
    meta = jnp.concatenate(meta + [section[None].astype(jnp.int32)])
    later = jnp.arange(count)[:, None] < jnp.arange(count)[None, :]
    rank = jnp.sum((sides[:, None] > sides[None, :]) | ((sides[:, None] == sides[None, :]) & later.T), axis=1)
    sorted_chains = jnp.sum(
        jnp.where(rank[None, :] == jnp.arange(count)[:, None], jnp.arange(count)[None, :], 0), axis=1
    )
    grad_meta = jnp.concatenate(
        [sorted_chains.astype(jnp.int32), jnp.sum(1 - sides)[None].astype(jnp.int32)]
        + [places[unit] for unit in (2, 1, 0)]
        + [value[None].astype(jnp.int32) for value in row_halves]
    )

    lead = 2
    call = functools.partial(layer_call, lead=lead, count=count, rows=rows_all, fbias=fbias_all, pieces=pieces)
    acts, grads, held = [None] * count, [None] * count, [None] * 7
    token = None

    def forward(c):
        nonlocal token
        out, _ = call(False, c, meta=after(meta, token), sources=[chains], held=[])
        acts[c], token = along(out, routes.up), out

    for c in range(count):
        forward(c)
    for slot in range(count + lead):
        sources = [chains]
        if slot < count:
            sources += [acts[slot], top_grad]
        if slot >= lead:
            sources.append(grads[slot - lead])
        out, held = call(True, slot, meta=after(meta, token), sources=sources, held=held)
        token = out
        if slot < count:
            grads[slot] = along(out, routes.down)
    act_all, grad_all, sums, fsums, s_left, s_right, give = held


    def gradient(unit, at, *others):
        return grad_call(unit, at, after(grad_meta, *others), s_left, s_right)

    act_move = by([pair for j in range(near) for pair in (((1, near + j), (0, near + j)), ((0, near + j), (1, j)))])
    grad_move = by([pair for j in range(near) for pair in (((0, j), (1, j)), ((1, j), (0, near + j)))])
    act_other, grad_other = act_move(give), grad_move(give)

    chosen = (sides[None, :] == jnp.arange(2, dtype=jnp.int32)[:, None]).astype(F32)
    row_sums = jnp.sum(chosen[:, :, None, None] * sums[None], axis=1)
    fbias_sums = jnp.sum(chosen[:, :, None] * fsums[None, :, 0], axis=1)
    small_grads = jnp.concatenate([jnp.swapaxes(row_sums, 1, 2), fbias_sums.reshape(2, D, 4)], -1)

    if fast:
        laid = jnp.concatenate([small_grads, jnp.zeros((2, D, EXTRA - 12), F32)], -1).astype(BF16)
        laid = jnp.swapaxes(laid.reshape(2, BLOCKS, ROWS, EXTRA), 0, 1)
        small_places = table(grad_masks(ROTATIONS[0]))
        pick = (small_places[:, None] == jnp.arange(BLOCKS, dtype=jnp.int32)[None, :]).astype(BF16)
        laid = dot_nn(pick, laid.reshape(BLOCKS, -1)).astype(BF16).reshape(2, 8, 2, ROWS, EXTRA)
        laid = jnp.transpose(laid, (2, 1, 0, 3, 4)).reshape(2, 8, 2 * ROWS, EXTRA)
        wave = Waves()

        def reduce_step(keep, got, step):
            width = 4 >> step
            send = [both(a[width:], b[width:]) for a, b in zip(keep, got)]
            return [both(a[:width], b[:width]) for a, b in zip(keep, got)], send

        def bits_out(send, step):
            return [(send[i], by_bit(ROTATIONS[i % 3][step])) for i in range(len(send))]

        units = (2, 1, 0)
        terms = [gradient(unit, 1) for unit in units]
        keep = [own for own, _ in terms]
        got = [swap_section(other) for _, other in terms]
        wave.before = (act_other, grad_other)
        near_terms = [gradient(2, 0, keep[2])]
        send = [both(a[4:], b[4:]) for a, b in zip(keep, got)]
        near_terms += [gradient(1, 0, *send)]
        near_terms += [gradient(0, 0, near_terms[1][0])]
        near_keep = [own for own, _ in near_terms]
        small_got, *far_got, other = wave((laid[1], swap_section), *bits_out(send, 0), (near_terms[0][1], swap_section))
        near_got = [other]
        keep = [both(after(a, *send)[:4], b[:4]) for a, b in zip(keep, got)]
        got = far_got
        small_keep = [laid[0]]
        for step in (1, 2):
            small_keep, small_send = reduce_step(small_keep, [small_got], step - 1)
            keep, send = reduce_step(keep, got, step)
            small_got, *got, other = wave(
                one_bit(small_send[0], step - 1), *bits_out(send, step), (near_terms[step][1], swap_section)
            )
            near_got.append(other)
        far_sum = jnp.concatenate([(a[0].astype(F32) + b[0].astype(F32)).astype(BF16) for a, b in zip(keep, got)], -1)

        keep, send = reduce_step(near_keep, near_got, 0)
        small_keep, small_send = reduce_step(small_keep, [small_got], 2)
        small_got, *got, cross_a = wave(
            one_bit(small_send[0], 2), *bits_out(send, 0), (far_sum[:, :WIDE], by(routes.crossed))
        )
        small_end = (small_keep[0][0].astype(F32) + small_got[0].astype(F32)).astype(BF16)
        keep, send = reduce_step(keep, got, 1)
        small_straight, *got, straight = wave(
            (small_end[ROWS:], by(routes.straight_back)), *bits_out(send, 1), (far_sum, by(routes.straight_back))
        )
        keep, send = reduce_step(keep, got, 2)
        *got, cross_b = wave(
            *bits_out(send, 2),
            (jnp.concatenate([far_sum[:, WIDE:], small_end[ROWS:]], -1), by(routes.crossed)),
        )
        near_sum = [a[0].astype(F32) + b[0].astype(F32) for a, b in zip(keep, got)] + [small_end[:ROWS].astype(F32)]
        (beside,) = wave((jnp.concatenate(near_sum, -1).astype(BF16), by(routes.away_to_home)))
        crossed = jnp.concatenate([cross_a, cross_b], -1)
        straight = jnp.concatenate([straight, small_straight], -1)

        def settle(i, width):
            cols = slice(i * WIDE, i * WIDE + width)
            mine = jnp.where(at_home, near_sum[i], straight[:, cols].astype(F32))
            twin = jnp.where(at_home, beside[:, cols].astype(F32), crossed[:, cols].astype(F32))
            return jnp.stack([jnp.where(section == 0, mine, twin), jnp.where(section == 0, twin, mine)])

        unit_out = [None] * 3
        for i, unit in enumerate(units):
            unit_out[unit] = settle(i, WIDE)
        small_out = settle(3, EXTRA)
    else:

        def summed(array):
            layers = jnp.stack([jnp.where(half == layer, array, jnp.zeros_like(array)) for layer in range(2)])
            layers = jnp.swapaxes(layers, 1, 2).reshape(2 * n_dp, rows, 2, array.shape[-1])
            out = lax.psum_scatter(layers, ("section", "dp"), scatter_dimension=0, tiled=True)
            return jnp.swapaxes(out[0], 0, 1)

        unit_out = []
        for unit in range(3):
            terms = [gradient(unit, at) for at in range(2)]
            group = [jnp.concatenate([part[side] for part in terms], 0).reshape(D, WIDE) for side in range(2)]
            unit_out.append(summed(jnp.stack(group).astype(F32)))
        small_out = summed(small_grads)

    act_out = jnp.where(at_home, act_all, act_other)
    grad_out = jnp.where(at_home, grad_all, grad_other.astype(F32))

    turned = jnp.swapaxes(small_out[:, :, :8], 1, 2)
    return (
        act_out[None],
        grad_out[None],
        unit_out[0][None, :, :, : 3 * D],
        unit_out[0][None, :, :, 3 * D :],
        unit_out[1][None],
        jnp.swapaxes(unit_out[2], 1, 2)[None],
        turned[None, :, 0:4],
        small_out[:, :, 8:12].reshape(1, 2, 4 * rows),
        turned[None, :, 4:6],
        turned[None, :, 6:8],
    )


def solution(mesh):
    in_specs = (
        P("dp", None, None),
        P("dp", None, None),
        P("dp"),
        P("dp"),
        P("section", None, "dp", None),
        P("section", None, "dp", None),
        P("section", None, "dp", None),
        P("section", None, None, "dp"),
        P("section", None, None, "dp"),
        P("section", None, "dp"),
        P("section", None, None, "dp"),
        P("section", None, None, "dp"),
    )
    out_specs = (
        P("section", "dp", None, None),
        P("section", "dp", None, None),
        P("section", None, "dp", None),
        P("section", None, "dp", None),
        P("section", None, "dp", None),
        P("section", None, None, "dp"),
        P("section", None, None, "dp"),
        P("section", None, "dp"),
        P("section", None, None, "dp"),
        P("section", None, None, "dp"),
    )
    return jax.shard_map(
        per_device, mesh=mesh, in_specs=in_specs, out_specs=out_specs, check_vma=False
    )
```

```python
import functools

import jax
import jax.numpy as jnp
from jax import lax
from jax.experimental import pallas as pl
from jax.experimental.pallas import tpu as pltpu
from jax.sharding import PartitionSpec as P

D = 768
HEADS = 12
HEAD_DIM = 64
FF = 3072
SEQ = 160
PAIRS = HEADS // 2
BLOCKS = 16
ROWS = D // BLOCKS
WIDE = 3072
EXTRA = 128
CHUNK = 768

EPS = 1e-05
NEG = -1e30
SQRT_HALF = 0.7071067811865476
INV_ROOT = 0.3989422804014327
SCALE = HEAD_DIM**-0.5

ROTATIONS = ((0, 1, 2), (1, 2, 0), (2, 0, 1))
F32 = jnp.float32
BF16 = jnp.bfloat16


def piece_masks(unit):
    one, two, three = (1 << bit for bit in ROTATIONS[unit])
    return [far | mask for far in (0, three) for mask in (0, one, two, two | one)]


def grad_masks(rotation):
    one, two, three = (1 << bit for bit in rotation)
    return [(one if p & 4 else 0) | (two if p & 2 else 0) | (three if p & 1 else 0) for p in range(8)]


def grad_place(mask, rotation):
    one, two, three = rotation
    return ((mask >> one) & 1) * 4 + ((mask >> two) & 1) * 2 + ((mask >> three) & 1)


def dot_nn(a, b):
    return jnp.dot(a, b, preferred_element_type=F32)


def dot_nt(a, b):
    return lax.dot_general(a, b, (((1,), (1,)), ((), ())), preferred_element_type=F32)


def dot_tn(a, b):
    return lax.dot_general(a, b, (((0,), (0,)), ((), ())), preferred_element_type=F32)


def row_mean(a):
    return jnp.sum(a, axis=-1, keepdims=True) * (1.0 / D)


def norm(summed):
    center = summed - row_mean(summed)
    inverse = lax.rsqrt(row_mean(center * center) + EPS)
    return center * inverse, inverse


def norm_back(grad, normed, inverse, gain):
    scaled = grad * gain
    return inverse * (scaled - row_mean(scaled) - normed * row_mean(scaled * normed))


def col_sum(a):
    return jnp.sum(a.astype(F32), axis=0, keepdims=True)


def lanes(start, width):
    return pl.ds(pl.multiple_of(start, 128), width)


def layer_kernel(back, slot, lead, count, *refs):
    refs = list(refs)
    take = lambda n: [refs.pop(0) for _ in range(n)]
    has_high, has_low = back and slot < count, not back or slot >= lead
    (meta,) = take(1)
    rows_ref, fbias_ref = take(2)
    own_pieces, twin_joined, twin_last = take(12), take(3), take(3)
    (chains_hbm,) = take(1)
    act_hbm, top_hbm = take(2) if has_high else (None, None)
    (grad_hbm,) = take(1) if back and has_low else (None,)
    n_out = 8 if back else 1
    n_scratch = 24 if back else 12
    take(len(refs) - n_out - n_scratch)
    outs = take(n_out)
    scr = take(n_scratch)
    win, wout, wfi, wfo, x_s, qkv, ctx, act, hl, y_s, acc, sems = scr[:12]
    if back:
        (gx16_o, y_o, gx_o, sum_o, fsum_o, sl_o, sr_o, give_o) = outs
        gy_s, probs, slope, n1_s, n2_s, dr0, dpre, dfn, gx_s, sum_s, fsum_s, low_s = scr[12:]
    else:
        (y1_o,) = outs
    high = meta[0] == 1
    low = meta[0] == 0
    active = (high | low) if has_high and has_low else (high if has_high else low)

    @pl.when(active)
    def _():
        shift = lead if back else 0
        index = jnp.where(high, slot, slot - shift)
        length = meta[1 + count + index]

        def fetch(src, dst, sem):
            pltpu.make_async_copy(src, dst, sem).start()

        if has_high:

            @pl.when(high)
            def _():
                fetch(act_hbm.at[0], x_s, sems.at[4, 0])
                fetch(top_hbm.at[slot], gy_s, sems.at[4, 1])

        if has_low:

            @pl.when(low)
            def _():
                fetch(chains_hbm.at[slot - shift], x_s, sems.at[4, 0])
                if back:
                    fetch(grad_hbm.at[0], gy_s, sems.at[4, 1])

        def load_from(side):
            def one(unit, col, width, dst, group):
                for q in range(4):
                    if side == 0:
                        src, first = own_pieces[unit * 4 + q], col
                    elif q < 3:
                        src, first = twin_joined[q], unit * WIDE + col
                    else:
                        src, first = twin_last[unit], col

                    def body(e, carry):
                        k = q * 4 + e
                        row = pl.multiple_of(meta[1 + 3 * count + unit * BLOCKS + k] * ROWS, 16)
                        fetch(src.at[e, :, first : first + width], dst.at[pl.ds(row, ROWS)], sems.at[group, k])
                        return carry

                    lax.fori_loop(0, 4, body, 0)

            one(0, 0, 3 * D, win, 0)
            one(0, 3 * D, D, wout, 1)
            one(1, 0, FF, wfi, 2)
            one(2, 0, FF, wfo, 3)

        side = meta[1 + 2 * count + index]
        pl.when(side == 0)(lambda: load_from(0))
        pl.when(side != 0)(lambda: load_from(1))

        def landed(dst, group):
            def body(k, carry):
                part = dst.at[pl.ds(0, ROWS)]
                pltpu.make_async_copy(part, part, sems.at[group, k]).wait()
                return carry

            lax.fori_loop(0, BLOCKS, body, 0)

        def small(row):
            return rows_ref[side, row : row + 1, :]

        pltpu.make_async_copy(x_s, x_s, sems.at[4, 0]).wait()
        landed(win, 0)
        x = x_s[...]
        zero_row = jnp.zeros((1, D), F32)
        for n, bias in enumerate((small(0), zero_row, small(1))):
            cols = slice(n * D, (n + 1) * D)
            qkv[:, cols] = (dot_nn(x, win[:, cols]) + bias).astype(BF16)

        low_half = lax.broadcasted_iota(jnp.int32, (1, 2 * HEAD_DIM), 1) < HEAD_DIM
        head_mask = (low_half.astype(F32).astype(BF16), (1 - low_half.astype(F32)).astype(BF16))
        live = lax.broadcasted_iota(jnp.int32, (SEQ, SEQ), 1) < length

        def heads_fwd(pair, carry):
            off = pair * 2 * HEAD_DIM
            q2 = qkv[:, lanes(off, 128)]
            k2 = qkv[:, lanes(D + off, 128)]
            v2 = qkv[:, lanes(2 * D + off, 128)]
            joined = None
            for side in range(2):
                raw = dot_nt(q2 * head_mask[side], k2)
                scores = jnp.where(live, raw * SCALE, NEG)
                expo = jnp.exp(scores - jnp.max(scores, axis=-1, keepdims=True))
                prob = expo * (1.0 / jnp.sum(expo, axis=-1, keepdims=True))
                if back:
                    probs[2 * pair + side] = prob
                part = dot_nn(prob.astype(BF16), v2 * head_mask[side])
                joined = part if joined is None else joined + part
            ctx[:, lanes(off, 128)] = joined.astype(BF16)
            return carry

        lax.fori_loop(0, PAIRS, heads_fwd, 0, unroll=True)

        landed(wout, 1)
        branch = dot_nn(ctx[...], wout[...]) + small(2)
        n1, i1 = norm(x.astype(F32) + branch)
        hidden = n1 * small(4) + small(6)
        if back:
            n1_s[...] = n1
        hl[...] = hidden.astype(BF16)
        acc[...] = hidden
        landed(wfi, 2)
        landed(wfo, 3)

        def ffn_fwd(n, carry):
            cols = lanes(n * CHUNK, CHUNK)
            pre = dot_nn(hl[...], wfi[:, cols]) + fbias_ref[side, :, cols]
            phi = 0.5 * (1.0 + lax.erf(pre * SQRT_HALF))
            act[:, cols] = (pre * phi).astype(BF16)
            if back:
                slope[:, cols] = phi + pre * jnp.exp(-0.5 * pre * pre) * INV_ROOT
            return carry

        lax.fori_loop(0, FF // CHUNK, ffn_fwd, 0, unroll=True)
        branch = dot_nt(act[...], wfo[...]) + small(3)
        n2, i2 = norm(acc[...] + branch)
        y_s[...] = (n2 * small(5) + small(7)).astype(BF16)
        copies = []

        def put(src, dst, sem):
            copy = pltpu.make_async_copy(src, dst, sem)
            copy.start()
            copies.append(copy)

        if not back:
            put(y_s, y1_o.at[0], sems.at[5, 1])
        else:
            put(y_s, y_o.at[index], sems.at[5, 0])
            put(x_s, sl_o.at[2, index], sems.at[5, 2])
            put(ctx, sl_o.at[3, index], sems.at[5, 3])
            put(hl, sl_o.at[1, index], sems.at[5, 4])
            put(act, sr_o.at[2, index], sems.at[5, 5])
            pltpu.make_async_copy(gy_s, gy_s, sems.at[4, 1]).wait()
            alive = lax.broadcasted_iota(jnp.int32, (SEQ, D), 0) < jnp.where(high, length, SEQ)
            gy = jnp.where(alive, gy_s[...].astype(F32), 0.0)
            sum_s[5:6, :] = col_sum(gy * n2)
            sum_s[7:8, :] = col_sum(gy)
            gr2 = norm_back(gy, n2, i2, small(5))
            dfn[...] = gr2.astype(BF16)
            sum_s[3:4, :] = col_sum(dfn[...])
            put(dfn, sl_o.at[0, index], sems.at[5, 6])
            n2_s[...] = gr2

            def ffn_back(n, carry):
                cols = lanes(n * CHUNK, CHUNK)
                d_act = dot_nn(dfn[...], wfo[:, cols])
                d_pre = (d_act * slope[:, cols]).astype(BF16)
                dpre[:, cols] = d_pre
                fsum_s[:, cols] = col_sum(d_pre)
                return carry

            lax.fori_loop(0, FF // CHUNK, ffn_back, 0, unroll=True)
            put(dpre, sr_o.at[1, index], sems.at[5, 7])
            gh = n2_s[...] + dot_nt(dpre[...], wfi[...]).astype(BF16).astype(F32)
            n1 = n1_s[...]
            sum_s[4:5, :] = col_sum(gh * n1)
            sum_s[6:7, :] = col_sum(gh)
            gr1 = norm_back(gh, n1, i1, small(4))
            acc[...] = gr1
            d_attn = gr1.astype(BF16)
            dr0[:, 3 * D :] = d_attn
            sum_s[2:3, :] = col_sum(d_attn)
            gx_s[...] = dot_nt(d_attn, wout[...]).astype(BF16)

            def heads_back(pair, carry):
                off = pair * 2 * HEAD_DIM
                q2 = qkv[:, lanes(off, 128)]
                k2 = qkv[:, lanes(D + off, 128)]
                v2 = qkv[:, lanes(2 * D + off, 128)]
                dc2 = gx_s[:, lanes(off, 128)]
                dq = dk = dv = None
                for side in range(2):
                    prob = probs[2 * pair + side]
                    dch = dc2 * head_mask[side]
                    d_prob = dot_nt(dch, v2)
                    inner = jnp.sum(prob * d_prob, axis=-1, keepdims=True)
                    d_raw = (prob * (d_prob - inner) * SCALE).astype(BF16)
                    a = dot_nn(d_raw, k2 * head_mask[side])
                    b = dot_tn(d_raw, q2 * head_mask[side])
                    c = dot_tn(prob.astype(BF16), dch)
                    dq, dk, dv = (a, b, c) if dq is None else (dq + a, dk + b, dv + c)
                dr0[:, lanes(off, 128)] = dq.astype(BF16)
                dr0[:, lanes(D + off, 128)] = dk.astype(BF16)
                dr0[:, lanes(2 * D + off, 128)] = dv.astype(BF16)
                return carry

            lax.fori_loop(0, PAIRS, heads_back, 0, unroll=True)
            put(dr0, sr_o.at[0, index], sems.at[5, 8])
            sum_s[0:1, :] = col_sum(dr0[:, :D])
            sum_s[1:2, :] = col_sum(dr0[:, 2 * D : 3 * D])
            grad_a = dot_nt(dr0[:, : 3 * D], win[...]) + acc[...]
            n1_s[...] = grad_a
            low_s[...] = grad_a.astype(BF16)
            put(sum_s, sum_o.at[index], sems.at[5, 11])
            put(fsum_s, fsum_o.at[index], sems.at[5, 12])
            put(n1_s, gx_o.at[index], sems.at[5, 9])
            put(low_s, gx16_o.at[0], sems.at[5, 10])
            section = meta[1 + 3 * count + 3 * BLOCKS]
            for here, core, source in ((high, 1, x_s), (high, 0, y_s), (low, 0, gy_s), (low, 1, low_s)):
                pl.when(here & (section == core))(functools.partial(fetch, source, give_o.at[index], sems.at[5, 13]))
            pltpu.make_async_copy(low_s, low_s, sems.at[5, 13]).wait()
        for copy in copies:
            copy.wait()


def grad_kernel(unit, at, meta, *refs):
    n_left = 2 if unit == 0 else 1
    left, (right,), outs, (turned,) = refs[:n_left], refs[n_left : n_left + 1], refs[n_left + 1 : n_left + 3], refs[-1:]
    count = right.shape[0]
    n = pl.program_id(0)
    chain_of = [[meta[c] for c in range(count)], [meta[count - 1 - c] for c in range(count)]]

    @pl.when(n == 0)
    def _():
        for i in range(n_left):
            for side in range(2):
                turned[i, side] = jnp.concatenate([left[i][c] for c in chain_of[side]], 0).T

    pick = jnp.where(n == 3, 1, 0) if unit == 0 else 0

    def put(side, total):
        for block in range(8):
            place = meta[count + 1 + (2 - unit) * 8 + block]
            outs[side][place] = total[block * ROWS : (block + 1) * ROWS]

    def with_first(first):
        @pl.when(meta[count] == first)
        def _():
            for side, many in ((0, first), (1, count - first)):
                if many:
                    rows = jnp.concatenate([right[c] for c in chain_of[side][:many]], 0)
                    put(side, dot_nn(turned[pick, side, :, : many * SEQ], rows).astype(BF16))
                else:
                    put(side, jnp.zeros((D // 2, CHUNK), BF16))

    for first in range(count + 1):
        with_first(first)


ANY = pl.BlockSpec(memory_space=pl.ANY)
SMEM = pl.BlockSpec(memory_space=pltpu.SMEM)
VMEM = pl.BlockSpec(memory_space=pltpu.VMEM)


def shaped(shape, dtype):
    return jax.ShapeDtypeStruct(shape, dtype)


def saved_shapes(count):
    narrow = shaped((count, SEQ, D), BF16)
    return [
        narrow,
        shaped((count, SEQ, D), F32),
        shaped((count, 8, D), F32),
        shaped((count, 1, FF), F32),
        shaped((4, count, SEQ, D), BF16),
        shaped((3, count, SEQ, WIDE), BF16),
        narrow,
    ]


def layer_call(back, slot, lead, count, meta, rows, fbias, pieces, sources, held):
    scratch = [
        pltpu.VMEM((D, 3 * D), BF16),
        pltpu.VMEM((D, D), BF16),
        pltpu.VMEM((D, FF), BF16),
        pltpu.VMEM((D, FF), BF16),
        pltpu.VMEM((SEQ, D), BF16),
        pltpu.VMEM((SEQ, 3 * D), BF16),
        pltpu.VMEM((SEQ, D), BF16),
        pltpu.VMEM((SEQ, FF), BF16),
        pltpu.VMEM((SEQ, D), BF16),
        pltpu.VMEM((SEQ, D), BF16),
        pltpu.VMEM((SEQ, D), F32),
        pltpu.SemaphoreType.DMA((6, BLOCKS)),
    ]
    if back:
        scratch += [
            pltpu.VMEM((SEQ, D), BF16),
            pltpu.VMEM((HEADS, SEQ, SEQ), F32),
            pltpu.VMEM((SEQ, FF), F32),
            pltpu.VMEM((SEQ, D), F32),
            pltpu.VMEM((SEQ, D), F32),
            pltpu.VMEM((SEQ, WIDE), BF16),
            pltpu.VMEM((SEQ, FF), BF16),
            pltpu.VMEM((SEQ, D), BF16),
            pltpu.VMEM((SEQ, D), BF16),
            pltpu.VMEM((8, D), F32),
            pltpu.VMEM((1, FF), F32),
            pltpu.VMEM((SEQ, D), BF16),
        ]
    operands = [meta, rows, fbias, *pieces, *sources]
    specs = [SMEM, VMEM, VMEM] + [ANY] * (len(pieces) + len(sources))
    first = [shaped((1, SEQ, D), BF16)]
    kept = saved_shapes(count) if back else []
    aliases = {}
    for at, array in enumerate(held):
        if array is not None:
            aliases[len(operands)] = at + 1
            operands.append(array)
            specs.append(ANY)
    outs = pl.pallas_call(
        functools.partial(layer_kernel, back, slot, lead, count),
        out_shape=first + kept,
        in_specs=specs,
        out_specs=[ANY] * (1 + len(kept)),
        scratch_shapes=scratch,
        input_output_aliases=aliases,
        compiler_params=pltpu.CompilerParams(vmem_limit_bytes=50 * 1024 * 1024),
        cost_estimate=pl.CostEstimate(flops=1, bytes_accessed=1, transcendentals=0),
        name="layer_back" if back else "layer_fwd",
    )(*operands)
    return outs[0], list(outs[1:])


def grad_call(unit, at, meta, left, right):
    count = left.shape[1]
    which = {2: [0], 1: [1], 0: [2, 3]}[unit]

    def left_of(which):
        return pl.BlockSpec((None, count, SEQ, D // 2), lambda n, m: (which, 0, 0, m[count + 1 + 24 + at]))

    return pl.pallas_call(
        functools.partial(grad_kernel, unit, at),
        out_shape=[shaped((8, ROWS, WIDE), BF16)] * 2,
        grid_spec=pltpu.PrefetchScalarGridSpec(
            num_scalar_prefetch=1,
            grid=(WIDE // CHUNK,),
            in_specs=[left_of(i) for i in which]
            + [pl.BlockSpec((None, count, SEQ, CHUNK), lambda n, m: (unit, 0, 0, n))],
            out_specs=[pl.BlockSpec((8, ROWS, CHUNK), lambda n, m: (0, 0, n))] * 2,
            scratch_shapes=[pltpu.VMEM((len(which), 2, D // 2, count * SEQ), BF16)],
        ),
        compiler_params=pltpu.CompilerParams(vmem_limit_bytes=50 * 1024 * 1024),
        cost_estimate=pl.CostEstimate(flops=1, bytes_accessed=1, transcendentals=0),
        name="layer_grad",
    )(meta, *[left] * len(which), right)


def swap_bit(array, bit):
    count = lax.axis_size("dp")
    return lax.ppermute(array, "dp", [(i, i ^ (1 << bit)) for i in range(count)])


def swap_section(array):
    return lax.ppermute(array, "section", [(0, 1), (1, 0)])


def along(array, pairs):
    count = lax.axis_size("dp")
    flat = [(s * count + i, t * count + k) for (s, i), (t, k) in pairs]
    return lax.ppermute(array, ("section", "dp"), flat)


def both(first, second):
    return (first.astype(F32) + second.astype(F32)).astype(BF16)


def after(array, *others):
    others = [other for other in others if other is not None]
    return lax.optimization_barrier((array, *others))[0] if others else array


class Waves:
    def __init__(self):
        self.before = ()

    def __call__(self, *sends):
        arrays = lax.optimization_barrier(tuple(array for array, _ in sends) + self.before)[: len(sends)]
        self.before = tuple(move(array) for array, (_, move) in zip(arrays, sends))
        return list(self.before)


def by_bit(bit):
    return lambda array: swap_bit(array, bit)


def by(pairs):
    return lambda array: along(array, pairs)


class Routes:
    def __init__(self, near):
        self.home_to_away = [((h, h * near + j), (1 - h, h * near + j)) for h in range(2) for j in range(near)]
        self.away_to_home = [(b, a) for a, b in self.home_to_away]
        self.straight = [((s, (1 - s) * near + j), (s, s * near + j)) for s in range(2) for j in range(near)]
        self.straight_back = [(b, a) for a, b in self.straight]
        self.crossed = [((s, (1 - s) * near + j), (1 - s, s * near + j)) for s in range(2) for j in range(near)]
        self.up = [((s, j), (s, near + j)) for s in range(2) for j in range(near)]
        self.down = [(b, a) for a, b in self.up]


def per_device(
    inputs,
    cotangent,
    chain_tags,
    chain_lengths,
    attn_in,
    attn_out,
    ffn_in,
    ffn_out,
    proj_bias,
    ffn_bias,
    norm_gain,
    norm_shift,
):
    n_dp = lax.axis_size("dp")
    near = n_dp // 2
    rows = attn_in.shape[2]
    count = inputs.shape[0]
    fast = near == 8 and rows == ROWS
    routes = Routes(near)
    section = lax.axis_index("section")
    place = lax.axis_index("dp")
    half = place // near
    spot = place % near
    at_home = section == half

    native = jnp.concatenate(
        [
            attn_in[0].astype(BF16),
            attn_out[0].astype(BF16),
            ffn_in[0].astype(BF16),
            jnp.swapaxes(ffn_out[0].astype(BF16), 1, 2),
        ],
        -1,
    )
    smalls = jnp.concatenate([proj_bias[0], norm_gain[0], norm_shift[0]], 1).astype(BF16)
    wides = ffn_bias[0].astype(BF16)
    numbers = jnp.concatenate([chain_tags, chain_lengths])
    crossing = routes.straight_back
    if fast:
        mine = jnp.where(section == 0, native[0], native[1])
        twin = jnp.where(section == 0, native[1], native[0])
        wave = Waves()
        cuts = (0, WIDE, 2 * WIDE, 3 * WIDE)

        def bits(held, step):
            return [(held[unit], by_bit(ROTATIONS[unit][step])) for unit in range(3)]

        def joined(held, got):
            return [jnp.concatenate([a, b], 0) for a, b in zip(held, got)]

        def own(blocks):
            return [blocks[None, :, cuts[unit] : cuts[unit + 1]] for unit in range(3)]

        def merged(held):
            return jnp.concatenate(held, -1)

        def one_bit(array, bit):
            return (array, by_bit(bit))

        small = jnp.pad(smalls, ((0, 0), (0, 0), (0, EXTRA - rows)))
        wide = jnp.pad(wides, ((0, 0), (0, 2 * EXTRA - 4 * rows))).reshape(2, 2, EXTRA)
        small = jnp.pad(jnp.concatenate([small, wide], 1), ((0, 0), (0, 6), (0, 0)))
        small = small.at[:, 10, : 2 * count].set(numbers.astype(BF16)[None])
        home, small_home = wave((twin, by(routes.home_to_away)), (small, by(routes.home_to_away)))
        near_held = own(jnp.where(at_home, mine, home))
        *got, small_straight, cross_a = wave(
            *bits(near_held, 0), (small, by(routes.straight)), (twin[:, : cuts[1]], by(routes.crossed))
        )
        near_held = joined(near_held, got)
        *got, small_crossed, cross_b = wave(
            *bits(near_held, 1), (small, by(routes.crossed)), (twin[:, cuts[1] :], by(routes.crossed))
        )
        small_held = jnp.stack(
            [jnp.where(at_home, small, small_home), jnp.where(at_home, small_straight, small_crossed)]
        )[None]
        near_held = joined(near_held, got)
        *near_far, small_got, straight = wave(
            *bits(near_held, 2), one_bit(small_held, 0), (mine, by(routes.straight))
        )
        small_held = jnp.concatenate([small_held, small_got], 0)
        away_held = own(jnp.where(at_home, straight, jnp.concatenate([cross_a, cross_b], -1)))
        *got, small_got, twin_near_held = wave(
            *bits(away_held, 0), one_bit(small_held, 1), (merged(near_held), swap_section)
        )
        small_held = jnp.concatenate([small_held, small_got], 0)
        away_held = joined(away_held, got)
        *got, moved, twin_near_far = wave(
            *bits(away_held, 1),
            (jnp.where(half == 1, inputs, cotangent), by(crossing)),
            (merged(near_far), swap_section),
        )
        away_held = joined(away_held, got)
        *away_far, small_got, twin_away_held = wave(
            *bits(away_held, 2), one_bit(small_held, 2), (merged(away_held), swap_section)
        )
        small_held = jnp.concatenate([small_held, small_got], 0)
        twin_last = wave(*[(array, swap_section) for array in away_far])
        numbers_got = small_crossed[0, 10, : 2 * count].astype(F32).astype(jnp.int32)
        pieces = [array for group in zip(near_held, near_far, away_held, away_far) for array in group]
        pieces += [twin_near_held, twin_near_far, twin_away_held, *twin_last]

        def table(masks):
            near_ones = spot ^ jnp.asarray(masks, jnp.int32)
            return jnp.concatenate([near_ones + near * half, near_ones + near * (1 - half)])

        tables = [table(piece_masks(unit)) for unit in range(3)]
        places = [grad_place(spot ^ jnp.arange(8, dtype=jnp.int32), ROTATIONS[2 - unit]) for unit in range(3)]
        row_halves = [half, 1 - half]
        first_side = section
        small_order = (spot ^ jnp.arange(8, dtype=jnp.int32))
        small_order = jnp.stack([small_order + near * half, small_order + near * (1 - half)], 1).reshape(BLOCKS)
        pick = (small_order[None, :] == jnp.arange(BLOCKS, dtype=jnp.int32)[:, None]).astype(BF16)
        row_list, fbias_list = [], []
        laid = dot_nn(pick, small_held.reshape(BLOCKS, 2 * 16 * EXTRA)).reshape(BLOCKS, 2, 16, EXTRA)
        laid = jnp.where(section == 0, laid, laid[:, ::-1])
        for side in range(2):
            row_list.append(jnp.swapaxes(laid[:, side, :8, :rows], 0, 1).reshape(8, D))
            fbias_list.append(laid[:, side, 8:10].reshape(BLOCKS, 2 * EXTRA)[:, : 4 * rows].reshape(1, FF))
        rows_all = jnp.stack(row_list)
        fbias_all = jnp.stack(fbias_list)
    else:
        tables = [jnp.arange(BLOCKS, dtype=jnp.int32)] * 3
        places = [jnp.arange(8, dtype=jnp.int32)] * 3
        row_halves = [jnp.int32(0), jnp.int32(1)]
        first_side = 0
        moved = along(jnp.where(half == 1, inputs, cotangent), crossing)
        numbers_got = along(numbers, crossing)

        def whole(array, dim):
            full = lax.all_gather(array, ("section", "dp"), axis=0).reshape((2, n_dp) + array.shape)
            full = lax.dynamic_index_in_dim(full, half, 0, keepdims=False)
            shape = array.shape[:dim] + (n_dp * array.shape[dim],) + array.shape[dim + 1 :]
            return jnp.moveaxis(full, 0, dim).reshape(shape)

        full = whole(native, 1).reshape(2, 4, 4, ROWS, 3 * WIDE)
        pieces = [full[0, q, :, :, unit * WIDE : (unit + 1) * WIDE] for unit in range(3) for q in range(4)]
        pieces += [full[1, q] for q in range(3)]
        pieces += [full[1, 3, :, :, unit * WIDE : (unit + 1) * WIDE] for unit in range(3)]
        rows_all = whole(smalls, 2).astype(F32)
        fbias_all = whole(wides, 1).astype(F32)[:, None, :]

    numbers = jnp.where(at_home, numbers, numbers_got)
    chains = jnp.where(at_home, inputs, moved)
    top_grad = jnp.where(at_home, cotangent, moved)
    sides = numbers[:count] ^ first_side
    meta = [half[None].astype(jnp.int32), numbers, sides.astype(jnp.int32)] + tables
    meta = jnp.concatenate(meta + [section[None].astype(jnp.int32)])
    later = jnp.arange(count)[:, None] < jnp.arange(count)[None, :]
    rank = jnp.sum((sides[:, None] > sides[None, :]) | ((sides[:, None] == sides[None, :]) & later.T), axis=1)
    sorted_chains = jnp.sum(
        jnp.where(rank[None, :] == jnp.arange(count)[:, None], jnp.arange(count)[None, :], 0), axis=1
    )
    grad_meta = jnp.concatenate(
        [sorted_chains.astype(jnp.int32), jnp.sum(1 - sides)[None].astype(jnp.int32)]
        + [places[unit] for unit in (2, 1, 0)]
        + [value[None].astype(jnp.int32) for value in row_halves]
    )

    lead = 2
    call = functools.partial(layer_call, lead=lead, count=count, rows=rows_all, fbias=fbias_all, pieces=pieces)
    acts, grads, held = [None] * count, [None] * count, [None] * 7
    token = None

    def forward(c):
        nonlocal token
        out, _ = call(False, c, meta=after(meta, token), sources=[chains], held=[])
        acts[c], token = along(out, routes.up), out

    for c in range(count):
        forward(c)
    for slot in range(count + lead):
        sources = [chains]
        if slot < count:
            sources += [acts[slot], top_grad]
        if slot >= lead:
            sources.append(grads[slot - lead])
        out, held = call(True, slot, meta=after(meta, token), sources=sources, held=held)
        token = out
        if slot < count:
            grads[slot] = along(out, routes.down)
    act_all, grad_all, sums, fsums, s_left, s_right, give = held


    def gradient(unit, at, *others):
        return grad_call(unit, at, after(grad_meta, *others), s_left, s_right)

    act_move = by([pair for j in range(near) for pair in (((1, near + j), (0, near + j)), ((0, near + j), (1, j)))])
    grad_move = by([pair for j in range(near) for pair in (((0, j), (1, j)), ((1, j), (0, near + j)))])
    act_other, grad_other = act_move(give), grad_move(give)

    chosen = (sides[None, :] == jnp.arange(2, dtype=jnp.int32)[:, None]).astype(F32)
    row_sums = jnp.sum(chosen[:, :, None, None] * sums[None], axis=1)
    fbias_sums = jnp.sum(chosen[:, :, None] * fsums[None, :, 0], axis=1)
    small_grads = jnp.concatenate([jnp.swapaxes(row_sums, 1, 2), fbias_sums.reshape(2, D, 4)], -1)

    if fast:
        laid = jnp.concatenate([small_grads, jnp.zeros((2, D, EXTRA - 12), F32)], -1).astype(BF16)
        laid = jnp.swapaxes(laid.reshape(2, BLOCKS, ROWS, EXTRA), 0, 1)
        small_places = table(grad_masks(ROTATIONS[0]))
        pick = (small_places[:, None] == jnp.arange(BLOCKS, dtype=jnp.int32)[None, :]).astype(BF16)
        laid = dot_nn(pick, laid.reshape(BLOCKS, -1)).astype(BF16).reshape(2, 8, 2, ROWS, EXTRA)
        laid = jnp.transpose(laid, (2, 1, 0, 3, 4)).reshape(2, 8, 2 * ROWS, EXTRA)
        wave = Waves()

        def reduce_step(keep, got, step):
            width = 4 >> step
            send = [both(a[width:], b[width:]) for a, b in zip(keep, got)]
            return [both(a[:width], b[:width]) for a, b in zip(keep, got)], send

        def bits_out(send, step):
            return [(send[i], by_bit(ROTATIONS[i % 3][step])) for i in range(len(send))]

        units = (2, 1, 0)
        terms = [gradient(unit, 1) for unit in units]
        keep = [own for own, _ in terms]
        got = [swap_section(other) for _, other in terms]
        wave.before = (act_other, grad_other)
        near_terms = [gradient(2, 0, keep[2])]
        send = [both(a[4:], b[4:]) for a, b in zip(keep, got)]
        near_terms += [gradient(1, 0, *send)]
        near_terms += [gradient(0, 0, near_terms[1][0])]
        near_keep = [own for own, _ in near_terms]
        small_got, *far_got, other = wave((laid[1], swap_section), *bits_out(send, 0), (near_terms[0][1], swap_section))
        near_got = [other]
        keep = [both(after(a, *send)[:4], b[:4]) for a, b in zip(keep, got)]
        got = far_got
        small_keep = [laid[0]]
        for step in (1, 2):
            small_keep, small_send = reduce_step(small_keep, [small_got], step - 1)
            keep, send = reduce_step(keep, got, step)
            small_got, *got, other = wave(
                one_bit(small_send[0], step - 1), *bits_out(send, step), (near_terms[step][1], swap_section)
            )
            near_got.append(other)
        far_sum = jnp.concatenate([(a[0].astype(F32) + b[0].astype(F32)).astype(BF16) for a, b in zip(keep, got)], -1)

        keep, send = reduce_step(near_keep, near_got, 0)
        small_keep, small_send = reduce_step(small_keep, [small_got], 2)
        small_got, *got, cross_a = wave(
            one_bit(small_send[0], 2), *bits_out(send, 0), (far_sum[:, : 2 * WIDE], by(routes.crossed))
        )
        small_end = (small_keep[0][0].astype(F32) + small_got[0].astype(F32)).astype(BF16)
        keep, send = reduce_step(keep, got, 1)
        small_straight, *got, straight = wave(
            (small_end[ROWS:], by(routes.straight_back)), *bits_out(send, 1), (far_sum, by(routes.straight_back))
        )
        keep, send = reduce_step(keep, got, 2)
        *got, cross_b = wave(
            *bits_out(send, 2),
            (jnp.concatenate([far_sum[:, 2 * WIDE :], small_end[ROWS:]], -1), by(routes.crossed)),
        )
        near_sum = [a[0].astype(F32) + b[0].astype(F32) for a, b in zip(keep, got)] + [small_end[:ROWS].astype(F32)]
        (beside,) = wave((jnp.concatenate(near_sum, -1).astype(BF16), by(routes.away_to_home)))
        crossed = jnp.concatenate([cross_a, cross_b], -1)
        straight = jnp.concatenate([straight, small_straight], -1)

        def settle(i, width):
            cols = slice(i * WIDE, i * WIDE + width)
            mine = jnp.where(at_home, near_sum[i], straight[:, cols].astype(F32))
            twin = jnp.where(at_home, beside[:, cols].astype(F32), crossed[:, cols].astype(F32))
            return jnp.stack([jnp.where(section == 0, mine, twin), jnp.where(section == 0, twin, mine)])

        unit_out = [None] * 3
        for i, unit in enumerate(units):
            unit_out[unit] = settle(i, WIDE)
        small_out = settle(3, EXTRA)
    else:

        def summed(array):
            layers = jnp.stack([jnp.where(half == layer, array, jnp.zeros_like(array)) for layer in range(2)])
            layers = jnp.swapaxes(layers, 1, 2).reshape(2 * n_dp, rows, 2, array.shape[-1])
            out = lax.psum_scatter(layers, ("section", "dp"), scatter_dimension=0, tiled=True)
            return jnp.swapaxes(out[0], 0, 1)

        unit_out = []
        for unit in range(3):
            terms = [gradient(unit, at) for at in range(2)]
            group = [jnp.concatenate([part[side] for part in terms], 0).reshape(D, WIDE) for side in range(2)]
            unit_out.append(summed(jnp.stack(group).astype(F32)))
        small_out = summed(small_grads)

    act_out = jnp.where(at_home, act_all, act_other)
    grad_out = jnp.where(at_home, grad_all, grad_other.astype(F32))

    turned = jnp.swapaxes(small_out[:, :, :8], 1, 2)
    return (
        act_out[None],
        grad_out[None],
        unit_out[0][None, :, :, : 3 * D],
        unit_out[0][None, :, :, 3 * D :],
        unit_out[1][None],
        jnp.swapaxes(unit_out[2], 1, 2)[None],
        turned[None, :, 0:4],
        small_out[:, :, 8:12].reshape(1, 2, 4 * rows),
        turned[None, :, 4:6],
        turned[None, :, 6:8],
    )


def solution(mesh):
    in_specs = (
        P("dp", None, None),
        P("dp", None, None),
        P("dp"),
        P("dp"),
        P("section", None, "dp", None),
        P("section", None, "dp", None),
        P("section", None, "dp", None),
        P("section", None, None, "dp"),
        P("section", None, None, "dp"),
        P("section", None, "dp"),
        P("section", None, None, "dp"),
        P("section", None, None, "dp"),
    )
    out_specs = (
        P("section", "dp", None, None),
        P("section", "dp", None, None),
        P("section", None, "dp", None),
        P("section", None, "dp", None),
        P("section", None, "dp", None),
        P("section", None, None, "dp"),
        P("section", None, None, "dp"),
        P("section", None, "dp"),
        P("section", None, None, "dp"),
        P("section", None, None, "dp"),
    )
    return jax.shard_map(
        per_device, mesh=mesh, in_specs=in_specs, out_specs=out_specs, check_vma=False
    )
```
